32 devices in a mesh: dp: 4 (over y, x), expert: 8 (over z, core).
Axes of the slice: x: 2, y: 2, z: 4, core: 2. Of those that a mesh axis runs over, the one named last changes fastest.
Arguments:
- tokens: bfloat16 [2, 32, 256, 1024], P(None, ('dp', 'expert')), may hold values from -6 to 6
- segment_ids: int32 [2, 32, 256], P(None, ('dp', 'expert')), may hold values from 0 to 15, never falling along the last dimension, each value on 1 to 128 neighbouring positions
- routes: int32 [2, 32, 256, 1], P(None, ('dp', 'expert')), may hold values from 0 to 7
- cotangent: bfloat16 [2, 32, 256, 1024], P(None, ('dp', 'expert')), may hold values from -6 to 6
- w_qkv: bfloat16 [1024, 3072], P(('dp', 'expert')), may hold values from -0.25 to 0.25
- w_attn_out: bfloat16 [1024, 1024], P(('dp', 'expert')), may hold values from -0.5 to 0.5
- w_router: bfloat16 [1024, 8], P(('dp', 'expert')), may hold values from -0.125 to 0.125
- gain_attn: bfloat16 [1024], P(('dp', 'expert')), may hold values from 0.099609375 to 1.8984375
- gain_moe: bfloat16 [1024], P(('dp', 'expert')), may hold values from 0.099609375 to 1.8984375
- w_expert_in: bfloat16 [8, 1024, 4096], P('expert', 'dp'), may hold values from -0.1875 to 0.1875
- w_expert_out: bfloat16 [8, 4096, 1024], P('expert', 'dp'), may hold values from -0.75 to 0.75
Outputs:
- output: bfloat16 [2, 32, 256, 1024], P(None, ('dp', 'expert'))
- grad_tokens: float32 [2, 32, 256, 1024], P(None, ('dp', 'expert'))
- grad_qkv: float32 [1024, 3072], P(('dp', 'expert'))
- grad_attn_out: float32 [1024, 1024], P(('dp', 'expert'))
- grad_router: float32 [1024, 8], P(('dp', 'expert'))
- grad_gain_attn: float32 [1024], P(('dp', 'expert'))
- grad_gain_moe: float32 [1024], P(('dp', 'expert'))
- grad_expert_in: float32 [8, 1024, 4096], P('expert', 'dp')
- grad_expert_out: float32 [8, 4096, 1024], P('expert', 'dp')
The draws below stay inside these ranges and needn't reach their ends.
Inputs may be any that keep to these rules, and one draw needn't show every extreme that they name: `segment_ids`: in each sequence the numbers never fall; a document spans 1 to 128 positions, and in each sequence one spans exactly that many.
All inputs are finite; a program needn't handle non-finite values.
Results may differ from the reference program's by a relative error of at most 0.014.
The reference program's roundings to bfloat16 on the way count: a program that leaves them out, or rounds other values in their place, can miss the bound.
Values may be sent and summed in bfloat16 or wider, within the bound.
A program may use at most 256 MiB of HBM per device.

```python
import math
import jax
import jax.numpy as jnp
import numpy as np
from jax import lax

D = 1024
HEADS = 16
FF = 4096
SEQ = 256
MICRO = 2
HEAD_DIM = 64
EXPERTS = 8
SEQS = 32
CAP = 36


def block_levels(key, shape, cuts, least, largest):
    loudness = 1.0
    for dim, blocks in cuts:
        heights = jax.random.uniform(jax.random.fold_in(jax.random.fold_in(key, 6), dim), (blocks,), jnp.float32, least / len(cuts), largest / len(cuts))
        loudness = loudness * jnp.repeat(jnp.exp(heights), shape[dim] // blocks).reshape((-1,) + (1,) * (len(shape) - 1 - dim))
    return loudness


def choose_distinct(own_key, rows, number_of, top, lift):
    ranking = jax.random.permutation(jax.random.fold_in(own_key, 1), number_of)
    favour = ranking
    for power in range(3):
        favour = favour * favour // number_of
    favour = favour * lift // number_of
    lots = jax.random.randint(jax.random.fold_in(own_key, 2), (rows, number_of), 0, 4096) + favour
    fixed_rows = jax.random.permutation(jax.random.fold_in(own_key, 3), rows)[jnp.arange(number_of) % rows]
    lots = jnp.where(jnp.arange(rows)[:, None] == fixed_rows[None, :], 1 << 14, lots)
    priority = lots * number_of + jnp.arange(number_of)
    return lax.top_k(priority.astype(jnp.int32), top)[1].astype(jnp.int32)


def profile(number_of, total, most, skew):
    weights = [(1 << 20) // math.isqrt(grade ** skew) + 1 for grade in range(2, number_of + 1)]
    surplus, given = total - most - (number_of - 1), [1] * (number_of - 1)
    while surplus > 0:
        free = [i for i in range(number_of - 1) if given[i] < most]
        pool, budget = sum([weights[i] for i in free]), surplus
        for i in free:
            extra = min(most - given[i], max(1, budget * weights[i] // pool), surplus)
            given[i] = given[i] + extra
            surplus = surplus - extra
    return np.array([most] + given)


def ragged(stream_key, count, total, limit, lean):
    if count == 2:
        one = jax.random.randint(stream_key, (), max(1, total - limit), min(limit, total - 1) + 1)
        return jnp.stack([one, total - one])
    sizes = jnp.asarray(profile(count, total, limit, lean), jnp.int32)
    twos = (count - 1) // 2
    donor, receiver = sizes[1:1 + 2 * twos:2], sizes[2:2 + 2 * twos:2]
    margin = jnp.minimum(donor - 1, limit - receiver)
    passed = jax.random.randint(jax.random.fold_in(stream_key, 1), (twos,), 0, 1 << 20) % (margin + 1)
    sizes = sizes.at[1:1 + 2 * twos:2].set(donor - passed).at[2:2 + 2 * twos:2].set(receiver + passed)
    return sizes[jax.random.permutation(jax.random.fold_in(stream_key, 2), count)]


def normal_values(key, shape, width, bound, split=(), kind=jnp.bfloat16):
    level = block_levels(key, shape, split, -0.22, 0.18) if split else 1.0
    entries = jax.random.normal(key, shape, jnp.float32) * width * level
    return jnp.minimum(jnp.maximum(entries, -bound), bound).astype(kind)


def setup_inputs(seed: int = 0) -> dict:
    splits = jax.random.split(jax.random.key(seed), 12)
    tokens = normal_values(splits[0], (MICRO, SEQS, SEQ, D), 1.0, 6.0, ((1, 32),))
    segment_ids = jax.vmap(lambda own: jnp.searchsorted(jnp.cumsum(ragged(own, SEQ // 16, SEQ, SEQ // 2, 2)), jnp.arange(SEQ), side="right"))(jax.random.split(splits[1], MICRO * SEQS)).reshape((MICRO, SEQS, SEQ)).astype(jnp.int32)
    routes = choose_distinct(splits[2], MICRO * SEQS * SEQ, EXPERTS, 1, 1024).reshape((MICRO, SEQS, SEQ, 1))
    cotangent = normal_values(splits[3], (MICRO, SEQS, SEQ, D), 1.0, 6.0, ((1, 32),))
    w_qkv = normal_values(splits[4], (D, 3 * D), (D // 2) ** -0.5, 0.25, ((0, 32),))
    w_attn_out = normal_values(splits[5], (D, D), (D // 8) ** -0.5, 0.5, ((0, 32),))
    w_router = normal_values(splits[6], (D, EXPERTS), (2 * D) ** -0.5, 0.125, ((0, 32),))
    gain_attn = jnp.clip(1.0 + 0.18 * jax.random.normal(splits[7], (D,), jnp.float32), 0.099609375, 1.8984375).astype(jnp.bfloat16)
    gain_moe = jnp.clip(1.0 + 0.18 * jax.random.normal(splits[8], (D,), jnp.float32), 0.099609375, 1.8984375).astype(jnp.bfloat16)
    w_expert_in = normal_values(splits[9], (EXPERTS, D, FF), D ** -0.5, 0.1875, ((0, 8), (1, 4)))
    w_expert_out = normal_values(splits[10], (EXPERTS, FF, D), (max(1, FF // (EXPERTS * EXPERTS))) ** -0.5, 0.75, ((0, 8), (1, 4)))
    return dict(tokens=tokens, segment_ids=segment_ids, routes=routes, cotangent=cotangent, w_qkv=w_qkv, w_attn_out=w_attn_out, w_router=w_router, gain_attn=gain_attn, gain_moe=gain_moe, w_expert_in=w_expert_in, w_expert_out=w_expert_out)


epsilon = 1e-05
highest_mode = lax.Precision.HIGHEST

@jax.custom_vjp
def low(v):
    return lax.optimization_barrier(v.astype(jnp.bfloat16)).astype(jnp.float32)

@jax.custom_vjp
def low_back(v):
    return v

def low_keep(v):
    return (low(v), None)

def low_pass(kept, grad):
    return (grad,)

def back_keep(v):
    return (v, None)

def back_low(kept, grad):
    return (low(grad),)
low.defvjp(low_keep, low_pass)
low_back.defvjp(back_keep, back_low)

def normalize(values):
    row_mean = lax.optimization_barrier(jnp.mean(values, axis=-1, keepdims=True))
    centered = values - row_mean
    return centered * lax.rsqrt(lax.optimization_barrier(jnp.mean(centered * centered, axis=-1, keepdims=True)) + epsilon)

def sequence_layer(weights, inputs, segment_row, route_row):
    w_qkv, w_attn_out, w_router, gain_attn, gain_moe, w_expert_in, w_expert_out = weights
    length = inputs.shape[0]
    score_scale = 1.0 / math.sqrt(HEAD_DIM)
    normed = low(normalize(inputs) * gain_attn)
    qkv_rows = low_back(low(jnp.dot(normed, w_qkv, precision=highest_mode)))
    query_rows = qkv_rows[:, :D].reshape(length, HEADS, HEAD_DIM)
    key_rows = qkv_rows[:, D:2 * D].reshape(length, HEADS, HEAD_DIM)
    value_rows = qkv_rows[:, 2 * D:].reshape(length, HEADS, HEAD_DIM)
    scores = low_back(jnp.einsum('shd,thd->hst', query_rows, key_rows, precision=highest_mode) * score_scale)
    position = jnp.arange(length, dtype=jnp.int32)
    allowed = (position[None, :] <= position[:, None]) & (segment_row[:, None] == segment_row[None, :])
    attn_prob = low(jax.nn.softmax(jnp.where(allowed[None], scores, -1e+30), axis=-1))
    attn_mixed = jnp.einsum('hst,thd->shd', attn_prob, value_rows, precision=highest_mode).reshape(length, D)
    attn_mixed = low_back(low(attn_mixed))
    attn_branch = low_back(jnp.dot(attn_mixed, w_attn_out, precision=highest_mode))
    residual = inputs + attn_branch
    hidden_in = low(normalize(residual) * gain_moe)
    logits = low_back(jnp.dot(hidden_in, w_router, precision=highest_mode))
    router_prob = jax.nn.softmax(logits, axis=-1)
    one_hot = (route_row[:, None] == jnp.arange(EXPERTS, dtype=jnp.int32)[None, :]).astype(jnp.int32)
    gate_prob = lax.optimization_barrier(jnp.sum(router_prob * one_hot.astype(jnp.float32), axis=1))
    earlier = jnp.cumsum(one_hot, axis=0, dtype=jnp.int32) - one_hot
    position_in = lax.optimization_barrier(jnp.sum(earlier * one_hot, axis=1, dtype=jnp.int32))
    kept_mask = position_in < CAP
    slot_index = jnp.where(kept_mask, route_row * CAP + position_in, EXPERTS * CAP).astype(jnp.int32)
    buffer = jnp.zeros((EXPERTS * CAP + 1, D), jnp.float32).at[slot_index].add(hidden_in)[:EXPERTS * CAP]
    buffer = low_back(buffer).reshape(EXPERTS, CAP, D)
    pre_act = low_back(jnp.einsum('ecd,edf->ecf', buffer, w_expert_in, precision=highest_mode))
    activation = low(jax.nn.gelu(pre_act))
    expert_rows = jnp.einsum('ecf,efd->ecd', activation, w_expert_out, precision=highest_mode)
    expert_rows = low_back(low(expert_rows)).reshape(EXPERTS * CAP, D)
    safe_index = jnp.minimum(slot_index, EXPERTS * CAP - 1).astype(jnp.int32)
    gathered = expert_rows[safe_index] * kept_mask[:, None].astype(jnp.float32)
    return residual + gate_prob[:, None] * gathered

def reference(tokens, segment_ids, routes, cotangent, w_qkv, w_attn_out, w_router, gain_attn, gain_moe, w_expert_in, w_expert_out):
    params = (w_qkv.astype(jnp.float32), w_attn_out.astype(jnp.float32), w_router.astype(jnp.float32), gain_attn.astype(jnp.float32), gain_moe.astype(jnp.float32), w_expert_in.astype(jnp.float32), w_expert_out.astype(jnp.float32))
    seq_total = MICRO * SEQS
    bundle = math.gcd(8, seq_total)
    seg_groups = segment_ids.reshape(seq_total // bundle, bundle, SEQ)
    route_groups = routes.reshape(seq_total // bundle, bundle, SEQ)

    def whole(weights, inputs):

        def run_group(group_data):
            inputs_group, seg_group, route_group = group_data

            def one_sequence(seq_inputs, seq_segments, seq_routes):
                return sequence_layer(weights, seq_inputs, seq_segments, seq_routes)
            return jax.vmap(one_sequence)(inputs_group, seg_group, route_group)
        grouped = lax.map(jax.checkpoint(run_group), (inputs.reshape(seq_total // bundle, bundle, SEQ, D), seg_groups, route_groups))
        return grouped.reshape(MICRO, SEQS, SEQ, D)
    output, pullback = jax.vjp(whole, params, tokens.astype(jnp.float32))
    grad_params, grad_tokens = pullback(cotangent.astype(jnp.float32))
    return (output.astype(jnp.bfloat16), grad_tokens, grad_params[0], grad_params[1], grad_params[2], grad_params[3], grad_params[4], grad_params[5], grad_params[6])
```

```python
import functools
import math

import jax
import jax.numpy as jnp
from jax import lax
from jax.experimental import pallas as pl
from jax.experimental.pallas import tpu as pltpu
from jax.sharding import PartitionSpec as P

HEADS = 16
epsilon = 1e-05
masked_value = -1e30
f32 = jnp.float32
bf16 = jnp.bfloat16

MESH = pl.DeviceIdType.MESH
DMA = pltpu.SemaphoreType.DMA


def flip(index, mask):
    bit = 1
    while bit <= mask:
        if mask & bit:
            index = index + bit - 2 * bit * ((index // bit) % 2)
        bit *= 2
    return index


def place_of(chips):
    block = lax.axis_index("dp")
    owner = lax.axis_index("expert")
    peer_x = {"dp": flip(block, 1)}
    peer_y = {"dp": flip(block, 2)}
    peer_core = {"expert": flip(owner, 1)}
    peers_z = [{"expert": flip(owner, 2 * k)} for k in range(chips)]
    return block, owner // 2, owner % 2, peer_x, peer_y, peer_core, peers_z


def greet(peers):
    barrier = pltpu.get_barrier_semaphore()
    for peer in peers:
        pl.semaphore_signal(barrier, inc=1, device_id=peer, device_id_type=MESH)
    pl.semaphore_wait(barrier, len(peers))


def send(src, dst, send_sem, recv_sem, peer):
    copy = pltpu.make_async_remote_copy(
        src_ref=src, dst_ref=dst, send_sem=send_sem, recv_sem=recv_sem,
        device_id=peer, device_id_type=MESH,
    )
    copy.start()
    return copy


def gather_kernel(chips, cut, shard, full, own_sem, sz, rz, sx, rx, sy, ry, sc, rc):
    block, chip, core, peer_x, peer_y, peer_core, peers_z = place_of(chips)
    rows, width = shard.shape
    halves = (pl.ds(0, cut), pl.ds(cut, width - cut))
    every = pl.ds(0, width)

    def part(origin, step, columns):
        start = ((flip(block, origin) * chips + flip(chip, step)) * 2 + core) * rows
        return full.at[pl.ds(pl.multiple_of(start, rows), rows), columns]

    greet([peer_x, peer_y, peer_core] + peers_z[1:])
    own = pltpu.make_async_copy(shard, part(0, 0, every), own_sem)
    own.start()
    along_z = [None] + [
        send(shard, part(0, 0, every), sz.at[k], rz.at[k], peers_z[k]) for k in range(1, chips)
    ]
    along_x = [[None] * 3 for _ in range(chips)]
    along_y = [[None] * 3 for _ in range(chips)]
    across = [[None] * 4 for _ in range(chips)]

    def to_core(k, origin):
        src = shard if k == 0 and origin == 0 else part(origin, k, every)
        across[k][origin] = send(
            src, part(origin, k, every), sc.at[k, origin], rc.at[k, origin], peer_core
        )

    def pass_on(k):
        along_x[k][1].wait_recv()
        to_core(k, 1)
        along_y[k][1].wait_recv()
        to_core(k, 2)
        along_x[k][2].wait_recv()
        along_y[k][2].wait_recv()
        to_core(k, 3)

    for k in range(chips):
        if k:
            along_z[k].wait_recv()
        for turn in range(2):
            first = turn
            for copies, s, r, peer, half in (
                (along_x, sx, rx, peer_x, first),
                (along_y, sy, ry, peer_y, 1 - first),
            ):
                dst = part(0, k, halves[half])
                src = dst if k else shard.at[:, halves[half]]
                copies[k][turn] = send(src, dst, s.at[k, turn], r.at[k, turn], peer)
        to_core(k, 0)
        if k:
            pass_on(k - 1)
        along_x[k][0].wait_recv()
        piece = part(1, k, halves[0])
        along_y[k][2] = send(piece, piece, sy.at[k, 2], ry.at[k, 2], peer_y)
        along_y[k][0].wait_recv()
        piece = part(2, k, halves[1])
        along_x[k][2] = send(piece, piece, sx.at[k, 2], rx.at[k, 2], peer_x)
    pass_on(chips - 1)
    own.wait()
    for k in range(chips):
        if k:
            along_z[k].wait_send()
        for turn in range(3):
            along_x[k][turn].wait_send()
            along_y[k][turn].wait_send()
        for origin in range(4):
            across[k][origin].wait()


def gather_rows(shard, chips):
    rows, width = shard.shape
    cut = (width // 128 + 1) // 2 * 128
    total = 4 * chips * 2 * rows
    return pl.pallas_call(
        functools.partial(gather_kernel, chips, cut),
        out_shape=jax.ShapeDtypeStruct((total, width), shard.dtype),
        in_specs=[pl.BlockSpec(memory_space=pl.ANY)],
        out_specs=pl.BlockSpec(memory_space=pl.ANY),
        scratch_shapes=[
            DMA,
            DMA((chips,)),
            DMA((chips,)),
            DMA((chips, 3)),
            DMA((chips, 3)),
            DMA((chips, 3)),
            DMA((chips, 3)),
            DMA((chips, 4)),
            DMA((chips, 4)),
        ],
        compiler_params=pltpu.CompilerParams(collective_id=1, has_side_effects=True),
        name="gather_rows",
    )(shard)


def reduce_kernel(chips, cut, widths, *refs):
    n = len(widths)
    grads, outs = refs[:n], refs[n : 2 * n]
    total, crecv, xrecv, yrecv, zrecv, part_z = refs[2 * n : 2 * n + 6]
    la, sc, rc, sx, rx, sy, ry, sz, rz = refs[2 * n + 6 :]
    block, chip, core, peer_x, peer_y, peer_core, peers_z = place_of(chips)
    rows, width = zrecv.shape[1:]
    wide = width - cut
    left, right = pl.ds(0, cut), pl.ds(cut, wide)
    columns = []
    for w in widths:
        columns.append(pl.ds(sum(widths[: len(columns)]), w))
    order = list(range(chips - 1, -1, -1))
    opposite = flip(core, 1)
    greet([peer_x, peer_y, peer_core] + peers_z[1:])
    across, local = {}, {}
    for k in order:
        step = flip(chip, k)
        across[k], local[k] = [], []
        for i in range(n):
            across[k].append(
                send(
                    grads[i].at[:, step, opposite],
                    crecv.at[:, step, :, columns[i]],
                    sc.at[k, i], rc.at[k, i], peer_core,
                )
            )
            copy = pltpu.make_async_copy(
                grads[i].at[:, step, core], total.at[:, step, :, columns[i]], la.at[k, i]
            )
            copy.start()
            local[k].append(copy)

    def spot(k, origin, cols):
        return (flip(block, origin), flip(chip, k), slice(None), cols)

    along_x, along_y, along_z = {}, {}, {}

    def begin(k):
        for i in range(n):
            local[k][i].wait()
            across[k][i].wait_recv()
        step = flip(chip, k)
        for origin in (3, 1, 2, 0):
            at = (flip(block, origin), step)
            total[at] = (total[at].astype(f32) + crecv[at].astype(f32)).astype(bf16)
            if origin == 3:
                along_x[k, 0] = send(
                    total.at[spot(k, 3, left)], xrecv.at[k, 0, :, left], sx.at[k, 0], rx.at[k, 0], peer_x
                )
                along_y[k, 0] = send(
                    total.at[spot(k, 3, right)], yrecv.at[k, 0, :, pl.ds(0, wide)], sy.at[k, 0], ry.at[k, 0], peer_y
                )
            if origin == 1:
                along_x[k, 1] = send(
                    total.at[spot(k, 1, left)], xrecv.at[k, 1, :, left], sx.at[k, 1], rx.at[k, 1], peer_x
                )
            if origin == 2:
                along_y[k, 1] = send(
                    total.at[spot(k, 2, right)], yrecv.at[k, 1, :, pl.ds(0, wide)], sy.at[k, 1], ry.at[k, 1], peer_y
                )

    def relay(k):
        along_x[k, 0].wait_recv()
        at = spot(k, 2, left)
        total[at] = (total[at].astype(f32) + xrecv[k, 0, :, left].astype(f32)).astype(bf16)
        along_y[k, 2] = send(total.at[at], yrecv.at[k, 2, :, left], sy.at[k, 2], ry.at[k, 2], peer_y)
        along_y[k, 0].wait_recv()
        at = spot(k, 1, right)
        total[at] = (total[at].astype(f32) + yrecv[k, 0, :, pl.ds(0, wide)].astype(f32)).astype(bf16)
        along_x[k, 2] = send(
            total.at[at], xrecv.at[k, 2, :, pl.ds(0, wide)], sx.at[k, 2], rx.at[k, 2], peer_x
        )

    def finish(k):
        for turn in (1, 2):
            along_x[k, turn].wait_recv()
            along_y[k, turn].wait_recv()
        lhs = (
            total[spot(k, 0, left)].astype(f32)
            + xrecv[k, 1, :, left].astype(f32)
            + yrecv[k, 2, :, left].astype(f32)
        )
        rhs = (
            total[spot(k, 0, right)].astype(f32)
            + yrecv[k, 1, :, pl.ds(0, wide)].astype(f32)
            + xrecv[k, 2, :, pl.ds(0, wide)].astype(f32)
        )
        if k:
            part_z[k, :, left] = lhs.astype(bf16)
            part_z[k, :, right] = rhs.astype(bf16)
            along_z[k] = send(part_z.at[k], zrecv.at[k], sz.at[k], rz.at[k], peers_z[k])
        else:
            for j in range(1, chips):
                along_z[j].wait_recv()
                lhs = lhs + zrecv[j, :, left].astype(f32)
                rhs = rhs + zrecv[j, :, right].astype(f32)
            start = 0
            for i, w in enumerate(widths):
                for lo, hi, value in ((0, cut, lhs), (cut, width, rhs)):
                    a, b = max(start, lo), min(start + w, hi)
                    if a < b:
                        outs[i][:, a - start : b - start] = value[:, a - lo : b - lo]
                start += w

    for i in range(chips + 2):
        if i < chips:
            begin(order[i])
        if 0 <= i - 1 < chips:
            relay(order[i - 1])
        if i - 2 >= 0:
            finish(order[i - 2])
    for k in order:
        for i in range(n):
            across[k][i].wait_send()
        for turn in range(3):
            along_x[k, turn].wait_send()
            along_y[k, turn].wait_send()
        if k:
            along_z[k].wait_send()


def reduce_rows(grads, chips):
    rows = grads[0].shape[0] // (8 * chips)
    widths = tuple(g.shape[1] for g in grads)
    width = sum(widths)
    cut = (width // 128 + 1) // 2 * 128
    n = len(grads)
    return pl.pallas_call(
        functools.partial(reduce_kernel, chips, cut, widths),
        out_shape=[jax.ShapeDtypeStruct((rows, w), f32) for w in widths],
        in_specs=[pl.BlockSpec(memory_space=pl.ANY)] * n,
        out_specs=[pl.BlockSpec(memory_space=pltpu.VMEM)] * n,
        scratch_shapes=[
            pltpu.VMEM((4, chips, rows, width), bf16),
            pltpu.VMEM((4, chips, rows, width), bf16),
            pltpu.VMEM((chips, 3, rows, cut), bf16),
            pltpu.VMEM((chips, 3, rows, cut), bf16),
            pltpu.VMEM((chips, rows, width), bf16),
            pltpu.VMEM((chips, rows, width), bf16),
            DMA((chips, n)),
            DMA((chips, n)),
            DMA((chips, n)),
            DMA((chips, 3)),
            DMA((chips, 3)),
            DMA((chips, 3)),
            DMA((chips, 3)),
            DMA((chips,)),
            DMA((chips,)),
        ],
        compiler_params=pltpu.CompilerParams(collective_id=2, has_side_effects=True),
        name="reduce_rows",
    )(*[g.reshape(4, chips, 2, rows, g.shape[1]) for g in grads])


PAIR_X = tuple((b, b ^ 1) for b in range(4))
PAIR_Y = tuple((b, b ^ 2) for b in range(4))


def mm(a, b):
    return jnp.dot(a, b, preferred_element_type=f32)


def mm_nt(a, b):
    return lax.dot_general(a, b, (((1,), (1,)), ((), ())), preferred_element_type=f32)


def mm_tn(a, b):
    return lax.dot_general(a, b, (((0,), (0,)), ((), ())), preferred_element_type=f32)


def swap_x(a):
    return lax.ppermute(a, "dp", PAIR_X)


def swap_y(a):
    return lax.ppermute(a, "dp", PAIR_Y)


def to_experts(a):
    return lax.all_to_all(a, "expert", split_axis=0, concat_axis=0, tiled=True)


def normalize(values):
    row_mean = jnp.mean(values, axis=-1, keepdims=True)
    centered = values - row_mean
    inv_scale = lax.rsqrt(jnp.mean(centered * centered, axis=-1, keepdims=True) + epsilon)
    return (centered * inv_scale, inv_scale)


def norm_back(grad_normed, normed, inv_scale):
    return inv_scale * (
        grad_normed
        - jnp.mean(grad_normed, axis=-1, keepdims=True)
        - normed * jnp.mean(grad_normed * normed, axis=-1, keepdims=True)
    )


def split_heads(qkv_rows, model_width):
    seq_len = qkv_rows.shape[0]
    head_dim = model_width // HEADS
    return tuple(
        qkv_rows[:, i * model_width : (i + 1) * model_width].reshape(seq_len, HEADS, head_dim)
        for i in range(3)
    )


def route_selector(route_row, expert_count, capacity, padded):
    seq_len = route_row.shape[0]
    one_hot = (route_row[:, None] == lax.iota(jnp.int32, expert_count)[None, :]).astype(f32)
    position = lax.iota(jnp.int32, seq_len)
    before = (position[None, :] < position[:, None]).astype(bf16)
    earlier = mm(before, one_hot.astype(bf16))
    place = jnp.sum(earlier * one_hot, axis=1).astype(jnp.int32)
    slot_index = jnp.where(place < capacity, route_row * padded + place, -1)
    columns = lax.iota(jnp.int32, expert_count * padded)
    selector = (slot_index[:, None] == columns[None, :]).astype(bf16)
    return (one_hot, selector)


def fetch_expert_weights(w_in, w_out, block):
    rows, width = w_in.shape
    half = width // 2
    row_y, row_x = block // 2, block % 2
    mine = lax.dynamic_slice(w_in, (0, row_y * half), (rows, half))
    theirs = lax.dynamic_slice(w_in, (0, (1 - row_y) * half), (rows, half))
    from_y = swap_y(theirs)
    from_x = swap_x(mine)
    from_xy = swap_x(from_y)
    out_x = swap_x(w_out)
    full_in = jnp.zeros((4, rows, half), w_in.dtype)
    for part, place in ((mine, block), (from_y, block ^ 2), (from_x, block ^ 1), (from_xy, block ^ 3)):
        full_in = lax.dynamic_update_slice(full_in, part[None], (place, 0, 0))
    full_out = jnp.zeros((2,) + w_out.shape, w_out.dtype)
    full_out = lax.dynamic_update_slice(full_out, w_out[None], (row_x, 0, 0))
    full_out = lax.dynamic_update_slice(full_out, out_x[None], (1 - row_x, 0, 0))
    return full_in.reshape(4 * rows, half), full_out.reshape(-1, w_out.shape[1])


def reduce_expert_grads(grad_in, grad_out, block):
    rows = grad_in.shape[0] // 4
    half = grad_in.shape[1]
    row_y, row_x = block // 2, block % 2
    parts_out = grad_out.reshape(2, -1, grad_out.shape[1])
    keep_out = lax.dynamic_slice_in_dim(parts_out, row_x, 1, 0)[0]
    send_out = lax.dynamic_slice_in_dim(parts_out, 1 - row_x, 1, 0)[0].astype(bf16)
    done_out = keep_out + swap_x(send_out).astype(f32)
    parts_in = grad_in.reshape(2, 2, rows, half)
    keep_in = lax.dynamic_slice_in_dim(parts_in, row_x, 1, 1)[:, 0]
    send_in = lax.dynamic_slice_in_dim(parts_in, 1 - row_x, 1, 1)[:, 0].astype(bf16)
    sums = keep_in + swap_x(send_in).astype(f32)
    own = lax.dynamic_slice_in_dim(sums, row_y, 1, 0)[0]
    other = lax.dynamic_slice_in_dim(sums, 1 - row_y, 1, 0)[0].astype(bf16)
    got = swap_y(other).astype(f32)
    done_in = jnp.zeros((rows, 2 * half), f32)
    done_in = lax.dynamic_update_slice(done_in, own, (0, row_y * half))
    done_in = lax.dynamic_update_slice(done_in, got, (0, (1 - row_y) * half))
    return done_in, done_out


def attention_forward(attn_in, segment_row, w_qkv):
    seq_len, model_width = attn_in.shape
    score_scale = 1.0 / math.sqrt(model_width // HEADS)
    qkv_rows = mm(attn_in, w_qkv).astype(bf16)
    query_rows, key_rows, value_rows = split_heads(qkv_rows, model_width)
    position = lax.iota(jnp.int32, seq_len)
    allowed = (position[None, :] <= position[:, None]) & (
        segment_row[:, None] == segment_row[None, :]
    )
    scores = jnp.einsum("shd,thd->hst", query_rows, key_rows, preferred_element_type=f32)
    masked = jnp.where(allowed[None], scores * score_scale, masked_value)
    row_max = jnp.max(masked, axis=-1, keepdims=True)
    log_norm = row_max + jnp.log(jnp.sum(jnp.exp(masked - row_max), axis=-1, keepdims=True))
    prob = jnp.exp(masked - log_norm)
    mixed = jnp.einsum("hst,thd->shd", prob.astype(bf16), value_rows, preferred_element_type=f32)
    return qkv_rows, allowed, log_norm, mixed.reshape(seq_len, model_width).astype(bf16)


def attention_backward(grad_mixed, qkv_rows, allowed, log_norm):
    seq_len, model_width = grad_mixed.shape
    score_scale = 1.0 / math.sqrt(model_width // HEADS)
    grad_mixed = grad_mixed.reshape(seq_len, HEADS, model_width // HEADS)
    query_rows, key_rows, value_rows = split_heads(qkv_rows, model_width)
    scores = jnp.einsum("shd,thd->hst", query_rows, key_rows, preferred_element_type=f32)
    masked = jnp.where(allowed[None], scores * score_scale, masked_value)
    prob = jnp.exp(masked - log_norm)
    grad_prob = jnp.einsum("shd,thd->hst", grad_mixed, value_rows, preferred_element_type=f32)
    grad_value = jnp.einsum(
        "hst,shd->thd", prob.astype(bf16), grad_mixed, preferred_element_type=f32
    )
    grad_score = prob * (grad_prob - jnp.sum(prob * grad_prob, axis=-1, keepdims=True))
    grad_score = grad_score.astype(bf16)
    grad_query = (
        jnp.einsum("hst,thd->shd", grad_score, key_rows, preferred_element_type=f32) * score_scale
    )
    grad_key = (
        jnp.einsum("hst,shd->thd", grad_score, query_rows, preferred_element_type=f32) * score_scale
    )
    return jnp.concatenate(
        [part.reshape(seq_len, model_width) for part in (grad_query, grad_key, grad_value)], axis=1
    ).astype(bf16)


def on_device(
    tokens,
    segment_ids,
    routes,
    cotangent,
    w_qkv,
    w_attn_out,
    w_router,
    gain_attn,
    gain_moe,
    w_expert_in,
    w_expert_out,
):
    micro_count, _, seq_len, model_width = tokens.shape
    experts = w_router.shape[1]
    capacity = (9 * seq_len + 8 * experts - 1) // (8 * experts)
    padded = (capacity + 7) // 8 * 8
    block = lax.axis_index("dp")
    expert = lax.axis_index("expert")
    chips = model_width // w_qkv.shape[0] // 8
    micros = range(micro_count)

    shard = w_qkv.shape[0]
    packed = jnp.concatenate(
        [
            w_qkv,
            w_attn_out,
            w_router,
            gain_attn[:, None],
            gain_moe[:, None],
            jnp.zeros((shard, 128 - 2 - experts), bf16),
        ],
        axis=1,
    )
    gathered = gather_rows(packed, chips)
    full_qkv = gathered[:, : 3 * model_width]
    full_out = gathered[:, 3 * model_width : 4 * model_width]
    small = gathered[:, 4 * model_width :]
    router = small[:, :experts]
    gain_one = small[:, experts].astype(f32)[None]
    gain_two = small[:, experts + 1].astype(f32)[None]

    choices = [route_selector(routes[m, 0, :, 0], experts, capacity, padded) for m in micros]
    w_in, w_out = fetch_expert_weights(w_expert_in[0], w_expert_out[0], block)

    def dispatch(selector, rows):
        slots = mm_tn(selector, rows).astype(bf16)
        got = to_experts(slots.reshape(experts, padded, model_width)).reshape(-1, model_width)
        return jnp.concatenate([got, swap_y(got)], axis=0)

    def give_back(partial):
        rows = partial.shape[0] // 2
        total = partial[:rows] + swap_y(partial[rows:].astype(bf16)).astype(f32)
        total = total.astype(bf16).reshape(experts, padded, model_width)
        return to_experts(total).reshape(-1, model_width)

    grad_slots = [dispatch(choices[m][1], cotangent[m, 0]) for m in micros]

    state = []
    for m in micros:
        inputs = tokens[m, 0].astype(f32)
        normed_one, inv_one = normalize(inputs)
        attn_in = (normed_one * gain_one).astype(bf16)
        qkv_rows, allowed, log_norm, mixed = attention_forward(attn_in, segment_ids[m, 0], full_qkv)
        residual = inputs + mm(mixed, full_out)
        normed_two, inv_two = normalize(residual)
        hidden = (normed_two * gain_two).astype(bf16)
        one_hot, selector = choices[m]
        received = dispatch(selector, hidden)
        router_prob = jax.nn.softmax(mm(hidden, router), axis=-1)
        gate = jnp.sum(router_prob * one_hot, axis=1, keepdims=True)
        state.append(
            dict(
                normed_one=normed_one,
                inv_one=inv_one,
                attn_in=attn_in,
                qkv_rows=qkv_rows,
                allowed=allowed,
                log_norm=log_norm,
                mixed=mixed,
                residual=residual,
                normed_two=normed_two,
                inv_two=inv_two,
                hidden=hidden,
                one_hot=one_hot,
                selector=selector,
                received=received,
                router_prob=router_prob,
                gate=gate,
            )
        )

    for m in micros:
        s = state[m]
        own_prob = jax.nn.softmax(mm(s["received"], router), axis=-1)
        picked = (lax.iota(jnp.int32, experts) == expert).astype(f32)[None]
        own_gate = jnp.sum(own_prob * picked, axis=1, keepdims=True)
        s["gz"] = (own_gate * grad_slots[m].astype(f32)).astype(bf16)
        pre_act = mm(s["received"], w_in)
        s["act"] = jax.nn.gelu(pre_act).astype(bf16)
        s["returned"] = give_back(mm(s["act"], w_out))
        slope = jax.vjp(jax.nn.gelu, pre_act)[1]
        s["gu"] = slope(mm_nt(s["gz"], w_out))[0].astype(bf16)
        s["grad_back"] = give_back(mm_nt(s["gu"], w_in))
    both = lambda name: jnp.concatenate([s[name] for s in state], axis=0)
    grad_w_out = mm_tn(both("act"), both("gz"))
    grad_w_in = mm_tn(both("received"), both("gu"))
    grad_in, grad_out = reduce_expert_grads(grad_w_in, grad_w_out, block)

    outputs = []
    for m in micros:
        s = state[m]
        g = cotangent[m, 0].astype(f32)
        moe_rows = mm(s["selector"], s["returned"])
        outputs.append((s["residual"] + s["gate"] * moe_rows).astype(bf16))
        grad_gate = jnp.sum(g * moe_rows, axis=1, keepdims=True)
        choice = s["one_hot"] * grad_gate
        prob = s["router_prob"]
        s["grad_logit"] = (prob * (choice - jnp.sum(prob * choice, axis=1, keepdims=True))).astype(bf16)
        grad_hidden = mm(s["selector"], s["grad_back"]) + mm_nt(s["grad_logit"], router)
        s["gain_moe"] = jnp.sum(grad_hidden * s["normed_two"], axis=0)
        grad_resid = g + norm_back(grad_hidden * gain_two, s["normed_two"], s["inv_two"])
        s["grad_branch"] = grad_resid.astype(bf16)
        grad_mixed = mm_nt(s["grad_branch"], full_out).astype(bf16)
        s["grad_qkv"] = attention_backward(grad_mixed, s["qkv_rows"], s["allowed"], s["log_norm"])
        grad_attn_in = mm_nt(s["grad_qkv"], full_qkv)
        s["gain_attn"] = jnp.sum(grad_attn_in * s["normed_one"], axis=0)
        s["grad_tokens"] = grad_resid + norm_back(
            grad_attn_in * gain_one, s["normed_one"], s["inv_one"]
        )

    term_router = mm_tn(both("hidden"), both("grad_logit"))
    term_out = mm_tn(both("mixed"), both("grad_branch")).astype(bf16)
    term_qkv = mm_tn(both("attn_in"), both("grad_qkv")).astype(bf16)
    gain_moe_sum = sum(s["gain_moe"] for s in state)[:, None]
    gain_attn_sum = sum(s["gain_attn"] for s in state)[:, None]
    spare = jnp.zeros((model_width, 128 - 2 - experts), f32)
    term_small = jnp.concatenate([term_router, gain_attn_sum, gain_moe_sum, spare], axis=1)
    grad_qkv, grad_attn_out, small_sum = reduce_rows(
        (term_qkv, term_out, term_small.astype(bf16)), chips
    )
    return (
        jnp.stack(outputs)[:, None],
        jnp.stack([s["grad_tokens"] for s in state])[:, None],
        grad_qkv,
        grad_attn_out,
        small_sum[:, :experts],
        small_sum[:, experts],
        small_sum[:, experts + 1],
        grad_in[None],
        grad_out[None],
    )


def solution(mesh):
    rows = P(("dp", "expert"))
    seqs = P(None, ("dp", "expert"))
    owned = P("expert", "dp", None)
    return jax.shard_map(
        on_device,
        mesh=mesh,
        in_specs=(seqs, seqs, seqs, seqs, rows, rows, rows, rows, rows, owned, owned),
        out_specs=(seqs, seqs, rows, rows, rows, rows, rows, owned, owned),
        check_vma=False,
    )
```

```python
import functools
import math

import jax
import jax.numpy as jnp
from jax import lax
from jax.experimental import pallas as pl
from jax.experimental.pallas import tpu as pltpu
from jax.sharding import PartitionSpec as P

HEADS = 16
epsilon = 1e-05
masked_value = -1e30
f32 = jnp.float32
bf16 = jnp.bfloat16

MESH = pl.DeviceIdType.MESH
DMA = pltpu.SemaphoreType.DMA


def flip(index, mask):
    bit = 1
    while bit <= mask:
        if mask & bit:
            index = index + bit - 2 * bit * ((index // bit) % 2)
        bit *= 2
    return index


def place_of(chips):
    block = lax.axis_index("dp")
    owner = lax.axis_index("expert")
    peer_x = {"dp": flip(block, 1)}
    peer_y = {"dp": flip(block, 2)}
    peer_core = {"expert": flip(owner, 1)}
    peers_z = [{"expert": flip(owner, 2 * k)} for k in range(chips)]
    return block, owner // 2, owner % 2, peer_x, peer_y, peer_core, peers_z


def greet(peers):
    barrier = pltpu.get_barrier_semaphore()
    for peer in peers:
        pl.semaphore_signal(barrier, inc=1, device_id=peer, device_id_type=MESH)
    pl.semaphore_wait(barrier, len(peers))


def send(src, dst, send_sem, recv_sem, peer):
    copy = pltpu.make_async_remote_copy(
        src_ref=src, dst_ref=dst, send_sem=send_sem, recv_sem=recv_sem,
        device_id=peer, device_id_type=MESH,
    )
    copy.start()
    return copy


def gather_kernel(chips, cut, shard, full, own_sem, sz, rz, sx, rx, sy, ry, sc, rc):
    block, chip, core, peer_x, peer_y, peer_core, peers_z = place_of(chips)
    rows, width = shard.shape
    halves = (pl.ds(0, cut), pl.ds(cut, width - cut))
    every = pl.ds(0, width)

    def part(origin, step, columns):
        start = ((flip(block, origin) * chips + flip(chip, step)) * 2 + core) * rows
        return full.at[pl.ds(pl.multiple_of(start, rows), rows), columns]

    greet([peer_x, peer_y, peer_core] + peers_z[1:])
    own = pltpu.make_async_copy(shard, part(0, 0, every), own_sem)
    own.start()
    along_z = [None] + [
        send(shard, part(0, 0, every), sz.at[k], rz.at[k], peers_z[k]) for k in range(1, chips)
    ]
    along_x = [[None] * 3 for _ in range(chips)]
    along_y = [[None] * 3 for _ in range(chips)]
    across = [[None] * 4 for _ in range(chips)]

    def to_core(k, origin):
        src = shard if k == 0 and origin == 0 else part(origin, k, every)
        across[k][origin] = send(
            src, part(origin, k, every), sc.at[k, origin], rc.at[k, origin], peer_core
        )

    def pass_on(k):
        along_x[k][1].wait_recv()
        to_core(k, 1)
        along_y[k][1].wait_recv()
        to_core(k, 2)
        along_x[k][2].wait_recv()
        along_y[k][2].wait_recv()
        to_core(k, 3)

    for k in range(chips):
        if k:
            along_z[k].wait_recv()
        for turn in range(2):
            first = turn
            for copies, s, r, peer, half in (
                (along_x, sx, rx, peer_x, first),
                (along_y, sy, ry, peer_y, 1 - first),
            ):
                dst = part(0, k, halves[half])
                src = dst if k else shard.at[:, halves[half]]
                copies[k][turn] = send(src, dst, s.at[k, turn], r.at[k, turn], peer)
        to_core(k, 0)
        if k:
            pass_on(k - 1)
        along_x[k][0].wait_recv()
        piece = part(1, k, halves[0])
        along_y[k][2] = send(piece, piece, sy.at[k, 2], ry.at[k, 2], peer_y)
        along_y[k][0].wait_recv()
        piece = part(2, k, halves[1])
        along_x[k][2] = send(piece, piece, sx.at[k, 2], rx.at[k, 2], peer_x)
    pass_on(chips - 1)
    own.wait()
    for k in range(chips):
        if k:
            along_z[k].wait_send()
        for turn in range(3):
            along_x[k][turn].wait_send()
            along_y[k][turn].wait_send()
        for origin in range(4):
            across[k][origin].wait()


def gather_rows(shard, chips):
    rows, width = shard.shape
    cut = (width // 128 + 1) // 2 * 128
    total = 4 * chips * 2 * rows
    return pl.pallas_call(
        functools.partial(gather_kernel, chips, cut),
        out_shape=jax.ShapeDtypeStruct((total, width), shard.dtype),
        in_specs=[pl.BlockSpec(memory_space=pl.ANY)],
        out_specs=pl.BlockSpec(memory_space=pl.ANY),
        scratch_shapes=[
            DMA,
            DMA((chips,)),
            DMA((chips,)),
            DMA((chips, 3)),
            DMA((chips, 3)),
            DMA((chips, 3)),
            DMA((chips, 3)),
            DMA((chips, 4)),
            DMA((chips, 4)),
        ],
        compiler_params=pltpu.CompilerParams(collective_id=1, has_side_effects=True),
        name="gather_rows",
    )(shard)


def reduce_kernel(chips, cut, widths, *refs):
    n = len(widths)
    grads, outs = refs[:n], refs[n : 2 * n]
    total, crecv, xrecv, yrecv, zrecv, part_z = refs[2 * n : 2 * n + 6]
    la, sc, rc, sx, rx, sy, ry, sz, rz = refs[2 * n + 6 :]
    block, chip, core, peer_x, peer_y, peer_core, peers_z = place_of(chips)
    rows, width = zrecv.shape[1:]
    wide = width - cut
    left, right = pl.ds(0, cut), pl.ds(cut, wide)
    columns = []
    for w in widths:
        columns.append(pl.ds(sum(widths[: len(columns)]), w))
    order = list(range(chips - 1, -1, -1))
    opposite = flip(core, 1)
    greet([peer_x, peer_y, peer_core] + peers_z[1:])
    across, local = {}, {}
    for k in order:
        step = flip(chip, k)
        across[k], local[k] = [], []
        for i in range(n):
            across[k].append(
                send(
                    grads[i].at[:, step, opposite],
                    crecv.at[:, step, :, columns[i]],
                    sc.at[k, i], rc.at[k, i], peer_core,
                )
            )
            copy = pltpu.make_async_copy(
                grads[i].at[:, step, core], total.at[:, step, :, columns[i]], la.at[k, i]
            )
            copy.start()
            local[k].append(copy)

    def spot(k, origin, cols):
        return (flip(block, origin), flip(chip, k), slice(None), cols)

    along_x, along_y, along_z = {}, {}, {}

    def begin(k):
        for i in range(n):
            local[k][i].wait()
            across[k][i].wait_recv()
        step = flip(chip, k)
        for origin in (3, 1, 2, 0):
            at = (flip(block, origin), step)
            total[at] = (total[at].astype(f32) + crecv[at].astype(f32)).astype(bf16)
            if origin == 3:
                along_x[k, 0] = send(
                    total.at[spot(k, 3, left)], xrecv.at[k, 0, :, left], sx.at[k, 0], rx.at[k, 0], peer_x
                )
                along_y[k, 0] = send(
                    total.at[spot(k, 3, right)], yrecv.at[k, 0, :, pl.ds(0, wide)], sy.at[k, 0], ry.at[k, 0], peer_y
                )
            if origin == 1:
                along_x[k, 1] = send(
                    total.at[spot(k, 1, left)], xrecv.at[k, 1, :, left], sx.at[k, 1], rx.at[k, 1], peer_x
                )
            if origin == 2:
                along_y[k, 1] = send(
                    total.at[spot(k, 2, right)], yrecv.at[k, 1, :, pl.ds(0, wide)], sy.at[k, 1], ry.at[k, 1], peer_y
                )

    def relay(k):
        along_x[k, 0].wait_recv()
        at = spot(k, 2, left)
        total[at] = (total[at].astype(f32) + xrecv[k, 0, :, left].astype(f32)).astype(bf16)
        along_y[k, 2] = send(total.at[at], yrecv.at[k, 2, :, left], sy.at[k, 2], ry.at[k, 2], peer_y)
        along_y[k, 0].wait_recv()
        at = spot(k, 1, right)
        total[at] = (total[at].astype(f32) + yrecv[k, 0, :, pl.ds(0, wide)].astype(f32)).astype(bf16)
        along_x[k, 2] = send(
            total.at[at], xrecv.at[k, 2, :, pl.ds(0, wide)], sx.at[k, 2], rx.at[k, 2], peer_x
        )

    def finish(k):
        for turn in (1, 2):
            along_x[k, turn].wait_recv()
            along_y[k, turn].wait_recv()
        lhs = (
            total[spot(k, 0, left)].astype(f32)
            + xrecv[k, 1, :, left].astype(f32)
            + yrecv[k, 2, :, left].astype(f32)
        )
        rhs = (
            total[spot(k, 0, right)].astype(f32)
            + yrecv[k, 1, :, pl.ds(0, wide)].astype(f32)
            + xrecv[k, 2, :, pl.ds(0, wide)].astype(f32)
        )
        if k:
            part_z[k, :, left] = lhs.astype(bf16)
            part_z[k, :, right] = rhs.astype(bf16)
            along_z[k] = send(part_z.at[k], zrecv.at[k], sz.at[k], rz.at[k], peers_z[k])
        else:
            for j in range(1, chips):
                along_z[j].wait_recv()
                lhs = lhs + zrecv[j, :, left].astype(f32)
                rhs = rhs + zrecv[j, :, right].astype(f32)
            start = 0
            for i, w in enumerate(widths):
                for lo, hi, value in ((0, cut, lhs), (cut, width, rhs)):
                    a, b = max(start, lo), min(start + w, hi)
                    if a < b:
                        outs[i][:, a - start : b - start] = value[:, a - lo : b - lo]
                start += w

    for i in range(chips + 2):
        if i < chips:
            begin(order[i])
        if 0 <= i - 1 < chips:
            relay(order[i - 1])
        if i - 2 >= 0:
            finish(order[i - 2])
    for k in order:
        for i in range(n):
            across[k][i].wait_send()
        for turn in range(3):
            along_x[k, turn].wait_send()
            along_y[k, turn].wait_send()
        if k:
            along_z[k].wait_send()


def reduce_rows(grads, chips):
    rows = grads[0].shape[0] // (8 * chips)
    widths = tuple(g.shape[1] for g in grads)
    width = sum(widths)
    cut = (width // 128 + 1) // 2 * 128
    n = len(grads)
    return pl.pallas_call(
        functools.partial(reduce_kernel, chips, cut, widths),
        out_shape=[jax.ShapeDtypeStruct((rows, w), f32) for w in widths],
        in_specs=[pl.BlockSpec(memory_space=pl.ANY)] * n,
        out_specs=[pl.BlockSpec(memory_space=pltpu.VMEM)] * n,
        scratch_shapes=[
            pltpu.VMEM((4, chips, rows, width), bf16),
            pltpu.VMEM((4, chips, rows, width), bf16),
            pltpu.VMEM((chips, 3, rows, cut), bf16),
            pltpu.VMEM((chips, 3, rows, cut), bf16),
            pltpu.VMEM((chips, rows, width), bf16),
            pltpu.VMEM((chips, rows, width), bf16),
            DMA((chips, n)),
            DMA((chips, n)),
            DMA((chips, n)),
            DMA((chips, 3)),
            DMA((chips, 3)),
            DMA((chips, 3)),
            DMA((chips, 3)),
            DMA((chips,)),
            DMA((chips,)),
        ],
        compiler_params=pltpu.CompilerParams(collective_id=2, has_side_effects=True),
        name="reduce_rows",
    )(*[g.reshape(4, chips, 2, rows, g.shape[1]) for g in grads])


PAIR_X = tuple((b, b ^ 1) for b in range(4))
PAIR_Y = tuple((b, b ^ 2) for b in range(4))
PAIR_XY = tuple((b, b ^ 3) for b in range(4))


def swap_x(a):
    return lax.ppermute(a, "dp", PAIR_X)


def swap_y(a):
    return lax.ppermute(a, "dp", PAIR_Y)


def to_experts(a):
    return lax.all_to_all(a, "expert", split_axis=0, concat_axis=0, tiled=True)


def swap_xy(a):
    return lax.ppermute(a, "dp", PAIR_XY)


def normalize(values):
    row_mean = jnp.mean(values, axis=-1, keepdims=True)
    centered = values - row_mean
    inv_scale = lax.rsqrt(jnp.mean(centered * centered, axis=-1, keepdims=True) + epsilon)
    return (centered * inv_scale, inv_scale)


def norm_back(grad_normed, normed, inv_scale):
    return inv_scale * (
        grad_normed
        - jnp.mean(grad_normed, axis=-1, keepdims=True)
        - normed * jnp.mean(grad_normed * normed, axis=-1, keepdims=True)
    )


def dot(a, b):
    return jnp.dot(a, b, preferred_element_type=f32)


def dot_nt(a, b):
    return lax.dot_general(a, b, (((1,), (1,)), ((), ())), preferred_element_type=f32)


def dot_tn(a, b):
    return lax.dot_general(a, b, (((0,), (0,)), ((), ())), preferred_element_type=f32)


def lanes_of(shape):
    return lax.broadcasted_iota(jnp.int32, shape, 1)


def rows_of(shape):
    return lax.broadcasted_iota(jnp.int32, shape, 0)


def forward_kernel(
    experts,
    x_ref,
    seg_col_ref,
    seg_row_ref,
    slot_row_ref,
    full_ref,
    gains_ref,
    a_ref,
    qkv_ref,
    lse_ref,
    o_ref,
    y1_ref,
    h_ref,
    prob_ref,
    slots_ref,
):
    seq_len, model_width = x_ref.shape
    scale = 1.0 / math.sqrt(model_width // HEADS)
    x = x_ref[...].astype(f32)
    a_ref[...] = (normalize(x)[0] * gains_ref[0:1, :]).astype(bf16)

    @pl.loop(0, 3 * model_width // 512)
    def _(j):
        at = pl.ds(pl.multiple_of(j * 512, 512), 512)
        qkv_ref[:, at] = dot(a_ref[...], full_ref[:, at]).astype(bf16)

    square = (seq_len, seq_len)
    allowed = (lanes_of(square) <= rows_of(square)) & (seg_col_ref[...] == seg_row_ref[...])
    low_half = lanes_of((seq_len, 128)) < 64
    lse_ref[...] = jnp.zeros_like(lse_ref)

    @pl.loop(0, model_width // 128)
    def _(pair):
        at = pl.multiple_of(pair * 128, 128)
        query = qkv_ref[:, pl.ds(at, 128)]
        key = qkv_ref[:, pl.ds(model_width + at, 128)]
        value = qkv_ref[:, pl.ds(2 * model_width + at, 128)]
        mixed = []
        for side in range(2):
            mine = low_half if side == 0 else jnp.logical_not(low_half)
            scores = dot_nt(jnp.where(mine, query, 0.0).astype(bf16), key) * scale
            masked = jnp.where(allowed, scores, masked_value)
            top = jnp.max(masked, axis=1, keepdims=True)
            weight = jnp.exp(masked - top)
            norm = jnp.sum(weight, axis=1, keepdims=True)
            mixed.append(dot((weight / norm).astype(bf16), value))
            head = lanes_of(lse_ref.shape) == 2 * pair + side
            lse_ref[...] = jnp.where(head, top + jnp.log(norm), lse_ref[...])
        o_ref[:, pl.ds(at, 128)] = jnp.where(low_half, mixed[0], mixed[1]).astype(bf16)

    y1 = x + dot(o_ref[...], full_ref[:, pl.ds(3 * model_width, model_width)])
    y1_ref[...] = y1
    hidden = (normalize(y1)[0] * gains_ref[1:2, :]).astype(bf16)
    h_ref[...] = hidden
    logits = dot(hidden, full_ref[:, pl.ds(4 * model_width, 128)])
    real = lanes_of(logits.shape) < experts
    logits = jnp.where(real, logits, masked_value)
    weight = jnp.where(real, jnp.exp(logits - jnp.max(logits, axis=1, keepdims=True)), 0.0)
    prob_ref[...] = weight / jnp.sum(weight, axis=1, keepdims=True)
    spots = (slots_ref.shape[0], seq_len)
    chosen = jnp.where(rows_of(spots) == slot_row_ref[...], 1.0, 0.0).astype(bf16)
    slots_ref[...] = dot(chosen, hidden).astype(bf16)


def backward_kernel(
    x_ref,
    g_ref,
    seg_col_ref,
    seg_row_ref,
    slot_col_ref,
    route_col_ref,
    full_ref,
    gains_ref,
    qkv_ref,
    lse_ref,
    y1_ref,
    prob_ref,
    returned_ref,
    back_ref,
    out_ref,
    grad_x_ref,
    branch_ref,
    gqkv_ref,
    glog_ref,
    gain_ref,
    go_ref,
    gy1_ref,
):
    seq_len, model_width = x_ref.shape
    scale = 1.0 / math.sqrt(model_width // HEADS)
    g = g_ref[...].astype(f32)
    spots = (seq_len, returned_ref.shape[0])
    chosen = jnp.where(lanes_of(spots) == slot_col_ref[...], 1.0, 0.0).astype(bf16)
    moe = dot(chosen, returned_ref[...])
    prob = prob_ref[...]
    one_hot = jnp.where(lanes_of(prob.shape) == route_col_ref[...], 1.0, 0.0)
    gate = jnp.sum(prob * one_hot, axis=1, keepdims=True)
    y1 = y1_ref[...]
    out_ref[...] = (y1 + gate * moe).astype(bf16)
    choice = one_hot * jnp.sum(g * moe, axis=1, keepdims=True)
    glog = (prob * (choice - jnp.sum(prob * choice, axis=1, keepdims=True))).astype(bf16)
    glog_ref[...] = glog
    grad_h = dot(chosen, back_ref[...]) + dot_nt(glog, full_ref[:, pl.ds(4 * model_width, 128)])
    n2, inv2 = normalize(y1)
    gain_ref[1:2, :] = jnp.sum(grad_h * n2, axis=0, keepdims=True)
    gy1 = g + norm_back(grad_h * gains_ref[1:2, :], n2, inv2)
    gy1_ref[...] = gy1
    branch_ref[...] = gy1.astype(bf16)
    go_ref[...] = dot_nt(branch_ref[...], full_ref[:, pl.ds(3 * model_width, model_width)]).astype(bf16)

    square = (seq_len, seq_len)
    allowed = (lanes_of(square) <= rows_of(square)) & (seg_col_ref[...] == seg_row_ref[...])
    low_half = lanes_of((seq_len, 128)) < 64

    @pl.loop(0, model_width // 128)
    def _(pair):
        at = pl.multiple_of(pair * 128, 128)
        query = qkv_ref[:, pl.ds(at, 128)]
        key = qkv_ref[:, pl.ds(model_width + at, 128)]
        value = qkv_ref[:, pl.ds(2 * model_width + at, 128)]
        grad_o = go_ref[:, pl.ds(at, 128)]
        parts = []
        for side in range(2):
            mine = low_half if side == 0 else jnp.logical_not(low_half)
            scores = dot_nt(jnp.where(mine, query, 0.0).astype(bf16), key) * scale
            head = lanes_of(lse_ref.shape) == 2 * pair + side
            lse = jnp.sum(jnp.where(head, lse_ref[...], 0.0), axis=1, keepdims=True)
            p = jnp.exp(jnp.where(allowed, scores, masked_value) - lse)
            gp = dot_nt(jnp.where(mine, grad_o, 0.0).astype(bf16), value)
            gs = (p * (gp - jnp.sum(p * gp, axis=1, keepdims=True))).astype(bf16)
            parts.append((dot(gs, key) * scale, dot_tn(gs, query) * scale, dot_tn(p.astype(bf16), grad_o)))
        for i in range(3):
            both = jnp.where(low_half, parts[0][i], parts[1][i]).astype(bf16)
            gqkv_ref[:, pl.ds(i * model_width + at, 128)] = both

    ga = dot_nt(gqkv_ref[...], full_ref[:, pl.ds(0, 3 * model_width)])
    n1, inv1 = normalize(x_ref[...].astype(f32))
    gain_ref[0:1, :] = jnp.sum(ga * n1, axis=0, keepdims=True)
    grad_x_ref[...] = gy1_ref[...] + norm_back(ga * gains_ref[0:1, :], n1, inv1)


def kernel_params(flops):
    return dict(
        compiler_params=pltpu.CompilerParams(vmem_limit_bytes=56 * 2**20),
        cost_estimate=pl.CostEstimate(flops=flops, bytes_accessed=2**20, transcendentals=0),
    )


def attention_forward(x, seg_col, seg_row, slot_row, full, gains, experts, spots):
    seq_len, model_width = x.shape
    shape = jax.ShapeDtypeStruct
    return pl.pallas_call(
        functools.partial(forward_kernel, experts),
        out_shape=[
            shape((seq_len, model_width), bf16),
            shape((seq_len, 3 * model_width), bf16),
            shape((seq_len, 128), f32),
            shape((seq_len, model_width), bf16),
            shape((seq_len, model_width), f32),
            shape((seq_len, model_width), bf16),
            shape((seq_len, 128), f32),
            shape((spots, model_width), bf16),
        ],
        name="attention_forward",
        **kernel_params(20 * 10**9),
    )(x, seg_col, seg_row, slot_row, full, gains)


def attention_backward(*operands):
    seq_len, model_width = operands[0].shape
    shape = jax.ShapeDtypeStruct
    return pl.pallas_call(
        backward_kernel,
        out_shape=[
            shape((seq_len, model_width), bf16),
            shape((seq_len, model_width), f32),
            shape((seq_len, model_width), bf16),
            shape((seq_len, 3 * model_width), bf16),
            shape((seq_len, 128), bf16),
            shape((2, model_width), f32),
        ],
        scratch_shapes=[
            pltpu.VMEM((seq_len, model_width), bf16),
            pltpu.VMEM((seq_len, model_width), f32),
        ],
        name="attention_backward",
        **kernel_params(30 * 10**9),
    )(*operands)


def slots_of(route_row, experts, capacity, padded):
    seq_len = route_row.shape[0]
    one_hot = (route_row[:, None] == lax.iota(jnp.int32, experts)[None, :]).astype(f32)
    position = lax.iota(jnp.int32, seq_len)
    before = (position[None, :] < position[:, None]).astype(bf16)
    place = jnp.sum(dot(before, one_hot.astype(bf16)) * one_hot, axis=1).astype(jnp.int32)
    return jnp.where(place < capacity, route_row * padded + place, -1)


def fetch_expert_weights(w_in, w_out, block):
    rows, width = w_in.shape
    half = width // 2
    row_y, row_x = block // 2, block % 2
    mine = lax.dynamic_slice(w_in, (0, row_y * half), (rows, half))
    theirs = lax.dynamic_slice(w_in, (0, (1 - row_y) * half), (rows, half))
    from_y = swap_y(theirs)
    from_x = swap_x(mine)
    from_xy = swap_xy(theirs)
    out_x = swap_x(w_out)
    full_in = jnp.zeros((4, rows, half), w_in.dtype)
    for part, place in ((mine, block), (from_y, block ^ 2), (from_x, block ^ 1), (from_xy, block ^ 3)):
        full_in = lax.dynamic_update_slice(full_in, part[None], (place, 0, 0))
    full_out = jnp.zeros((2,) + w_out.shape, w_out.dtype)
    full_out = lax.dynamic_update_slice(full_out, w_out[None], (row_x, 0, 0))
    full_out = lax.dynamic_update_slice(full_out, out_x[None], (1 - row_x, 0, 0))
    return full_in.reshape(4 * rows, half), full_out.reshape(-1, w_out.shape[1])


def reduce_expert_grads(grad_in, grad_out, block):
    rows = grad_in.shape[0] // 4
    half = grad_in.shape[1]
    row_y, row_x = block // 2, block % 2
    parts_out = grad_out.reshape(2, -1, grad_out.shape[1])
    keep_out = lax.dynamic_slice_in_dim(parts_out, row_x, 1, 0)[0]
    send_out = lax.dynamic_slice_in_dim(parts_out, 1 - row_x, 1, 0)[0].astype(bf16)
    done_out = keep_out + swap_x(send_out).astype(f32)
    parts_in = grad_in.reshape(2, 2, rows, half)
    keep_in = lax.dynamic_slice_in_dim(parts_in, row_x, 1, 1)[:, 0]
    send_in = lax.dynamic_slice_in_dim(parts_in, 1 - row_x, 1, 1)[:, 0].astype(bf16)
    sums = keep_in + swap_x(send_in).astype(f32)
    own = lax.dynamic_slice_in_dim(sums, row_y, 1, 0)[0]
    other = lax.dynamic_slice_in_dim(sums, 1 - row_y, 1, 0)[0].astype(bf16)
    got = swap_y(other).astype(f32)
    done_in = jnp.zeros((rows, 2 * half), f32)
    done_in = lax.dynamic_update_slice(done_in, own, (0, row_y * half))
    done_in = lax.dynamic_update_slice(done_in, got, (0, (1 - row_y) * half))
    return done_in, done_out


def on_device(
    tokens,
    segment_ids,
    routes,
    cotangent,
    w_qkv,
    w_attn_out,
    w_router,
    gain_attn,
    gain_moe,
    w_expert_in,
    w_expert_out,
):
    micro_count, _, seq_len, model_width = tokens.shape
    experts = w_router.shape[1]
    capacity = (9 * seq_len + 8 * experts - 1) // (8 * experts)
    padded = (capacity + 7) // 8 * 8
    block = lax.axis_index("dp")
    expert = lax.axis_index("expert")
    chips = model_width // w_qkv.shape[0] // 8
    micros = range(micro_count)

    shard = w_qkv.shape[0]
    packed = jnp.concatenate(
        [
            w_qkv,
            w_attn_out,
            w_router,
            gain_attn[:, None],
            gain_moe[:, None],
            jnp.zeros((shard, 128 - 2 - experts), bf16),
        ],
        axis=1,
    )
    gathered = gather_rows(packed, chips)
    small = gathered[:, 4 * model_width :]
    router = small[:, :experts]
    gains = small[:, experts : experts + 2].astype(f32).T

    spots = experts * padded
    slot = [slots_of(routes[m, 0, :, 0], experts, capacity, padded) for m in micros]
    w_in, w_out = fetch_expert_weights(w_expert_in[0], w_expert_out[0], block)

    def dispatch(slots):
        got = to_experts(slots.reshape(experts, padded, model_width)).reshape(-1, model_width)
        return jnp.concatenate([got, swap_y(got)], axis=0)

    def give_back(partial):
        rows = partial.shape[0] // 2
        total = partial[:rows] + swap_y(partial[rows:].astype(bf16)).astype(f32)
        total = total.astype(bf16).reshape(experts, padded, model_width)
        return to_experts(total).reshape(-1, model_width)

    grad_slots = []
    for m in micros:
        chosen = (lax.iota(jnp.int32, spots)[:, None] == slot[m][None]).astype(bf16)
        grad_slots.append(dispatch(dot(chosen, cotangent[m, 0]).astype(bf16)))

    state = []
    for m in micros:
        segments = segment_ids[m, 0]
        names = ("attn_in", "qkv", "lse", "mixed", "residual", "hidden", "prob", "slots")
        s = dict(
            zip(
                names,
                attention_forward(
                    tokens[m, 0],
                    segments[:, None],
                    segments[None],
                    slot[m][None],
                    gathered,
                    gains,
                    experts,
                    spots,
                ),
            )
        )
        s["received"] = dispatch(s["slots"])
        state.append(s)

    for m in micros:
        s = state[m]
        own_prob = jax.nn.softmax(dot(s["received"], router), axis=-1)
        picked = (lax.iota(jnp.int32, experts) == expert).astype(f32)[None]
        own_gate = jnp.sum(own_prob * picked, axis=1, keepdims=True)
        s["gz"] = (own_gate * grad_slots[m].astype(f32)).astype(bf16)
        pre_act = dot(s["received"], w_in)
        s["act"] = jax.nn.gelu(pre_act).astype(bf16)
        s["returned"] = give_back(dot(s["act"], w_out))
        slope = jax.vjp(jax.nn.gelu, pre_act)[1]
        s["gu"] = slope(dot_nt(s["gz"], w_out))[0].astype(bf16)
        s["grad_back"] = give_back(dot_nt(s["gu"], w_in))
    both = lambda name: jnp.concatenate([s[name] for s in state], axis=0)
    grad_w_out = dot_tn(both("act"), both("gz"))
    grad_w_in = dot_tn(both("received"), both("gu"))
    grad_in, grad_out = reduce_expert_grads(grad_w_in, grad_w_out, block)

    for m in micros:
        s = state[m]
        segments = segment_ids[m, 0]
        names = ("output", "grad_tokens", "branch", "grad_qkv", "grad_logit", "gain")
        s.update(
            zip(
                names,
                attention_backward(
                    tokens[m, 0],
                    cotangent[m, 0],
                    segments[:, None],
                    segments[None],
                    slot[m][:, None],
                    routes[m, 0],
                    gathered,
                    gains,
                    s["qkv"],
                    s["lse"],
                    s["residual"],
                    s["prob"],
                    s["returned"],
                    s["grad_back"],
                ),
            )
        )
    term_router = dot_tn(both("hidden"), both("grad_logit"))[:, :experts]
    term_out = dot_tn(both("mixed"), both("branch")).astype(bf16)
    term_qkv = dot_tn(both("attn_in"), both("grad_qkv")).astype(bf16)
    gain_sum = sum(s["gain"] for s in state).T
    spare = jnp.zeros((model_width, 128 - 2 - experts), f32)
    term_small = jnp.concatenate([term_router, gain_sum, spare], axis=1).astype(bf16)
    grad_qkv, grad_attn_out, small_sum = reduce_rows((term_qkv, term_out, term_small), chips)
    return (
        jnp.stack([s["output"] for s in state])[:, None],
        jnp.stack([s["grad_tokens"] for s in state])[:, None],
        grad_qkv,
        grad_attn_out,
        small_sum[:, :experts],
        small_sum[:, experts],
        small_sum[:, experts + 1],
        grad_in[None],
        grad_out[None],
    )


def solution(mesh):
    rows = P(("dp", "expert"))
    seqs = P(None, ("dp", "expert"))
    owned = P("expert", "dp", None)
    return jax.shard_map(
        on_device,
        mesh=mesh,
        in_specs=(seqs, seqs, seqs, seqs, rows, rows, rows, rows, rows, owned, owned),
        out_specs=(seqs, seqs, rows, rows, rows, rows, rows, owned, owned),
        check_vma=False,
    )
```

```python
import functools
import math

import jax
import jax.numpy as jnp
from jax import lax
from jax.experimental import pallas as pl
from jax.experimental.pallas import tpu as pltpu
from jax.sharding import PartitionSpec as P

HEADS = 16
epsilon = 1e-05
masked_value = -1e30
f32 = jnp.float32
bf16 = jnp.bfloat16

MESH = pl.DeviceIdType.MESH
DMA = pltpu.SemaphoreType.DMA


def flip(index, mask):
    bit = 1
    while bit <= mask:
        if mask & bit:
            index = index + bit - 2 * bit * ((index // bit) % 2)
        bit *= 2
    return index


def place_of(chips):
    block = lax.axis_index("dp")
    owner = lax.axis_index("expert")
    peer_x = {"dp": flip(block, 1)}
    peer_y = {"dp": flip(block, 2)}
    peer_core = {"expert": flip(owner, 1)}
    peers_z = [{"expert": flip(owner, 2 * k)} for k in range(chips)]
    return block, owner // 2, owner % 2, peer_x, peer_y, peer_core, peers_z


def greet(peers):
    barrier = pltpu.get_barrier_semaphore()
    for peer in peers:
        pl.semaphore_signal(barrier, inc=1, device_id=peer, device_id_type=MESH)
    pl.semaphore_wait(barrier, len(peers))


def send(src, dst, send_sem, recv_sem, peer):
    copy = pltpu.make_async_remote_copy(
        src_ref=src, dst_ref=dst, send_sem=send_sem, recv_sem=recv_sem,
        device_id=peer, device_id_type=MESH,
    )
    copy.start()
    return copy


def reduce_kernel(chips, cut, widths, *refs):
    n = len(widths)
    grads, outs = refs[:n], refs[n : 2 * n]
    total, crecv, xrecv, yrecv, zrecv, part_z = refs[2 * n : 2 * n + 6]
    la, sc, rc, sx, rx, sy, ry, sz, rz = refs[2 * n + 6 :]
    block, chip, core, peer_x, peer_y, peer_core, peers_z = place_of(chips)
    rows, width = zrecv.shape[1:]
    wide = width - cut
    left, right = pl.ds(0, cut), pl.ds(cut, wide)
    columns = []
    for w in widths:
        columns.append(pl.ds(sum(widths[: len(columns)]), w))
    order = list(range(chips - 1, -1, -1))
    opposite = flip(core, 1)
    greet([peer_x, peer_y, peer_core] + peers_z[1:])
    across, local = {}, {}
    for k in order:
        step = flip(chip, k)
        across[k], local[k] = [], []
        for i in range(n):
            across[k].append(
                send(
                    grads[i].at[:, step, opposite],
                    crecv.at[:, step, :, columns[i]],
                    sc.at[k, i], rc.at[k, i], peer_core,
                )
            )
            copy = pltpu.make_async_copy(
                grads[i].at[:, step, core], total.at[:, step, :, columns[i]], la.at[k, i]
            )
            copy.start()
            local[k].append(copy)

    def spot(k, origin, cols):
        return (flip(block, origin), flip(chip, k), slice(None), cols)

    along_x, along_y, along_z = {}, {}, {}

    def begin(k):
        for i in range(n):
            local[k][i].wait()
            across[k][i].wait_recv()
        step = flip(chip, k)
        for origin in (3, 1, 2, 0):
            at = (flip(block, origin), step)
            total[at] = (total[at].astype(f32) + crecv[at].astype(f32)).astype(bf16)
            if origin == 3:
                along_x[k, 0] = send(
                    total.at[spot(k, 3, left)], xrecv.at[k, 0, :, left], sx.at[k, 0], rx.at[k, 0], peer_x
                )
                along_y[k, 0] = send(
                    total.at[spot(k, 3, right)], yrecv.at[k, 0, :, pl.ds(0, wide)], sy.at[k, 0], ry.at[k, 0], peer_y
                )
            if origin == 1:
                along_x[k, 1] = send(
                    total.at[spot(k, 1, left)], xrecv.at[k, 1, :, left], sx.at[k, 1], rx.at[k, 1], peer_x
                )
            if origin == 2:
                along_y[k, 1] = send(
                    total.at[spot(k, 2, right)], yrecv.at[k, 1, :, pl.ds(0, wide)], sy.at[k, 1], ry.at[k, 1], peer_y
                )

    def relay(k):
        along_x[k, 0].wait_recv()
        at = spot(k, 2, left)
        total[at] = (total[at].astype(f32) + xrecv[k, 0, :, left].astype(f32)).astype(bf16)
        along_y[k, 2] = send(total.at[at], yrecv.at[k, 2, :, left], sy.at[k, 2], ry.at[k, 2], peer_y)
        along_y[k, 0].wait_recv()
        at = spot(k, 1, right)
        total[at] = (total[at].astype(f32) + yrecv[k, 0, :, pl.ds(0, wide)].astype(f32)).astype(bf16)
        along_x[k, 2] = send(
            total.at[at], xrecv.at[k, 2, :, pl.ds(0, wide)], sx.at[k, 2], rx.at[k, 2], peer_x
        )

    def finish(k):
        for turn in (1, 2):
            along_x[k, turn].wait_recv()
            along_y[k, turn].wait_recv()
        lhs = (
            total[spot(k, 0, left)].astype(f32)
            + xrecv[k, 1, :, left].astype(f32)
            + yrecv[k, 2, :, left].astype(f32)
        )
        rhs = (
            total[spot(k, 0, right)].astype(f32)
            + yrecv[k, 1, :, pl.ds(0, wide)].astype(f32)
            + xrecv[k, 2, :, pl.ds(0, wide)].astype(f32)
        )
        if k:
            part_z[k, :, left] = lhs.astype(bf16)
            part_z[k, :, right] = rhs.astype(bf16)
            along_z[k] = send(part_z.at[k], zrecv.at[k], sz.at[k], rz.at[k], peers_z[k])
        else:
            for j in range(1, chips):
                along_z[j].wait_recv()
                lhs = lhs + zrecv[j, :, left].astype(f32)
                rhs = rhs + zrecv[j, :, right].astype(f32)
            start = 0
            for i, w in enumerate(widths):
                for lo, hi, value in ((0, cut, lhs), (cut, width, rhs)):
                    a, b = max(start, lo), min(start + w, hi)
                    if a < b:
                        outs[i][:, a - start : b - start] = value[:, a - lo : b - lo]
                start += w

    for i in range(chips + 2):
        if i < chips:
            begin(order[i])
        if 0 <= i - 1 < chips:
            relay(order[i - 1])
        if i - 2 >= 0:
            finish(order[i - 2])
    for k in order:
        for i in range(n):
            across[k][i].wait_send()
        for turn in range(3):
            along_x[k, turn].wait_send()
            along_y[k, turn].wait_send()
        if k:
            along_z[k].wait_send()


def reduce_rows(grads, chips):
    rows = grads[0].shape[0] // (8 * chips)
    widths = tuple(g.shape[1] for g in grads)
    width = sum(widths)
    cut = (width // 128 + 1) // 2 * 128
    n = len(grads)
    return pl.pallas_call(
        functools.partial(reduce_kernel, chips, cut, widths),
        out_shape=[jax.ShapeDtypeStruct((rows, w), f32) for w in widths],
        in_specs=[pl.BlockSpec(memory_space=pl.ANY)] * n,
        out_specs=[pl.BlockSpec(memory_space=pltpu.VMEM)] * n,
        scratch_shapes=[
            pltpu.VMEM((4, chips, rows, width), bf16),
            pltpu.VMEM((4, chips, rows, width), bf16),
            pltpu.VMEM((chips, 3, rows, cut), bf16),
            pltpu.VMEM((chips, 3, rows, cut), bf16),
            pltpu.VMEM((chips, rows, width), bf16),
            pltpu.VMEM((chips, rows, width), bf16),
            DMA((chips, n)),
            DMA((chips, n)),
            DMA((chips, n)),
            DMA((chips, 3)),
            DMA((chips, 3)),
            DMA((chips, 3)),
            DMA((chips, 3)),
            DMA((chips,)),
            DMA((chips,)),
        ],
        compiler_params=pltpu.CompilerParams(collective_id=2, has_side_effects=True),
        name="reduce_rows",
    )(*[g.reshape(4, chips, 2, rows, g.shape[1]) for g in grads])


PAIR_X = tuple((b, b ^ 1) for b in range(4))
PAIR_Y = tuple((b, b ^ 2) for b in range(4))


def swap_x(a):
    return lax.ppermute(a, "dp", PAIR_X)


def swap_y(a):
    return lax.ppermute(a, "dp", PAIR_Y)


def to_experts(a):
    return lax.all_to_all(a, "expert", split_axis=0, concat_axis=0, tiled=True)


def normalize(values):
    row_mean = jnp.mean(values, axis=-1, keepdims=True)
    centered = values - row_mean
    inv_scale = lax.rsqrt(jnp.mean(centered * centered, axis=-1, keepdims=True) + epsilon)
    return (centered * inv_scale, inv_scale)


def norm_back(grad_normed, normed, inv_scale):
    return inv_scale * (
        grad_normed
        - jnp.mean(grad_normed, axis=-1, keepdims=True)
        - normed * jnp.mean(grad_normed * normed, axis=-1, keepdims=True)
    )


def dot(a, b):
    return jnp.dot(a, b, preferred_element_type=f32)


def dot_nt(a, b):
    return lax.dot_general(a, b, (((1,), (1,)), ((), ())), preferred_element_type=f32)


def dot_tn(a, b):
    return lax.dot_general(a, b, (((0,), (0,)), ((), ())), preferred_element_type=f32)


def lanes_of(shape):
    return lax.broadcasted_iota(jnp.int32, shape, 1)


def rows_of(shape):
    return lax.broadcasted_iota(jnp.int32, shape, 0)


def column(row):
    return jnp.transpose(jnp.broadcast_to(row.astype(f32), (128, row.shape[1])))[:, :1]


def one_hot_of(route):
    return jnp.where(lanes_of((route.shape[0], 128)).astype(f32) == route, 1.0, 0.0)


def choose_slots(route, spots, experts):
    seq_len = route.shape[0]
    capacity = (9 * seq_len + 8 * experts - 1) // (8 * experts)
    one_hot = one_hot_of(route)
    square = (seq_len, seq_len)
    before = jnp.where(lanes_of(square) < rows_of(square), 1.0, 0.0).astype(bf16)
    place = jnp.sum(dot(before, one_hot.astype(bf16)) * one_hot, axis=1, keepdims=True)
    slot = jnp.where(place < capacity, route * (spots // experts) + place, -1.0)
    return jnp.where(lanes_of((seq_len, spots)).astype(f32) == slot, 1.0, 0.0).astype(bf16)


def allowed_pairs(segment_row):
    square = (segment_row.shape[1],) * 2
    same = column(segment_row) == segment_row.astype(f32)
    return (lanes_of(square) <= rows_of(square)) & same


def begin_kernel(
    chips,
    experts,
    tokens,
    segments,
    routes,
    cotangent,
    shard_qkv,
    shard_out,
    shard_small,
    w_in,
    w_out,
    attn_in,
    qkv,
    lse,
    mixed,
    residual,
    hidden,
    probs,
    gains,
    kept_full,
    full_in,
    full_out,
    got_g,
    got_h,
    full,
    slots_g,
    slots_h,
    hold_in,
    hold_out,
    own_sem,
    sz,
    rz,
    sx,
    rx,
    sy,
    ry,
    sc,
    rc,
    sw,
    rw,
    lw,
    sd,
    rd,
    se,
    re,
    ld,
):
    block, chip, core, peer_x, peer_y, peer_core, peers_z = place_of(chips)
    owner = lax.axis_index("expert")
    micros, seq_len, model_width = tokens.shape
    rows = shard_qkv.shape[0]
    width = full.shape[1]
    cut = (width // 128 + 1) // 2 * 128
    halves = (pl.ds(0, cut), pl.ds(cut, width - cut))
    every = pl.ds(0, width)
    half = w_in.shape[1] // 2
    row_y, row_x = block // 2, block % 2

    def part(origin, step, columns):
        start = ((flip(block, origin) * chips + flip(chip, step)) * 2 + core) * rows
        return full.at[pl.ds(pl.multiple_of(start, rows), rows), columns]

    own_copies = []
    for i, (src, at) in enumerate(
        ((shard_qkv, 0), (shard_out, 3 * model_width), (shard_small, 4 * model_width))
    ):
        dst = part(0, 0, pl.ds(at, src.shape[1]))
        own_copies.append(pltpu.make_async_copy(src, dst, own_sem.at[i]))
        own_copies[-1].start()
    others = [{"expert": lax.rem(owner + k, experts)} for k in range(1, experts)]
    greet([peer_x, peer_y] + others)
    for copy in own_copies:
        copy.wait()

    mine = part(0, 0, every)
    along_z = [None] + [send(mine, mine, sz.at[k], rz.at[k], peers_z[k]) for k in range(1, chips)]
    along_x = [[None] * 3 for _ in range(chips)]
    along_y = [[None] * 3 for _ in range(chips)]
    across = [[None] * 4 for _ in range(chips)]

    def to_core(k, origin):
        piece = part(origin, k, every)
        across[k][origin] = send(
            piece, piece, sc.at[k, origin], rc.at[k, origin], peer_core
        )

    def pass_on(k):
        along_x[k][1].wait_recv()
        to_core(k, 1)
        along_y[k][1].wait_recv()
        to_core(k, 2)
        along_x[k][2].wait_recv()
        along_y[k][2].wait_recv()
        to_core(k, 3)

    def spread(k):
        for turn in range(2):
            for copies, s, r, peer, side in (
                (along_x, sx, rx, peer_x, turn),
                (along_y, sy, ry, peer_y, 1 - turn),
            ):
                piece = part(0, k, halves[side])
                copies[k][turn] = send(piece, piece, s.at[k, turn], r.at[k, turn], peer)
        to_core(k, 0)

    def turn_corner(k):
        along_x[k][0].wait_recv()
        piece = part(1, k, halves[0])
        along_y[k][2] = send(piece, piece, sy.at[k, 2], ry.at[k, 2], peer_y)
        along_y[k][0].wait_recv()
        piece = part(2, k, halves[1])
        along_x[k][2] = send(piece, piece, sx.at[k, 2], rx.at[k, 2], peer_x)

    spread(0)

    def put_slots(slots, m, values):
        packed = dot_tn(choose_slots(column(routes[m]), experts * slots.shape[2], experts), values)
        packed = packed.astype(bf16)
        for e in range(experts):
            size = slots.shape[2]
            slots[m, e] = packed[e * size : (e + 1) * size]

    for m in range(micros):
        put_slots(slots_g, m, cotangent[m])

    for k in range(chips):
        if k:
            along_z[k].wait_recv()
            spread(k)
            pass_on(k - 1)
        turn_corner(k)

    local_in = pltpu.make_async_copy(w_in.at[:, pl.ds(row_y * half, half)], hold_in, lw.at[0])
    local_out = pltpu.make_async_copy(w_out, hold_out, lw.at[1])
    local_in.start()
    local_out.start()
    from_y = send(
        w_in.at[:, pl.ds((1 - row_y) * half, half)], full_in.at[block], sw.at[0], rw.at[0], peer_y
    )
    from_x = send(
        w_in.at[:, pl.ds(row_y * half, half)], full_in.at[block], sw.at[1], rw.at[1], peer_x
    )
    out_x = send(w_out, full_out.at[row_x], sw.at[3], rw.at[3], peer_x)

    def slot_copies(way, slots, got, m):
        def to_owner(k):
            peer = lax.rem(owner + k, experts)
            return pltpu.make_async_remote_copy(
                src_ref=slots.at[m, peer],
                dst_ref=got.at[m, 0, owner],
                send_sem=sd.at[way, m, k],
                recv_sem=rd.at[way, m, k],
                device_id={"expert": peer},
                device_id_type=MESH,
            )

        def to_y(k):
            origin = lax.rem(owner - k + experts, experts)
            return pltpu.make_async_remote_copy(
                src_ref=got.at[m, 0, origin],
                dst_ref=got.at[m, 1, origin],
                send_sem=se.at[way, m, k],
                recv_sem=re.at[way, m, k],
                device_id=peer_y,
                device_id_type=MESH,
            )

        own = pltpu.make_async_copy(slots.at[m, owner], got.at[m, 0, owner], ld.at[way, m])
        return to_owner, to_y, own

    def start_slots(way, slots, got, m):
        to_owner, to_y, own = slot_copies(way, slots, got, m)
        own.start()

        @pl.loop(1, experts)
        def _(k):
            to_owner(k).start()

    def relay_slots(way, slots, got, m):
        to_owner, to_y, own = slot_copies(way, slots, got, m)
        own.wait()
        to_y(0).start()

        @pl.loop(1, experts)
        def _(k):
            to_owner(k).wait_recv()
            to_y(k).start()

    def end_slots(way, slots, got, m):
        to_owner, to_y, own = slot_copies(way, slots, got, m)

        @pl.loop(1, experts)
        def _(k):
            to_owner(k).wait_send()

        @pl.loop(0, experts)
        def _(k):
            to_y(k).wait()

    for m in range(micros):
        start_slots(0, slots_g, got_g, m)
    pass_on(chips - 1)
    for k in range(chips):
        for origin in range(4):
            across[k][origin].wait_recv()
    keep = pltpu.make_async_copy(full, kept_full, own_sem.at[3])
    keep.start()
    small = jnp.transpose(full[:, pl.ds(4 * model_width, 128)].astype(f32))
    gains[...] = small[experts : experts + 2]
    local_in.wait()
    local_out.wait()
    store_in = pltpu.make_async_copy(hold_in, full_in.at[block], lw.at[0])
    store_out = pltpu.make_async_copy(hold_out, full_out.at[row_x], lw.at[1])
    store_in.start()
    store_out.start()

    scale = 1.0 / math.sqrt(model_width // HEADS)
    low_half = lanes_of((seq_len, 128)) < 64
    diagonal = None
    for m in range(micros):
        x = tokens[m].astype(f32)
        attn_in[m] = (normalize(x)[0] * gains[0:1, :]).astype(bf16)

        @pl.loop(0, 3 * model_width // 512)
        def _(j):
            at = pl.ds(pl.multiple_of(j * 512, 512), 512)
            qkv[m, :, at] = dot(attn_in[m], full[:, at]).astype(bf16)

        allowed = allowed_pairs(segments[m])
        lse[m] = jnp.zeros(lse.shape[1:], f32)

        @pl.loop(0, model_width // 128)
        def _(pair):
            at = pl.multiple_of(pair * 128, 128)
            query = qkv[m, :, pl.ds(at, 128)]
            key = qkv[m, :, pl.ds(model_width + at, 128)]
            value = qkv[m, :, pl.ds(2 * model_width + at, 128)]
            outs = []
            for side in range(2):
                here = low_half if side == 0 else jnp.logical_not(low_half)
                scores = dot_nt(jnp.where(here, query, 0.0).astype(bf16), key) * scale
                masked = jnp.where(allowed, scores, masked_value)
                top = jnp.max(masked, axis=1, keepdims=True)
                weight = jnp.exp(masked - top)
                norm = jnp.sum(weight, axis=1, keepdims=True)
                outs.append(dot((weight / norm).astype(bf16), value))
                head = lanes_of(lse.shape[1:]) == 2 * pair + side
                lse[m] = jnp.where(head, top + jnp.log(norm), lse[m])
            mixed[m, :, pl.ds(at, 128)] = jnp.where(low_half, outs[0], outs[1]).astype(bf16)

        y1 = x + dot(mixed[m], full[:, pl.ds(3 * model_width, model_width)])
        residual[m] = y1
        low = (normalize(y1)[0] * gains[1:2, :]).astype(bf16)
        hidden[m] = low
        put_slots(slots_h, m, low)
        start_slots(1, slots_h, got_h, m)
        logits = dot(low, full[:, pl.ds(4 * model_width, 128)])
        real = lanes_of(logits.shape) < experts
        logits = jnp.where(real, logits, masked_value)
        weight = jnp.where(real, jnp.exp(logits - jnp.max(logits, axis=1, keepdims=True)), 0.0)
        probs[m] = weight / jnp.sum(weight, axis=1, keepdims=True)
        if m == 0:
            from_y.wait_recv()
            piece = full_in.at[flip(block, 2)]
            diagonal = send(piece, piece, sw.at[2], rw.at[2], peer_x)
        relay_slots(0, slots_g, got_g, m)
        if m:
            relay_slots(1, slots_h, got_h, m - 1)
    relay_slots(1, slots_h, got_h, micros - 1)

    for m in range(micros):
        end_slots(0, slots_g, got_g, m)
        end_slots(1, slots_h, got_h, m)
    keep.wait()
    store_in.wait()
    store_out.wait()
    from_y.wait_send()
    for copy in (from_x, out_x, diagonal):
        copy.wait()
    for k in range(chips):
        if k:
            along_z[k].wait_send()
        for turn in range(3):
            along_x[k][turn].wait_send()
            along_y[k][turn].wait_send()
        for origin in range(4):
            across[k][origin].wait_send()


def begin_layer(tokens, segments, routes, cotangent, shards, w_in, w_out, chips):
    experts = 2 * chips
    micros, seq_len, model_width = tokens.shape
    capacity = (9 * seq_len + 8 * experts - 1) // (8 * experts)
    padded = (capacity + 7) // 8 * 8
    width = 4 * model_width + 128
    rows, half = w_in.shape[0], w_in.shape[1] // 2
    shape = jax.ShapeDtypeStruct
    vmem, hbm = pl.BlockSpec(memory_space=pltpu.VMEM), pl.BlockSpec(memory_space=pl.ANY)
    spots = (micros, experts, padded, model_width)
    return pl.pallas_call(
        functools.partial(begin_kernel, chips, experts),
        out_shape=[
            shape((micros, seq_len, model_width), bf16),
            shape((micros, seq_len, 3 * model_width), bf16),
            shape((micros, seq_len, 128), f32),
            shape((micros, seq_len, model_width), bf16),
            shape((micros, seq_len, model_width), f32),
            shape((micros, seq_len, model_width), bf16),
            shape((micros, seq_len, 128), f32),
            shape((2, model_width), f32),
            shape((model_width, width), bf16),
            shape((4, rows, half), bf16),
            shape((2,) + w_out.shape, bf16),
            shape((micros, 2, experts, padded, model_width), bf16),
            shape((micros, 2, experts, padded, model_width), bf16),
        ],
        in_specs=[vmem] * 4 + [hbm] * 5,
        out_specs=[vmem] * 8 + [hbm] * 5,
        scratch_shapes=[
            pltpu.VMEM((model_width, width), bf16),
            pltpu.VMEM(spots, bf16),
            pltpu.VMEM(spots, bf16),
            pltpu.VMEM((rows, half), bf16),
            pltpu.VMEM(w_out.shape, bf16),
            DMA((4,)),
            DMA((chips,)),
            DMA((chips,)),
            DMA((chips, 3)),
            DMA((chips, 3)),
            DMA((chips, 3)),
            DMA((chips, 3)),
            DMA((chips, 4)),
            DMA((chips, 4)),
            DMA((4,)),
            DMA((4,)),
            DMA((2,)),
            DMA((2, micros, experts)),
            DMA((2, micros, experts)),
            DMA((2, micros, experts)),
            DMA((2, micros, experts)),
            DMA((2, micros)),
        ],
        compiler_params=pltpu.CompilerParams(
            collective_id=1, has_side_effects=True, vmem_limit_bytes=60 * 2**20
        ),
        name="begin_layer",
    )(tokens, segments, routes, cotangent, *shards, w_in, w_out)


def backward_kernel(
    experts,
    x_ref,
    g_ref,
    segment_ref,
    route_ref,
    full_ref,
    gains_ref,
    qkv_ref,
    lse_ref,
    y1_ref,
    prob_ref,
    returned_ref,
    back_ref,
    out_ref,
    grad_x_ref,
    branch_ref,
    gqkv_ref,
    glog_ref,
    gain_ref,
    go_ref,
    gy1_ref,
):
    seq_len, model_width = x_ref.shape
    scale = 1.0 / math.sqrt(model_width // HEADS)
    g = g_ref[...].astype(f32)
    route = column(route_ref[...])
    chosen = choose_slots(route, returned_ref.shape[0], experts)
    moe = dot(chosen, returned_ref[...])
    prob = prob_ref[...]
    one_hot = one_hot_of(route)
    gate = jnp.sum(prob * one_hot, axis=1, keepdims=True)
    y1 = y1_ref[...]
    out_ref[...] = (y1 + gate * moe).astype(bf16)
    choice = one_hot * jnp.sum(g * moe, axis=1, keepdims=True)
    glog = (prob * (choice - jnp.sum(prob * choice, axis=1, keepdims=True))).astype(bf16)
    glog_ref[...] = glog
    grad_h = dot(chosen, back_ref[...]) + dot_nt(glog, full_ref[:, pl.ds(4 * model_width, 128)])
    n2, inv2 = normalize(y1)
    gain_ref[1:2, :] = jnp.sum(grad_h * n2, axis=0, keepdims=True)
    gy1 = g + norm_back(grad_h * gains_ref[1:2, :], n2, inv2)
    gy1_ref[...] = gy1
    branch_ref[...] = gy1.astype(bf16)
    go_ref[...] = dot_nt(branch_ref[...], full_ref[:, pl.ds(3 * model_width, model_width)]).astype(bf16)

    allowed = allowed_pairs(segment_ref[...])
    low_half = lanes_of((seq_len, 128)) < 64

    @pl.loop(0, model_width // 128)
    def _(pair):
        at = pl.multiple_of(pair * 128, 128)
        query = qkv_ref[:, pl.ds(at, 128)]
        key = qkv_ref[:, pl.ds(model_width + at, 128)]
        value = qkv_ref[:, pl.ds(2 * model_width + at, 128)]
        grad_o = go_ref[:, pl.ds(at, 128)]
        parts = []
        for side in range(2):
            mine = low_half if side == 0 else jnp.logical_not(low_half)
            scores = dot_nt(jnp.where(mine, query, 0.0).astype(bf16), key) * scale
            head = lanes_of(lse_ref.shape) == 2 * pair + side
            lse = jnp.sum(jnp.where(head, lse_ref[...], 0.0), axis=1, keepdims=True)
            p = jnp.exp(jnp.where(allowed, scores, masked_value) - lse)
            gp = dot_nt(jnp.where(mine, grad_o, 0.0).astype(bf16), value)
            gs = (p * (gp - jnp.sum(p * gp, axis=1, keepdims=True))).astype(bf16)
            parts.append((dot(gs, key) * scale, dot_tn(gs, query) * scale, dot_tn(p.astype(bf16), grad_o)))
        for i in range(3):
            both = jnp.where(low_half, parts[0][i], parts[1][i]).astype(bf16)
            gqkv_ref[:, pl.ds(i * model_width + at, 128)] = both

    ga = dot_nt(gqkv_ref[...], full_ref[:, pl.ds(0, 3 * model_width)])
    n1, inv1 = normalize(x_ref[...].astype(f32))
    gain_ref[0:1, :] = jnp.sum(ga * n1, axis=0, keepdims=True)
    grad_x_ref[...] = gy1_ref[...] + norm_back(ga * gains_ref[0:1, :], n1, inv1)


def kernel_params(flops):
    return dict(
        compiler_params=pltpu.CompilerParams(vmem_limit_bytes=56 * 2**20),
        cost_estimate=pl.CostEstimate(flops=flops, bytes_accessed=2**20, transcendentals=0),
    )


def attention_backward(experts, *operands):
    seq_len, model_width = operands[0].shape
    shape = jax.ShapeDtypeStruct
    return pl.pallas_call(
        functools.partial(backward_kernel, experts),
        out_shape=[
            shape((seq_len, model_width), bf16),
            shape((seq_len, model_width), f32),
            shape((seq_len, model_width), bf16),
            shape((seq_len, 3 * model_width), bf16),
            shape((seq_len, 128), bf16),
            shape((2, model_width), f32),
        ],
        scratch_shapes=[
            pltpu.VMEM((seq_len, model_width), bf16),
            pltpu.VMEM((seq_len, model_width), f32),
        ],
        name="attention_backward",
        **kernel_params(30 * 10**9),
    )(*operands)


def reduce_expert_grads(grad_in, grad_out, block):
    rows = grad_in.shape[0] // 4
    half = grad_in.shape[1]
    row_y, row_x = block // 2, block % 2
    parts_out = grad_out.reshape(2, -1, grad_out.shape[1])
    keep_out = lax.dynamic_slice_in_dim(parts_out, row_x, 1, 0)[0]
    send_out = lax.dynamic_slice_in_dim(parts_out, 1 - row_x, 1, 0)[0].astype(bf16)
    parts_in = grad_in.reshape(2, 2, rows, half)
    keep_in = lax.dynamic_slice_in_dim(parts_in, row_x, 1, 1)[:, 0]
    send_in = lax.dynamic_slice_in_dim(parts_in, 1 - row_x, 1, 1)[:, 0].astype(bf16)
    sums = keep_in + swap_x(send_in).astype(f32)
    done_out = keep_out + swap_x(send_out).astype(f32)
    own = lax.dynamic_slice_in_dim(sums, row_y, 1, 0)[0]
    other = lax.dynamic_slice_in_dim(sums, 1 - row_y, 1, 0)[0].astype(bf16)
    return own, other, done_out


def join_expert_grads(own, other, block):
    rows, half = own.shape
    row_y = block // 2
    got = swap_y(other).astype(f32)
    done_in = jnp.zeros((rows, 2 * half), f32)
    done_in = lax.dynamic_update_slice(done_in, own, (0, row_y * half))
    done_in = lax.dynamic_update_slice(done_in, got, (0, (1 - row_y) * half))
    return done_in


def on_device(
    tokens,
    segment_ids,
    routes,
    cotangent,
    w_qkv,
    w_attn_out,
    w_router,
    gain_attn,
    gain_moe,
    w_expert_in,
    w_expert_out,
):
    micro_count, _, seq_len, model_width = tokens.shape
    experts = w_router.shape[1]
    block = lax.axis_index("dp")
    expert = lax.axis_index("expert")
    chips = model_width // w_qkv.shape[0] // 8
    micros = range(micro_count)

    spare = jnp.zeros((w_qkv.shape[0], 128 - 2 - experts), bf16)
    small = jnp.concatenate([w_router, gain_attn[:, None], gain_moe[:, None], spare], axis=1)
    tokens, cotangent, segment_ids = tokens[:, 0], cotangent[:, 0], segment_ids
    routes = routes.reshape(micro_count, 1, seq_len)
    begun = begin_layer(
        tokens,
        segment_ids,
        routes,
        cotangent,
        (w_qkv, w_attn_out, small),
        w_expert_in[0],
        w_expert_out[0],
        chips,
    )
    gains, gathered, w_in, w_out, got_g, got_h = begun[7:]
    w_in = w_in.reshape(model_width, -1)
    w_out = w_out.reshape(-1, model_width)
    padded = got_g.shape[3]
    router = gathered[:, 4 * model_width :][:, :experts]
    names = names_all = ("attn_in", "qkv", "lse", "mixed", "residual", "hidden", "prob")
    state = [dict(zip(names, (value[m] for value in begun[:7]))) for m in micros]
    grad_slots = [got_g[m].reshape(-1, model_width) for m in micros]
    for m in micros:
        state[m]["received"] = got_h[m].reshape(-1, model_width)

    def give_back(partial):
        rows = partial.shape[0] // 2
        total = partial[:rows] + swap_y(partial[rows:].astype(bf16)).astype(f32)
        total = total.astype(bf16).reshape(experts, padded, model_width)
        return to_experts(total).reshape(-1, model_width)

    for m in micros:
        s = state[m]
        own_prob = jax.nn.softmax(dot(s["received"], router), axis=-1)
        picked = (lax.iota(jnp.int32, experts) == expert).astype(f32)[None]
        own_gate = jnp.sum(own_prob * picked, axis=1, keepdims=True)
        s["gz"] = (own_gate * grad_slots[m].astype(f32)).astype(bf16)
        pre_act = dot(s["received"], w_in)
        s["act"] = jax.nn.gelu(pre_act).astype(bf16)
        s["returned"] = give_back(dot(s["act"], w_out))
        slope = jax.vjp(jax.nn.gelu, pre_act)[1]
        s["gu"] = slope(dot_nt(s["gz"], w_out))[0].astype(bf16)
        s["grad_back"] = give_back(dot_nt(s["gu"], w_in))
    def both(name):
        if name in names_all:
            return begun[names_all.index(name)].reshape(-1, begun[names_all.index(name)].shape[2])
        return jnp.concatenate([s[name] for s in state], axis=0)

    grad_w_out = dot_tn(both("act"), both("gz"))
    grad_w_in = dot_tn(both("received"), both("gu"))
    own, other, grad_out = reduce_expert_grads(grad_w_in, grad_w_out, block)

    for m in micros:
        s = state[m]
        names = ("output", "grad_tokens", "branch", "grad_qkv", "grad_logit", "gain")
        s.update(
            zip(
                names,
                attention_backward(
                    experts,
                    tokens[m],
                    cotangent[m],
                    segment_ids[m],
                    routes[m],
                    gathered,
                    gains,
                    s["qkv"],
                    s["lse"],
                    s["residual"],
                    s["prob"],
                    s["returned"],
                    s["grad_back"],
                ),
            )
        )
    term_router = dot_tn(both("hidden"), both("grad_logit"))[:, :experts]
    term_out = dot_tn(both("mixed"), both("branch")).astype(bf16)
    term_qkv = dot_tn(both("attn_in"), both("grad_qkv")).astype(bf16)
    gain_sum = sum(s["gain"] for s in state).T
    spare = jnp.zeros((model_width, 128 - 2 - experts), f32)
    term_small = jnp.concatenate([term_router, gain_sum, spare], axis=1).astype(bf16)
    term_small, other = lax.optimization_barrier((term_small, other))
    grad_in = join_expert_grads(own, other, block)
    grad_qkv, grad_attn_out, small_sum = reduce_rows((term_qkv, term_out, term_small), chips)
    return (
        jnp.stack([s["output"] for s in state])[:, None],
        jnp.stack([s["grad_tokens"] for s in state])[:, None],
        grad_qkv,
        grad_attn_out,
        small_sum[:, :experts],
        small_sum[:, experts],
        small_sum[:, experts + 1],
        grad_in[None],
        grad_out[None],
    )


def solution(mesh):
    rows = P(("dp", "expert"))
    seqs = P(None, ("dp", "expert"))
    owned = P("expert", "dp", None)
    return jax.shard_map(
        on_device,
        mesh=mesh,
        in_specs=(seqs, seqs, seqs, seqs, rows, rows, rows, rows, rows, owned, owned),
        out_specs=(seqs, seqs, rows, rows, rows, rows, rows, owned, owned),
        check_vma=False,
    )
```

```python
import functools
import math

import jax
import jax.numpy as jnp
from jax import lax
from jax.experimental import pallas as pl
from jax.experimental.pallas import tpu as pltpu
from jax.sharding import PartitionSpec as P

HEADS = 16
epsilon = 1e-05
masked_value = -1e30
f32 = jnp.float32
bf16 = jnp.bfloat16

MESH = pl.DeviceIdType.MESH
DMA = pltpu.SemaphoreType.DMA


def flip(index, mask):
    bit = 1
    while bit <= mask:
        if mask & bit:
            index = index + bit - 2 * bit * ((index // bit) % 2)
        bit *= 2
    return index


def place_of(chips):
    block = lax.axis_index("dp")
    owner = lax.axis_index("expert")
    peer_x = {"dp": flip(block, 1)}
    peer_y = {"dp": flip(block, 2)}
    peer_core = {"expert": flip(owner, 1)}
    peers_z = [{"expert": flip(owner, 2 * k)} for k in range(chips)]
    return block, owner // 2, owner % 2, peer_x, peer_y, peer_core, peers_z


def greet(peers):
    barrier = pltpu.get_barrier_semaphore()
    for peer in peers:
        pl.semaphore_signal(barrier, inc=1, device_id=peer, device_id_type=MESH)
    pl.semaphore_wait(barrier, len(peers))


def send(src, dst, send_sem, recv_sem, peer):
    copy = pltpu.make_async_remote_copy(
        src_ref=src, dst_ref=dst, send_sem=send_sem, recv_sem=recv_sem,
        device_id=peer, device_id_type=MESH,
    )
    copy.start()
    return copy


def reduce_kernel(chips, cut, widths, *refs):
    n = len(widths)
    grads, outs = refs[:n], refs[n : 2 * n]
    total, crecv, xrecv, yrecv, zrecv, part_z = refs[2 * n : 2 * n + 6]
    la, sc, rc, sx, rx, sy, ry, sz, rz = refs[2 * n + 6 :]
    block, chip, core, peer_x, peer_y, peer_core, peers_z = place_of(chips)
    rows, width = zrecv.shape[1:]
    wide = width - cut
    left, right = pl.ds(0, cut), pl.ds(cut, wide)
    columns = []
    for w in widths:
        columns.append(pl.ds(sum(widths[: len(columns)]), w))
    order = list(range(chips - 1, -1, -1))
    opposite = flip(core, 1)
    greet([peer_x, peer_y, peer_core] + peers_z[1:])
    across, local = {}, {}
    for k in order:
        step = flip(chip, k)
        across[k], local[k] = [], []
        for i in range(n):
            across[k].append(
                send(
                    grads[i].at[:, step, opposite],
                    crecv.at[:, step, :, columns[i]],
                    sc.at[k, i], rc.at[k, i], peer_core,
                )
            )
            copy = pltpu.make_async_copy(
                grads[i].at[:, step, core], total.at[:, step, :, columns[i]], la.at[k, i]
            )
            copy.start()
            local[k].append(copy)

    def spot(k, origin, cols):
        return (flip(block, origin), flip(chip, k), slice(None), cols)

    along_x, along_y, along_z = {}, {}, {}

    def begin(k):
        for i in range(n):
            local[k][i].wait()
            across[k][i].wait_recv()
        step = flip(chip, k)
        for origin in (3, 1, 2, 0):
            at = (flip(block, origin), step)
            total[at] = (total[at].astype(f32) + crecv[at].astype(f32)).astype(bf16)
            if origin == 3:
                along_x[k, 0] = send(
                    total.at[spot(k, 3, left)], xrecv.at[k, 0, :, left], sx.at[k, 0], rx.at[k, 0], peer_x
                )
                along_y[k, 0] = send(
                    total.at[spot(k, 3, right)], yrecv.at[k, 0, :, pl.ds(0, wide)], sy.at[k, 0], ry.at[k, 0], peer_y
                )
            if origin == 1:
                along_x[k, 1] = send(
                    total.at[spot(k, 1, left)], xrecv.at[k, 1, :, left], sx.at[k, 1], rx.at[k, 1], peer_x
                )
            if origin == 2:
                along_y[k, 1] = send(
                    total.at[spot(k, 2, right)], yrecv.at[k, 1, :, pl.ds(0, wide)], sy.at[k, 1], ry.at[k, 1], peer_y
                )

    def relay(k):
        along_x[k, 0].wait_recv()
        at = spot(k, 2, left)
        total[at] = (total[at].astype(f32) + xrecv[k, 0, :, left].astype(f32)).astype(bf16)
        along_y[k, 2] = send(total.at[at], yrecv.at[k, 2, :, left], sy.at[k, 2], ry.at[k, 2], peer_y)
        along_y[k, 0].wait_recv()
        at = spot(k, 1, right)
        total[at] = (total[at].astype(f32) + yrecv[k, 0, :, pl.ds(0, wide)].astype(f32)).astype(bf16)
        along_x[k, 2] = send(
            total.at[at], xrecv.at[k, 2, :, pl.ds(0, wide)], sx.at[k, 2], rx.at[k, 2], peer_x
        )

    def finish(k):
        for turn in (1, 2):
            along_x[k, turn].wait_recv()
            along_y[k, turn].wait_recv()
        lhs = (
            total[spot(k, 0, left)].astype(f32)
            + xrecv[k, 1, :, left].astype(f32)
            + yrecv[k, 2, :, left].astype(f32)
        )
        rhs = (
            total[spot(k, 0, right)].astype(f32)
            + yrecv[k, 1, :, pl.ds(0, wide)].astype(f32)
            + xrecv[k, 2, :, pl.ds(0, wide)].astype(f32)
        )
        if k:
            part_z[k, :, left] = lhs.astype(bf16)
            part_z[k, :, right] = rhs.astype(bf16)
            along_z[k] = send(part_z.at[k], zrecv.at[k], sz.at[k], rz.at[k], peers_z[k])
        else:
            for j in range(1, chips):
                along_z[j].wait_recv()
                lhs = lhs + zrecv[j, :, left].astype(f32)
                rhs = rhs + zrecv[j, :, right].astype(f32)
            start = 0
            for i, w in enumerate(widths):
                for lo, hi, value in ((0, cut, lhs), (cut, width, rhs)):
                    a, b = max(start, lo), min(start + w, hi)
                    if a < b:
                        outs[i][:, a - start : b - start] = value[:, a - lo : b - lo]
                start += w

    for i in range(chips + 2):
        if i < chips:
            begin(order[i])
        if 0 <= i - 1 < chips:
            relay(order[i - 1])
        if i - 2 >= 0:
            finish(order[i - 2])
    for k in order:
        for i in range(n):
            across[k][i].wait_send()
        for turn in range(3):
            along_x[k, turn].wait_send()
            along_y[k, turn].wait_send()
        if k:
            along_z[k].wait_send()


def reduce_rows(grads, chips):
    rows = grads[0].shape[0] // (8 * chips)
    widths = tuple(g.shape[1] for g in grads)
    width = sum(widths)
    cut = (width // 128 + 1) // 2 * 128
    n = len(grads)
    return pl.pallas_call(
        functools.partial(reduce_kernel, chips, cut, widths),
        out_shape=[jax.ShapeDtypeStruct((rows, w), f32) for w in widths],
        in_specs=[pl.BlockSpec(memory_space=pl.ANY)] * n,
        out_specs=[pl.BlockSpec(memory_space=pltpu.VMEM)] * n,
        scratch_shapes=[
            pltpu.VMEM((4, chips, rows, width), bf16),
            pltpu.VMEM((4, chips, rows, width), bf16),
            pltpu.VMEM((chips, 3, rows, cut), bf16),
            pltpu.VMEM((chips, 3, rows, cut), bf16),
            pltpu.VMEM((chips, rows, width), bf16),
            pltpu.VMEM((chips, rows, width), bf16),
            DMA((chips, n)),
            DMA((chips, n)),
            DMA((chips, n)),
            DMA((chips, 3)),
            DMA((chips, 3)),
            DMA((chips, 3)),
            DMA((chips, 3)),
            DMA((chips,)),
            DMA((chips,)),
        ],
        compiler_params=pltpu.CompilerParams(collective_id=2, has_side_effects=True),
        name="reduce_rows",
    )(*[g.reshape(4, chips, 2, rows, g.shape[1]) for g in grads])


PAIR_X = tuple((b, b ^ 1) for b in range(4))
PAIR_Y = tuple((b, b ^ 2) for b in range(4))


def swap_x(a):
    return lax.ppermute(a, "dp", PAIR_X)


def swap_y(a):
    return lax.ppermute(a, "dp", PAIR_Y)


def normalize(values):
    row_mean = jnp.mean(values, axis=-1, keepdims=True)
    centered = values - row_mean
    inv_scale = lax.rsqrt(jnp.mean(centered * centered, axis=-1, keepdims=True) + epsilon)
    return (centered * inv_scale, inv_scale)


def norm_back(grad_normed, normed, inv_scale):
    return inv_scale * (
        grad_normed
        - jnp.mean(grad_normed, axis=-1, keepdims=True)
        - normed * jnp.mean(grad_normed * normed, axis=-1, keepdims=True)
    )


def dot(a, b):
    return jnp.dot(a, b, preferred_element_type=f32)


def dot_nt(a, b):
    return lax.dot_general(a, b, (((1,), (1,)), ((), ())), preferred_element_type=f32)


def dot_tn(a, b):
    return lax.dot_general(a, b, (((0,), (0,)), ((), ())), preferred_element_type=f32)


def lanes_of(shape):
    return lax.broadcasted_iota(jnp.int32, shape, 1)


def rows_of(shape):
    return lax.broadcasted_iota(jnp.int32, shape, 0)


def column(row):
    return jnp.transpose(jnp.broadcast_to(row.astype(f32), (128, row.shape[1])))[:, :1]


def one_hot_of(route):
    return jnp.where(lanes_of((route.shape[0], 128)).astype(f32) == route, 1.0, 0.0)


def choose_slots(route, spots, experts):
    seq_len = route.shape[0]
    capacity = (9 * seq_len + 8 * experts - 1) // (8 * experts)
    one_hot = one_hot_of(route)
    square = (seq_len, seq_len)
    before = jnp.where(lanes_of(square) < rows_of(square), 1.0, 0.0).astype(bf16)
    place = jnp.sum(dot(before, one_hot.astype(bf16)) * one_hot, axis=1, keepdims=True)
    slot = jnp.where(place < capacity, route * (spots // experts) + place, -1.0)
    return jnp.where(lanes_of((seq_len, spots)).astype(f32) == slot, 1.0, 0.0).astype(bf16)


def allowed_pairs(segment_row):
    square = (segment_row.shape[1],) * 2
    same = column(segment_row) == segment_row.astype(f32)
    return (lanes_of(square) <= rows_of(square)) & same


def begin_kernel(
    chips,
    experts,
    tokens,
    segments,
    routes,
    cotangent,
    shard_qkv,
    shard_out,
    shard_small,
    w_in,
    w_out,
    attn_in,
    qkv,
    lse,
    mixed,
    residual,
    hidden,
    probs,
    gains,
    kept_full,
    full_in,
    full_out,
    got_g,
    got_h,
    full,
    slots_g,
    slots_h,
    hold_in,
    hold_out,
    own_sem,
    sz,
    rz,
    sx,
    rx,
    sy,
    ry,
    sc,
    rc,
    sw,
    rw,
    lw,
    sd,
    rd,
    se,
    re,
    ld,
):
    block, chip, core, peer_x, peer_y, peer_core, peers_z = place_of(chips)
    owner = lax.axis_index("expert")
    micros, seq_len, model_width = tokens.shape
    rows = shard_qkv.shape[0]
    width = full.shape[1]
    cut = (width // 128 + 1) // 2 * 128
    halves = (pl.ds(0, cut), pl.ds(cut, width - cut))
    every = pl.ds(0, width)
    half = w_in.shape[1] // 2
    row_y, row_x = block // 2, block % 2

    def part(origin, step, columns):
        start = ((flip(block, origin) * chips + flip(chip, step)) * 2 + core) * rows
        return full.at[pl.ds(pl.multiple_of(start, rows), rows), columns]

    own_copies = []
    for i, (src, at) in enumerate(
        ((shard_qkv, 0), (shard_out, 3 * model_width), (shard_small, 4 * model_width))
    ):
        dst = part(0, 0, pl.ds(at, src.shape[1]))
        own_copies.append(pltpu.make_async_copy(src, dst, own_sem.at[i]))
        own_copies[-1].start()
    others = [{"expert": lax.rem(owner + k, experts)} for k in range(1, experts)]
    greet([peer_x, peer_y] + others)
    for copy in own_copies:
        copy.wait()

    mine = part(0, 0, every)
    along_z = [None] + [send(mine, mine, sz.at[k], rz.at[k], peers_z[k]) for k in range(1, chips)]
    along_x = [[None] * 3 for _ in range(chips)]
    along_y = [[None] * 3 for _ in range(chips)]
    across = [[None] * 4 for _ in range(chips)]

    def to_core(k, origin):
        piece = part(origin, k, every)
        across[k][origin] = send(
            piece, piece, sc.at[k, origin], rc.at[k, origin], peer_core
        )

    def pass_on(k):
        along_x[k][1].wait_recv()
        to_core(k, 1)
        along_y[k][1].wait_recv()
        to_core(k, 2)
        along_x[k][2].wait_recv()
        along_y[k][2].wait_recv()
        to_core(k, 3)

    def spread(k):
        for turn in range(2):
            for copies, s, r, peer, side in (
                (along_x, sx, rx, peer_x, turn),
                (along_y, sy, ry, peer_y, 1 - turn),
            ):
                piece = part(0, k, halves[side])
                copies[k][turn] = send(piece, piece, s.at[k, turn], r.at[k, turn], peer)
        to_core(k, 0)

    def turn_corner(k):
        along_x[k][0].wait_recv()
        piece = part(1, k, halves[0])
        along_y[k][2] = send(piece, piece, sy.at[k, 2], ry.at[k, 2], peer_y)
        along_y[k][0].wait_recv()
        piece = part(2, k, halves[1])
        along_x[k][2] = send(piece, piece, sx.at[k, 2], rx.at[k, 2], peer_x)

    spread(0)

    def put_slots(slots, m, values):
        packed = dot_tn(choose_slots(column(routes[m]), experts * slots.shape[2], experts), values)
        packed = packed.astype(bf16)
        for e in range(experts):
            size = slots.shape[2]
            slots[m, e] = packed[e * size : (e + 1) * size]

    for m in range(micros):
        put_slots(slots_g, m, cotangent[m])

    for k in range(chips):
        if k:
            along_z[k].wait_recv()
            spread(k)
            pass_on(k - 1)
        turn_corner(k)

    local_in = pltpu.make_async_copy(w_in.at[:, pl.ds(row_y * half, half)], hold_in, lw.at[0])
    local_out = pltpu.make_async_copy(w_out, hold_out, lw.at[1])
    local_in.start()
    local_out.start()
    from_y = send(
        w_in.at[:, pl.ds((1 - row_y) * half, half)], full_in.at[block], sw.at[0], rw.at[0], peer_y
    )
    from_x = send(
        w_in.at[:, pl.ds(row_y * half, half)], full_in.at[block], sw.at[1], rw.at[1], peer_x
    )
    out_x = send(w_out, full_out.at[row_x], sw.at[3], rw.at[3], peer_x)

    def slot_copies(way, slots, got, m):
        def to_owner(k):
            peer = lax.rem(owner + k, experts)
            return pltpu.make_async_remote_copy(
                src_ref=slots.at[m, peer],
                dst_ref=got.at[m, 0, owner],
                send_sem=sd.at[way, m, k],
                recv_sem=rd.at[way, m, k],
                device_id={"expert": peer},
                device_id_type=MESH,
            )

        def to_y(k):
            origin = lax.rem(owner - k + experts, experts)
            return pltpu.make_async_remote_copy(
                src_ref=got.at[m, 0, origin],
                dst_ref=got.at[m, 1, origin],
                send_sem=se.at[way, m, k],
                recv_sem=re.at[way, m, k],
                device_id=peer_y,
                device_id_type=MESH,
            )

        own = pltpu.make_async_copy(slots.at[m, owner], got.at[m, 0, owner], ld.at[way, m])
        return to_owner, to_y, own

    def start_slots(way, slots, got, m):
        to_owner, to_y, own = slot_copies(way, slots, got, m)
        own.start()

        @pl.loop(1, experts)
        def _(k):
            to_owner(k).start()

    def relay_slots(way, slots, got, m):
        to_owner, to_y, own = slot_copies(way, slots, got, m)
        own.wait()
        to_y(0).start()

        @pl.loop(1, experts)
        def _(k):
            to_owner(k).wait_recv()
            to_y(k).start()

    def end_slots(way, slots, got, m):
        to_owner, to_y, own = slot_copies(way, slots, got, m)

        @pl.loop(1, experts)
        def _(k):
            to_owner(k).wait_send()

        @pl.loop(0, experts)
        def _(k):
            to_y(k).wait()

    for m in range(micros):
        start_slots(0, slots_g, got_g, m)
    pass_on(chips - 1)
    for k in range(chips):
        for origin in range(4):
            across[k][origin].wait_recv()
    keep = pltpu.make_async_copy(full, kept_full, own_sem.at[3])
    keep.start()
    small = jnp.transpose(full[:, pl.ds(4 * model_width, 128)].astype(f32))
    gains[...] = small[experts : experts + 2]
    local_in.wait()
    local_out.wait()
    store_in = pltpu.make_async_copy(hold_in, full_in.at[block], lw.at[0])
    store_out = pltpu.make_async_copy(hold_out, full_out.at[row_x], lw.at[1])
    store_in.start()
    store_out.start()

    scale = 1.0 / math.sqrt(model_width // HEADS)
    low_half = lanes_of((seq_len, 128)) < 64
    diagonal = None
    for m in range(micros):
        x = tokens[m].astype(f32)
        attn_in[m] = (normalize(x)[0] * gains[0:1, :]).astype(bf16)

        @pl.loop(0, 3 * model_width // 512)
        def _(j):
            at = pl.ds(pl.multiple_of(j * 512, 512), 512)
            qkv[m, :, at] = dot(attn_in[m], full[:, at]).astype(bf16)

        allowed = allowed_pairs(segments[m])
        lse[m] = jnp.zeros(lse.shape[1:], f32)

        @pl.loop(0, model_width // 128)
        def _(pair):
            at = pl.multiple_of(pair * 128, 128)
            query = qkv[m, :, pl.ds(at, 128)]
            key = qkv[m, :, pl.ds(model_width + at, 128)]
            value = qkv[m, :, pl.ds(2 * model_width + at, 128)]
            outs = []
            for side in range(2):
                here = low_half if side == 0 else jnp.logical_not(low_half)
                scores = dot_nt(jnp.where(here, query, 0.0).astype(bf16), key) * scale
                masked = jnp.where(allowed, scores, masked_value)
                top = jnp.max(masked, axis=1, keepdims=True)
                weight = jnp.exp(masked - top)
                norm = jnp.sum(weight, axis=1, keepdims=True)
                outs.append(dot((weight / norm).astype(bf16), value))
                head = lanes_of(lse.shape[1:]) == 2 * pair + side
                lse[m] = jnp.where(head, top + jnp.log(norm), lse[m])
            mixed[m, :, pl.ds(at, 128)] = jnp.where(low_half, outs[0], outs[1]).astype(bf16)

        y1 = x + dot(mixed[m], full[:, pl.ds(3 * model_width, model_width)])
        residual[m] = y1
        low = (normalize(y1)[0] * gains[1:2, :]).astype(bf16)
        hidden[m] = low
        put_slots(slots_h, m, low)
        start_slots(1, slots_h, got_h, m)
        logits = dot(low, full[:, pl.ds(4 * model_width, 128)])
        real = lanes_of(logits.shape) < experts
        logits = jnp.where(real, logits, masked_value)
        weight = jnp.where(real, jnp.exp(logits - jnp.max(logits, axis=1, keepdims=True)), 0.0)
        probs[m] = weight / jnp.sum(weight, axis=1, keepdims=True)
        if m == 0:
            from_y.wait_recv()
            piece = full_in.at[flip(block, 2)]
            diagonal = send(piece, piece, sw.at[2], rw.at[2], peer_x)
        relay_slots(0, slots_g, got_g, m)
        if m:
            relay_slots(1, slots_h, got_h, m - 1)
    relay_slots(1, slots_h, got_h, micros - 1)

    for m in range(micros):
        end_slots(0, slots_g, got_g, m)
        end_slots(1, slots_h, got_h, m)
    keep.wait()
    store_in.wait()
    store_out.wait()
    from_y.wait_send()
    for copy in (from_x, out_x, diagonal):
        copy.wait()
    for k in range(chips):
        if k:
            along_z[k].wait_send()
        for turn in range(3):
            along_x[k][turn].wait_send()
            along_y[k][turn].wait_send()
        for origin in range(4):
            across[k][origin].wait_send()


def begin_layer(tokens, segments, routes, cotangent, shards, w_in, w_out, chips):
    experts = 2 * chips
    micros, seq_len, model_width = tokens.shape
    capacity = (9 * seq_len + 8 * experts - 1) // (8 * experts)
    padded = (capacity + 7) // 8 * 8
    width = 4 * model_width + 128
    rows, half = w_in.shape[0], w_in.shape[1] // 2
    shape = jax.ShapeDtypeStruct
    vmem, hbm = pl.BlockSpec(memory_space=pltpu.VMEM), pl.BlockSpec(memory_space=pl.ANY)
    spots = (micros, experts, padded, model_width)
    return pl.pallas_call(
        functools.partial(begin_kernel, chips, experts),
        out_shape=[
            shape((micros, seq_len, model_width), bf16),
            shape((micros, seq_len, 3 * model_width), bf16),
            shape((micros, seq_len, 128), f32),
            shape((micros, seq_len, model_width), bf16),
            shape((micros, seq_len, model_width), f32),
            shape((micros, seq_len, model_width), bf16),
            shape((micros, seq_len, 128), f32),
            shape((2, model_width), f32),
            shape((model_width, width), bf16),
            shape((4, rows, half), bf16),
            shape((2,) + w_out.shape, bf16),
            shape((micros, 2, experts, padded, model_width), bf16),
            shape((micros, 2, experts, padded, model_width), bf16),
        ],
        in_specs=[vmem] * 4 + [hbm] * 5,
        out_specs=[vmem] * 8 + [hbm] * 5,
        scratch_shapes=[
            pltpu.VMEM((model_width, width), bf16),
            pltpu.VMEM(spots, bf16),
            pltpu.VMEM(spots, bf16),
            pltpu.VMEM((rows, half), bf16),
            pltpu.VMEM(w_out.shape, bf16),
            DMA((4,)),
            DMA((chips,)),
            DMA((chips,)),
            DMA((chips, 3)),
            DMA((chips, 3)),
            DMA((chips, 3)),
            DMA((chips, 3)),
            DMA((chips, 4)),
            DMA((chips, 4)),
            DMA((4,)),
            DMA((4,)),
            DMA((2,)),
            DMA((2, micros, experts)),
            DMA((2, micros, experts)),
            DMA((2, micros, experts)),
            DMA((2, micros, experts)),
            DMA((2, micros)),
        ],
        compiler_params=pltpu.CompilerParams(
            collective_id=1, has_side_effects=True, vmem_limit_bytes=60 * 2**20
        ),
        name="begin_layer",
    )(tokens, segments, routes, cotangent, *shards, w_in, w_out)


def backward_kernel(
    experts,
    x_ref,
    g_ref,
    segment_ref,
    route_ref,
    full_ref,
    gains_ref,
    qkv_ref,
    lse_ref,
    y1_ref,
    prob_ref,
    returned_ref,
    back_ref,
    out_ref,
    grad_x_ref,
    branch_ref,
    gqkv_ref,
    glog_ref,
    gain_ref,
    go_ref,
    gy1_ref,
):
    seq_len, model_width = x_ref.shape
    scale = 1.0 / math.sqrt(model_width // HEADS)
    g = g_ref[...].astype(f32)
    route = column(route_ref[...])
    chosen = choose_slots(route, returned_ref.shape[0], experts)
    moe = dot(chosen, returned_ref[...])
    prob = prob_ref[...]
    one_hot = one_hot_of(route)
    gate = jnp.sum(prob * one_hot, axis=1, keepdims=True)
    y1 = y1_ref[...]
    out_ref[...] = (y1 + gate * moe).astype(bf16)
    choice = one_hot * jnp.sum(g * moe, axis=1, keepdims=True)
    glog = (prob * (choice - jnp.sum(prob * choice, axis=1, keepdims=True))).astype(bf16)
    glog_ref[...] = glog
    grad_h = dot(chosen, back_ref[...]) + dot_nt(glog, full_ref[:, pl.ds(4 * model_width, 128)])
    n2, inv2 = normalize(y1)
    gain_ref[1:2, :] = jnp.sum(grad_h * n2, axis=0, keepdims=True)
    gy1 = g + norm_back(grad_h * gains_ref[1:2, :], n2, inv2)
    gy1_ref[...] = gy1
    branch_ref[...] = gy1.astype(bf16)
    go_ref[...] = dot_nt(branch_ref[...], full_ref[:, pl.ds(3 * model_width, model_width)]).astype(bf16)

    allowed = allowed_pairs(segment_ref[...])
    low_half = lanes_of((seq_len, 128)) < 64

    @pl.loop(0, model_width // 128)
    def _(pair):
        at = pl.multiple_of(pair * 128, 128)
        query = qkv_ref[:, pl.ds(at, 128)]
        key = qkv_ref[:, pl.ds(model_width + at, 128)]
        value = qkv_ref[:, pl.ds(2 * model_width + at, 128)]
        grad_o = go_ref[:, pl.ds(at, 128)]
        parts = []
        for side in range(2):
            mine = low_half if side == 0 else jnp.logical_not(low_half)
            scores = dot_nt(jnp.where(mine, query, 0.0).astype(bf16), key) * scale
            head = lanes_of(lse_ref.shape) == 2 * pair + side
            lse = jnp.sum(jnp.where(head, lse_ref[...], 0.0), axis=1, keepdims=True)
            p = jnp.exp(jnp.where(allowed, scores, masked_value) - lse)
            gp = dot_nt(jnp.where(mine, grad_o, 0.0).astype(bf16), value)
            gs = (p * (gp - jnp.sum(p * gp, axis=1, keepdims=True))).astype(bf16)
            parts.append((dot(gs, key) * scale, dot_tn(gs, query) * scale, dot_tn(p.astype(bf16), grad_o)))
        for i in range(3):
            both = jnp.where(low_half, parts[0][i], parts[1][i]).astype(bf16)
            gqkv_ref[:, pl.ds(i * model_width + at, 128)] = both

    ga = dot_nt(gqkv_ref[...], full_ref[:, pl.ds(0, 3 * model_width)])
    n1, inv1 = normalize(x_ref[...].astype(f32))
    gain_ref[0:1, :] = jnp.sum(ga * n1, axis=0, keepdims=True)
    grad_x_ref[...] = gy1_ref[...] + norm_back(ga * gains_ref[0:1, :], n1, inv1)


def kernel_params(flops):
    return dict(
        compiler_params=pltpu.CompilerParams(vmem_limit_bytes=56 * 2**20),
        cost_estimate=pl.CostEstimate(flops=flops, bytes_accessed=2**20, transcendentals=0),
    )


def attention_backward(experts, *operands):
    seq_len, model_width = operands[0].shape
    shape = jax.ShapeDtypeStruct
    return pl.pallas_call(
        functools.partial(backward_kernel, experts),
        out_shape=[
            shape((seq_len, model_width), bf16),
            shape((seq_len, model_width), f32),
            shape((seq_len, model_width), bf16),
            shape((seq_len, 3 * model_width), bf16),
            shape((seq_len, 128), bf16),
            shape((2, model_width), f32),
        ],
        scratch_shapes=[
            pltpu.VMEM((seq_len, model_width), bf16),
            pltpu.VMEM((seq_len, model_width), f32),
        ],
        name="attention_backward",
        **kernel_params(30 * 10**9),
    )(*operands)


def expert_kernel(
    chips,
    experts,
    got_h,
    got_g,
    w_in_hbm,
    w_out_hbm,
    full,
    z0,
    b0,
    z1,
    b1,
    keep_in,
    send_in,
    keep_out,
    got_out,
    x_buf,
    gz_buf,
    w_in,
    w_out,
    router,
    act,
    gu,
    own,
    part,
    part_got,
    out_part,
    out_stage,
    in_part,
    in_stage,
    load,
    sy,
    ry,
    sz,
    rz,
    lz,
    sx,
    rx,
    st,
):
    block, chip, core, peer_x, peer_y, peer_core, peers_z = place_of(chips)
    owner = lax.axis_index("expert")
    micros, rows, model_width = got_h.shape
    half = w_in.shape[1]
    mine = rows // 2
    padded = part.shape[3]
    row_x = block % 2
    step = 256
    backs = ((z0, b0), (z1, b1))

    sources = [
        (got_h.at[0], x_buf.at[pl.ds(0, rows)]),
        (full.at[:, pl.ds(4 * model_width, 128)], router),
        (got_g.at[0], gz_buf.at[pl.ds(0, rows)]),
        (w_in_hbm, w_in),
        (w_out_hbm, w_out),
        (got_h.at[1], x_buf.at[pl.ds(rows, rows)]),
        (got_g.at[1], gz_buf.at[pl.ds(rows, rows)]),
    ]
    loads = []
    for i, (src, dst) in enumerate(sources):
        loads.append(pltpu.make_async_copy(src, dst, load.at[i]))
        loads[-1].start()
    greet(
        [peer_x, peer_y]
        + [{"expert": lax.rem(owner + k, experts)} for k in range(1, experts)]
    )

    def of(m):
        return pl.ds(m * rows, rows)

    def open_rows(m):
        logits = dot(x_buf[of(m), :], router[...])
        lanes = lanes_of(logits.shape)
        logits = jnp.where(lanes < experts, logits, masked_value)
        weight = jnp.exp(logits - jnp.max(logits, axis=1, keepdims=True))
        weight = jnp.where(lanes < experts, weight, 0.0)
        picked = jnp.sum(jnp.where(lanes == owner, weight, 0.0), axis=1, keepdims=True)
        gate = picked / jnp.sum(weight, axis=1, keepdims=True)
        gz_buf[of(m), :] = (gate * gz_buf[of(m), :].astype(f32)).astype(bf16)

        @pl.loop(0, half // step)
        def _(j):
            at = pl.ds(pl.multiple_of(j * step, step), step)
            u = dot(x_buf[of(m), :], w_in[:, at])
            back = dot_nt(gz_buf[of(m), :], w_out[at, :])
            root = math.sqrt(2.0 / math.pi)
            square = u * u
            bend = jnp.tanh(root * (u + 0.044715 * (u * square)))
            act[of(m), at] = (0.5 * u * (1.0 + bend)).astype(bf16)
            slope = 0.5 * (1.0 + bend) + 0.5 * u * (1.0 - bend * bend) * (
                root * (1.0 + (3.0 * 0.044715) * square)
            )
            gu[of(m), at] = (back * slope).astype(bf16)

    def swap(m, way):
        return pltpu.make_async_remote_copy(
            src_ref=part.at[m, way],
            dst_ref=part_got.at[m, way],
            send_sem=sy.at[m, way],
            recv_sem=ry.at[m, way],
            device_id=peer_y,
            device_id_type=MESH,
        )

    def close_rows(m, way):
        @pl.loop(0, model_width // step)
        def _(j):
            at = pl.ds(pl.multiple_of(j * step, step), step)
            if way == 0:
                total = dot(act[of(m), :], w_out[:, at])
            else:
                total = dot_nt(gu[of(m), :], w_in[at, :])
            own[m, way, :, at] = total[:mine]
            for e in range(experts):
                start = mine + e * padded
                part[m, way, e, :, at] = total[start : start + padded].astype(bf16)

        swap(m, way).start()

    def to_source(m, way, k):
        peer = lax.rem(owner + k, experts)
        return pltpu.make_async_remote_copy(
            src_ref=part.at[m, way, peer],
            dst_ref=backs[m][way].at[owner],
            send_sem=sz.at[m, way, k],
            recv_sem=rz.at[m, way, k],
            device_id={"expert": peer},
            device_id_type=MESH,
        )

    def to_self(m, way):
        return pltpu.make_async_copy(
            part.at[m, way, owner], backs[m][way].at[owner], lz.at[m, way]
        )

    def give_back(m, way):
        swap(m, way).wait()

        @pl.loop(0, experts)
        def _(e):
            at = pl.ds(pl.multiple_of(e * padded, padded), padded)
            total = own[m, way, at, :] + part_got[m, way, e].astype(f32)
            part[m, way, e] = total.astype(bf16)

        to_self(m, way).start()

        @pl.loop(1, experts)
        def _(k):
            to_source(m, way, k).start()

    def end_back(m, way):
        to_self(m, way).wait()

        @pl.loop(1, experts)
        def _(k):
            to_source(m, way, k).wait()

    chunks = out_part.shape[0]

    def out_rows(side, j):
        start = side * (half // 2) + j * step
        return dot_tn(act[:, pl.ds(pl.multiple_of(start, step), step)], gz_buf[...])

    def to_x(j):
        return pltpu.make_async_remote_copy(
            src_ref=out_part.at[j],
            dst_ref=got_out.at[j],
            send_sem=sx.at[j],
            recv_sem=rx.at[j],
            device_id=peer_x,
            device_id_type=MESH,
        )

    def put_out(j, slot):
        return pltpu.make_async_copy(out_stage.at[slot], keep_out.at[j], st.at[slot])

    def send_out_rows():
        @pl.loop(0, chunks)
        def _(j):
            out_part[j] = out_rows(1 - row_x, j).astype(bf16)
            to_x(j).start()

    def keep_out_rows():
        for j in range(chunks):
            if j > 1:
                put_out(j - 2, j % 2).wait()
            out_stage[j % 2] = out_rows(row_x, j)
            put_out(j, j % 2).start()

    quarter = in_stage.shape[0]

    def in_rows(y, x):
        start = (2 * y + x) * quarter
        return pl.ds(pl.multiple_of(start, quarter), quarter)

    def in_copies(y):
        return (
            pltpu.make_async_copy(in_part, send_in.at[y], st.at[2]),
            pltpu.make_async_copy(in_stage, keep_in.at[y], st.at[3]),
        )

    def first_rows():
        for y in range(2):
            for kind in range(2):
                if y:
                    in_copies(0)[kind].wait()
                cols = in_rows(y, 1 - row_x if kind == 0 else row_x)

                @pl.loop(0, half // (2 * step))
                def _(j):
                    at = pl.ds(pl.multiple_of(j * 2 * step, 2 * step), 2 * step)
                    value = dot_tn(x_buf[:, cols], gu[:, at])
                    if kind == 0:
                        in_part[:, at] = value.astype(bf16)
                    else:
                        in_stage[:, at] = value

                in_copies(y)[kind].start()

    for i in range(5):
        loads[i].wait()
    open_rows(0)
    close_rows(0, 0)
    close_rows(0, 1)
    for i in range(5, 7):
        loads[i].wait()
    open_rows(1)
    close_rows(1, 0)
    give_back(0, 0)
    close_rows(1, 1)
    send_out_rows()
    give_back(0, 1)
    first_rows()
    keep_out_rows()
    give_back(1, 0)
    give_back(1, 1)
    for j in range(chunks - 2, chunks):
        put_out(j, j % 2).wait()
    for copy in in_copies(1):
        copy.wait()
    for m in range(micros):
        for way in range(2):
            end_back(m, way)

    @pl.loop(0, chunks)
    def _(j):
        to_x(j).wait()


def run_experts(got_h, got_g, w_in, w_out, full, chips):
    experts = 2 * chips
    micros, _, _, padded, model_width = got_h.shape
    rows = 2 * experts * padded
    half = w_in.shape[1]
    shape = jax.ShapeDtypeStruct
    hbm = pl.BlockSpec(memory_space=pl.ANY)
    slots = shape((experts, padded, model_width), bf16)
    chunks = half // 2 // 256
    quarter = model_width // 4
    spots = (micros, 2, experts, padded, model_width)
    return pl.pallas_call(
        functools.partial(expert_kernel, chips, experts),
        out_shape=[
            slots,
            slots,
            slots,
            slots,
            shape((2, quarter, half), f32),
            shape((2, quarter, half), bf16),
            shape((chunks, 256, model_width), f32),
            shape((chunks, 256, model_width), bf16),
        ],
        in_specs=[hbm] * 5,
        out_specs=[hbm] * 8,
        scratch_shapes=[
            pltpu.VMEM((micros * rows, model_width), bf16),
            pltpu.VMEM((micros * rows, model_width), bf16),
            pltpu.VMEM((model_width, half), bf16),
            pltpu.VMEM((half, model_width), bf16),
            pltpu.VMEM((model_width, 128), bf16),
            pltpu.VMEM((micros * rows, half), bf16),
            pltpu.VMEM((micros * rows, half), bf16),
            pltpu.VMEM((micros, 2, rows // 2, model_width), f32),
            pltpu.VMEM(spots, bf16),
            pltpu.VMEM(spots, bf16),
            pltpu.VMEM((chunks, 256, model_width), bf16),
            pltpu.VMEM((2, 256, model_width), f32),
            pltpu.VMEM((quarter, half), bf16),
            pltpu.VMEM((quarter, half), f32),
            DMA((7,)),
            DMA((micros, 2)),
            DMA((micros, 2)),
            DMA((micros, 2, experts)),
            DMA((micros, 2, experts)),
            DMA((micros, 2)),
            DMA((chunks,)),
            DMA((chunks,)),
            DMA((4,)),
        ],
        compiler_params=pltpu.CompilerParams(
            collective_id=3, has_side_effects=True, vmem_limit_bytes=63 * 2**20
        ),
        name="run_experts",
    )(
        got_h.reshape(micros, rows, model_width),
        got_g.reshape(micros, rows, model_width),
        w_in,
        w_out,
        full,
    )


def reduce_expert_grads(keep_in, send_in, block):
    row_y = block // 2
    sums = keep_in + swap_x(send_in).astype(f32)
    own = lax.dynamic_slice_in_dim(sums, row_y, 1, 0)[0]
    other = lax.dynamic_slice_in_dim(sums, 1 - row_y, 1, 0)[0].astype(bf16)
    return own, other


def join_expert_grads(own, other, block):
    rows, half = own.shape
    row_y = block // 2
    got = swap_y(other).astype(f32)
    done_in = jnp.zeros((rows, 2 * half), f32)
    done_in = lax.dynamic_update_slice(done_in, own, (0, row_y * half))
    done_in = lax.dynamic_update_slice(done_in, got, (0, (1 - row_y) * half))
    return done_in


def on_device(
    tokens,
    segment_ids,
    routes,
    cotangent,
    w_qkv,
    w_attn_out,
    w_router,
    gain_attn,
    gain_moe,
    w_expert_in,
    w_expert_out,
):
    micro_count, _, seq_len, model_width = tokens.shape
    experts = w_router.shape[1]
    block = lax.axis_index("dp")
    chips = model_width // w_qkv.shape[0] // 8
    micros = range(micro_count)

    spare = jnp.zeros((w_qkv.shape[0], 128 - 2 - experts), bf16)
    small = jnp.concatenate([w_router, gain_attn[:, None], gain_moe[:, None], spare], axis=1)
    tokens, cotangent, segment_ids = tokens[:, 0], cotangent[:, 0], segment_ids
    routes = routes.reshape(micro_count, 1, seq_len)
    begun = begin_layer(
        tokens,
        segment_ids,
        routes,
        cotangent,
        (w_qkv, w_attn_out, small),
        w_expert_in[0],
        w_expert_out[0],
        chips,
    )
    gains, gathered, w_in, w_out, got_g, got_h = begun[7:]
    w_in = w_in.reshape(model_width, -1)
    w_out = w_out.reshape(-1, model_width)
    names = names_all = ("attn_in", "qkv", "lse", "mixed", "residual", "hidden", "prob")
    state = [dict(zip(names, (value[m] for value in begun[:7]))) for m in micros]
    ran = run_experts(got_h, got_g, w_in, w_out, gathered, chips)
    for m in micros:
        state[m]["returned"] = ran[2 * m].reshape(-1, model_width)
        state[m]["grad_back"] = ran[2 * m + 1].reshape(-1, model_width)
    keep_in, send_in, keep_out, got_out = ran[4:]
    own, other = reduce_expert_grads(keep_in, send_in, block)
    grad_out = (keep_out + got_out.astype(f32)).reshape(-1, model_width)

    def both(name):
        if name in names_all:
            return begun[names_all.index(name)].reshape(-1, begun[names_all.index(name)].shape[2])
        return jnp.concatenate([s[name] for s in state], axis=0)

    for m in micros:
        s = state[m]
        names = ("output", "grad_tokens", "branch", "grad_qkv", "grad_logit", "gain")
        s.update(
            zip(
                names,
                attention_backward(
                    experts,
                    tokens[m],
                    cotangent[m],
                    segment_ids[m],
                    routes[m],
                    gathered,
                    gains,
                    s["qkv"],
                    s["lse"],
                    s["residual"],
                    s["prob"],
                    s["returned"],
                    s["grad_back"],
                ),
            )
        )
    term_router = dot_tn(both("hidden"), both("grad_logit"))[:, :experts]
    term_out = dot_tn(both("mixed"), both("branch")).astype(bf16)
    term_qkv = dot_tn(both("attn_in"), both("grad_qkv")).astype(bf16)
    gain_sum = sum(s["gain"] for s in state).T
    spare = jnp.zeros((model_width, 128 - 2 - experts), f32)
    term_small = jnp.concatenate([term_router, gain_sum, spare], axis=1).astype(bf16)
    term_small, other = lax.optimization_barrier((term_small, other))
    grad_in = join_expert_grads(own, other, block)
    grad_qkv, grad_attn_out, small_sum = reduce_rows((term_qkv, term_out, term_small), chips)
    return (
        jnp.stack([s["output"] for s in state])[:, None],
        jnp.stack([s["grad_tokens"] for s in state])[:, None],
        grad_qkv,
        grad_attn_out,
        small_sum[:, :experts],
        small_sum[:, experts],
        small_sum[:, experts + 1],
        grad_in[None],
        grad_out[None],
    )


def solution(mesh):
    rows = P(("dp", "expert"))
    seqs = P(None, ("dp", "expert"))
    owned = P("expert", "dp", None)
    return jax.shard_map(
        on_device,
        mesh=mesh,
        in_specs=(seqs, seqs, seqs, seqs, rows, rows, rows, rows, rows, owned, owned),
        out_specs=(seqs, seqs, rows, rows, rows, rows, rows, owned, owned),
        check_vma=False,
    )
```

```python
import functools
import math

import jax
import jax.numpy as jnp
from jax import lax
from jax.experimental import pallas as pl
from jax.experimental.pallas import tpu as pltpu
from jax.sharding import PartitionSpec as P

HEADS = 16
epsilon = 1e-05
masked_value = -1e30
pieces = 8
f32 = jnp.float32
bf16 = jnp.bfloat16

MESH = pl.DeviceIdType.MESH
DMA = pltpu.SemaphoreType.DMA


def flip(index, mask):
    bit = 1
    while bit <= mask:
        if mask & bit:
            index = index + bit - 2 * bit * ((index // bit) % 2)
        bit *= 2
    return index


def place_of(chips):
    block = lax.axis_index("dp")
    owner = lax.axis_index("expert")
    peer_x = {"dp": flip(block, 1)}
    peer_y = {"dp": flip(block, 2)}
    peer_core = {"expert": flip(owner, 1)}
    peers_z = [{"expert": flip(owner, 2 * k)} for k in range(chips)]
    return block, owner // 2, owner % 2, peer_x, peer_y, peer_core, peers_z


def greet(peers):
    barrier = pltpu.get_barrier_semaphore()
    for peer in peers:
        pl.semaphore_signal(barrier, inc=1, device_id=peer, device_id_type=MESH)
    pl.semaphore_wait(barrier, len(peers))


def send(src, dst, send_sem, recv_sem, peer):
    copy = pltpu.make_async_remote_copy(
        src_ref=src, dst_ref=dst, send_sem=send_sem, recv_sem=recv_sem,
        device_id=peer, device_id_type=MESH,
    )
    copy.start()
    return copy


def normalize(values):
    row_mean = jnp.mean(values, axis=-1, keepdims=True)
    centered = values - row_mean
    inv_scale = lax.rsqrt(jnp.mean(centered * centered, axis=-1, keepdims=True) + epsilon)
    return (centered * inv_scale, inv_scale)


def norm_back(grad_normed, normed, inv_scale):
    return inv_scale * (
        grad_normed
        - jnp.mean(grad_normed, axis=-1, keepdims=True)
        - normed * jnp.mean(grad_normed * normed, axis=-1, keepdims=True)
    )


def dot(a, b):
    return jnp.dot(a, b, preferred_element_type=f32)


def dot_nt(a, b):
    return lax.dot_general(a, b, (((1,), (1,)), ((), ())), preferred_element_type=f32)


def dot_tn(a, b):
    return lax.dot_general(a, b, (((0,), (0,)), ((), ())), preferred_element_type=f32)


def lanes_of(shape):
    return lax.broadcasted_iota(jnp.int32, shape, 1)


def rows_of(shape):
    return lax.broadcasted_iota(jnp.int32, shape, 0)


def column(row):
    return jnp.transpose(jnp.broadcast_to(row.astype(f32), (128, row.shape[1])))[:, :1]


def one_hot_of(route):
    return jnp.where(lanes_of((route.shape[0], 128)).astype(f32) == route, 1.0, 0.0)


def choose_slots(route, spots, experts):
    seq_len = route.shape[0]
    capacity = (9 * seq_len + 8 * experts - 1) // (8 * experts)
    one_hot = one_hot_of(route)
    square = (seq_len, seq_len)
    before = jnp.where(lanes_of(square) < rows_of(square), 1.0, 0.0).astype(bf16)
    place = jnp.sum(dot(before, one_hot.astype(bf16)) * one_hot, axis=1, keepdims=True)
    slot = jnp.where(place < capacity, route * (spots // experts) + place, -1.0)
    return jnp.where(lanes_of((seq_len, spots)).astype(f32) == slot, 1.0, 0.0).astype(bf16)


def allowed_pairs(segment_row):
    square = (segment_row.shape[1],) * 2
    same = column(segment_row) == segment_row.astype(f32)
    return (lanes_of(square) <= rows_of(square)) & same


def begin_kernel(
    chips,
    experts,
    tokens,
    segments,
    routes,
    cotangent,
    shard_qkv,
    shard_out,
    shard_small,
    w_in,
    w_out,
    attn_in,
    qkv,
    lse,
    mixed,
    residual,
    hidden,
    probs,
    gains,
    kept_full,
    full_in,
    full_out,
    got_g,
    got_h,
    full,
    slots_g,
    slots_h,
    hold_in,
    hold_out,
    own_sem,
    sz,
    rz,
    sx,
    rx,
    sy,
    ry,
    sc,
    rc,
    sw,
    rw,
    lw,
    sd,
    rd,
    se,
    re,
    ld,
):
    block, chip, core, peer_x, peer_y, peer_core, peers_z = place_of(chips)
    owner = lax.axis_index("expert")
    micros, seq_len, model_width = tokens.shape
    rows = shard_qkv.shape[0]
    width = full.shape[1]
    cut = (width // 128 + 1) // 2 * 128
    halves = (pl.ds(0, cut), pl.ds(cut, width - cut))
    every = pl.ds(0, width)
    half = w_in.shape[1] // 2
    row_y, row_x = block // 2, block % 2

    def part(origin, step, columns):
        start = ((flip(block, origin) * chips + flip(chip, step)) * 2 + core) * rows
        return full.at[pl.ds(pl.multiple_of(start, rows), rows), columns]

    own_copies = []
    for i, (src, at) in enumerate(
        ((shard_qkv, 0), (shard_out, 3 * model_width), (shard_small, 4 * model_width))
    ):
        dst = part(0, 0, pl.ds(at, src.shape[1]))
        own_copies.append(pltpu.make_async_copy(src, dst, own_sem.at[i]))
        own_copies[-1].start()
    others = [{"expert": lax.rem(owner + k, experts)} for k in range(1, experts)]
    greet([peer_x, peer_y] + others)
    for copy in own_copies:
        copy.wait()

    mine = part(0, 0, every)
    along_z = [None] + [send(mine, mine, sz.at[k], rz.at[k], peers_z[k]) for k in range(1, chips)]
    along_x = [[None] * 3 for _ in range(chips)]
    along_y = [[None] * 3 for _ in range(chips)]
    across = [[None] * 4 for _ in range(chips)]

    def to_core(k, origin):
        piece = part(origin, k, every)
        across[k][origin] = send(
            piece, piece, sc.at[k, origin], rc.at[k, origin], peer_core
        )

    def pass_on(k):
        along_x[k][1].wait_recv()
        to_core(k, 1)
        along_y[k][1].wait_recv()
        to_core(k, 2)
        along_x[k][2].wait_recv()
        along_y[k][2].wait_recv()
        to_core(k, 3)

    def spread(k):
        for turn in range(2):
            for copies, s, r, peer, side in (
                (along_x, sx, rx, peer_x, turn),
                (along_y, sy, ry, peer_y, 1 - turn),
            ):
                piece = part(0, k, halves[side])
                copies[k][turn] = send(piece, piece, s.at[k, turn], r.at[k, turn], peer)
        to_core(k, 0)

    def turn_corner(k):
        along_x[k][0].wait_recv()
        piece = part(1, k, halves[0])
        along_y[k][2] = send(piece, piece, sy.at[k, 2], ry.at[k, 2], peer_y)
        along_y[k][0].wait_recv()
        piece = part(2, k, halves[1])
        along_x[k][2] = send(piece, piece, sx.at[k, 2], rx.at[k, 2], peer_x)

    piece_rows = w_out.shape[0] // pieces
    out_x = []

    def send_piece():
        j = len(out_x)
        at = pl.ds(j * piece_rows, piece_rows)
        out_x.append(
            send(w_out.at[at], full_out.at[row_x, at], sw.at[3 + j], rw.at[3 + j], peer_x)
        )

    spread(0)

    def put_slots(slots, m, values):
        packed = dot_tn(choose_slots(column(routes[m]), experts * slots.shape[2], experts), values)
        packed = packed.astype(bf16)
        for e in range(experts):
            size = slots.shape[2]
            slots[m, e] = packed[e * size : (e + 1) * size]

    for m in range(micros):
        put_slots(slots_g, m, cotangent[m])

    for k in range(chips):
        if k:
            along_z[k].wait_recv()
            spread(k)
            pass_on(k - 1)
        turn_corner(k)
        if k < pieces // 2:
            send_piece()

    local_in = pltpu.make_async_copy(w_in.at[:, pl.ds(row_y * half, half)], hold_in, lw.at[0])
    local_out = pltpu.make_async_copy(w_out, hold_out, lw.at[1])
    local_in.start()
    local_out.start()
    from_y = send(
        w_in.at[:, pl.ds((1 - row_y) * half, half)], full_in.at[block], sw.at[0], rw.at[0], peer_y
    )
    from_x = send(
        w_in.at[:, pl.ds(row_y * half, half)], full_in.at[block], sw.at[1], rw.at[1], peer_x
    )
    while len(out_x) < pieces:
        send_piece()

    def slot_copies(way, slots, got, m):
        def to_owner(k):
            peer = lax.rem(owner + k, experts)
            return pltpu.make_async_remote_copy(
                src_ref=slots.at[m, peer],
                dst_ref=got.at[m, 0, owner],
                send_sem=sd.at[way, m, k],
                recv_sem=rd.at[way, m, k],
                device_id={"expert": peer},
                device_id_type=MESH,
            )

        def to_y(k):
            origin = lax.rem(owner - k + experts, experts)
            return pltpu.make_async_remote_copy(
                src_ref=got.at[m, 0, origin],
                dst_ref=got.at[m, 1, origin],
                send_sem=se.at[way, m, k],
                recv_sem=re.at[way, m, k],
                device_id=peer_y,
                device_id_type=MESH,
            )

        own = pltpu.make_async_copy(slots.at[m, owner], got.at[m, 0, owner], ld.at[way, m])
        return to_owner, to_y, own

    def start_slots(way, slots, got, m):
        to_owner, to_y, own = slot_copies(way, slots, got, m)
        own.start()

        @pl.loop(1, experts)
        def _(k):
            to_owner(k).start()

    def relay_slots(way, slots, got, m):
        to_owner, to_y, own = slot_copies(way, slots, got, m)
        own.wait()
        to_y(0).start()

        @pl.loop(1, experts)
        def _(k):
            to_owner(k).wait_recv()
            to_y(k).start()

    def end_slots(way, slots, got, m):
        to_owner, to_y, own = slot_copies(way, slots, got, m)

        @pl.loop(1, experts)
        def _(k):
            to_owner(k).wait_send()

        @pl.loop(0, experts)
        def _(k):
            to_y(k).wait()

    for m in range(micros):
        start_slots(0, slots_g, got_g, m)
    pass_on(chips - 1)
    for k in range(chips):
        for origin in range(4):
            across[k][origin].wait_recv()
    keep = pltpu.make_async_copy(full, kept_full, own_sem.at[3])
    keep.start()
    small = jnp.transpose(full[:, pl.ds(4 * model_width, 128)].astype(f32))
    gains[...] = small[experts : experts + 2]
    local_in.wait()
    local_out.wait()
    store_in = pltpu.make_async_copy(hold_in, full_in.at[block], lw.at[0])
    store_out = pltpu.make_async_copy(hold_out, full_out.at[row_x], lw.at[1])
    store_in.start()
    store_out.start()

    scale = 1.0 / math.sqrt(model_width // HEADS)
    low_half = lanes_of((seq_len, 128)) < 64
    diagonal = None
    for m in range(micros):
        x = tokens[m].astype(f32)
        attn_in[m] = (normalize(x)[0] * gains[0:1, :]).astype(bf16)

        @pl.loop(0, 3 * model_width // 512)
        def _(j):
            at = pl.ds(pl.multiple_of(j * 512, 512), 512)
            qkv[m, :, at] = dot(attn_in[m], full[:, at]).astype(bf16)

        allowed = allowed_pairs(segments[m])
        lse[m] = jnp.zeros(lse.shape[1:], f32)

        @pl.loop(0, model_width // 128)
        def _(pair):
            at = pl.multiple_of(pair * 128, 128)
            query = qkv[m, :, pl.ds(at, 128)]
            key = qkv[m, :, pl.ds(model_width + at, 128)]
            value = qkv[m, :, pl.ds(2 * model_width + at, 128)]
            outs = []
            for side in range(2):
                here = low_half if side == 0 else jnp.logical_not(low_half)
                scores = dot_nt(jnp.where(here, query, 0.0).astype(bf16), key) * scale
                masked = jnp.where(allowed, scores, masked_value)
                top = jnp.max(masked, axis=1, keepdims=True)
                weight = jnp.exp(masked - top)
                norm = jnp.sum(weight, axis=1, keepdims=True)
                outs.append(dot((weight / norm).astype(bf16), value))
                head = lanes_of(lse.shape[1:]) == 2 * pair + side
                lse[m] = jnp.where(head, top + jnp.log(norm), lse[m])
            mixed[m, :, pl.ds(at, 128)] = jnp.where(low_half, outs[0], outs[1]).astype(bf16)

        y1 = x + dot(mixed[m], full[:, pl.ds(3 * model_width, model_width)])
        residual[m] = y1
        low = (normalize(y1)[0] * gains[1:2, :]).astype(bf16)
        hidden[m] = low
        put_slots(slots_h, m, low)
        start_slots(1, slots_h, got_h, m)
        logits = dot(low, full[:, pl.ds(4 * model_width, 128)])
        real = lanes_of(logits.shape) < experts
        logits = jnp.where(real, logits, masked_value)
        weight = jnp.where(real, jnp.exp(logits - jnp.max(logits, axis=1, keepdims=True)), 0.0)
        probs[m] = weight / jnp.sum(weight, axis=1, keepdims=True)
        if m == 0:
            from_y.wait_recv()
            piece = full_in.at[flip(block, 2)]
            diagonal = send(piece, piece, sw.at[2], rw.at[2], peer_x)
        relay_slots(0, slots_g, got_g, m)
        if m:
            relay_slots(1, slots_h, got_h, m - 1)
    relay_slots(1, slots_h, got_h, micros - 1)

    for m in range(micros):
        end_slots(0, slots_g, got_g, m)
        end_slots(1, slots_h, got_h, m)
    keep.wait()
    store_in.wait()
    store_out.wait()
    from_y.wait_send()
    for copy in (from_x, diagonal, *out_x):
        copy.wait()
    for k in range(chips):
        if k:
            along_z[k].wait_send()
        for turn in range(3):
            along_x[k][turn].wait_send()
            along_y[k][turn].wait_send()
        for origin in range(4):
            across[k][origin].wait_send()


def begin_layer(tokens, segments, routes, cotangent, shards, w_in, w_out, chips):
    experts = 2 * chips
    micros, seq_len, model_width = tokens.shape
    capacity = (9 * seq_len + 8 * experts - 1) // (8 * experts)
    padded = (capacity + 7) // 8 * 8
    width = 4 * model_width + 128
    rows, half = w_in.shape[0], w_in.shape[1] // 2
    shape = jax.ShapeDtypeStruct
    vmem, hbm = pl.BlockSpec(memory_space=pltpu.VMEM), pl.BlockSpec(memory_space=pl.ANY)
    spots = (micros, experts, padded, model_width)
    return pl.pallas_call(
        functools.partial(begin_kernel, chips, experts),
        out_shape=[
            shape((micros, seq_len, model_width), bf16),
            shape((micros, seq_len, 3 * model_width), bf16),
            shape((micros, seq_len, 128), f32),
            shape((micros, seq_len, model_width), bf16),
            shape((micros, seq_len, model_width), f32),
            shape((micros, seq_len, model_width), bf16),
            shape((micros, seq_len, 128), f32),
            shape((2, model_width), f32),
            shape((model_width, width), bf16),
            shape((4, rows, half), bf16),
            shape((2,) + w_out.shape, bf16),
            shape((micros, 2, experts, padded, model_width), bf16),
            shape((micros, 2, experts, padded, model_width), bf16),
        ],
        in_specs=[vmem] * 4 + [hbm] * 5,
        out_specs=[vmem] * 8 + [hbm] * 5,
        scratch_shapes=[
            pltpu.VMEM((model_width, width), bf16),
            pltpu.VMEM(spots, bf16),
            pltpu.VMEM(spots, bf16),
            pltpu.VMEM((rows, half), bf16),
            pltpu.VMEM(w_out.shape, bf16),
            DMA((4,)),
            DMA((chips,)),
            DMA((chips,)),
            DMA((chips, 3)),
            DMA((chips, 3)),
            DMA((chips, 3)),
            DMA((chips, 3)),
            DMA((chips, 4)),
            DMA((chips, 4)),
            DMA((3 + pieces,)),
            DMA((3 + pieces,)),
            DMA((2,)),
            DMA((2, micros, experts)),
            DMA((2, micros, experts)),
            DMA((2, micros, experts)),
            DMA((2, micros, experts)),
            DMA((2, micros)),
        ],
        compiler_params=pltpu.CompilerParams(
            collective_id=1, has_side_effects=True, vmem_limit_bytes=60 * 2**20
        ),
        name="begin_layer",
    )(tokens, segments, routes, cotangent, *shards, w_in, w_out)


def expert_kernel(
    chips,
    experts,
    got_h,
    got_g,
    w_in_hbm,
    w_out_hbm,
    full,
    returned,
    grad_back,
    keep_in,
    send_in,
    grad_out,
    x_buf,
    gz_buf,
    w_in,
    w_out,
    router,
    act,
    gu,
    own,
    part,
    part_got,
    out_part,
    out_got,
    out_stage,
    in_part,
    in_stage,
    load,
    sy,
    ry,
    sz,
    rz,
    lz,
    sx,
    rx,
    st,
):
    block, chip, core, peer_x, peer_y, peer_core, peers_z = place_of(chips)
    owner = lax.axis_index("expert")
    micros, rows, model_width = got_h.shape
    half = w_in.shape[1]
    mine = rows // 2
    padded = part.shape[3]
    row_x = block % 2
    step = 256
    backs = (returned, grad_back)

    sources = [
        (got_h.at[0], x_buf.at[pl.ds(0, rows)]),
        (full.at[:, pl.ds(4 * model_width, 128)], router),
        (got_g.at[0], gz_buf.at[pl.ds(0, rows)]),
        (w_in_hbm, w_in),
        (w_out_hbm, w_out),
        (got_h.at[1], x_buf.at[pl.ds(rows, rows)]),
        (got_g.at[1], gz_buf.at[pl.ds(rows, rows)]),
    ]
    loads = []
    for i, (src, dst) in enumerate(sources):
        loads.append(pltpu.make_async_copy(src, dst, load.at[i]))
        loads[-1].start()
    greet(
        [peer_x, peer_y]
        + [{"expert": lax.rem(owner + k, experts)} for k in range(1, experts)]
    )

    def of(m):
        return pl.ds(m * rows, rows)

    def open_rows(m):
        logits = dot(x_buf[of(m), :], router[...])
        lanes = lanes_of(logits.shape)
        logits = jnp.where(lanes < experts, logits, masked_value)
        weight = jnp.exp(logits - jnp.max(logits, axis=1, keepdims=True))
        weight = jnp.where(lanes < experts, weight, 0.0)
        picked = jnp.sum(jnp.where(lanes == owner, weight, 0.0), axis=1, keepdims=True)
        gate = picked / jnp.sum(weight, axis=1, keepdims=True)
        gz_buf[of(m), :] = (gate * gz_buf[of(m), :].astype(f32)).astype(bf16)

        @pl.loop(0, half // step)
        def _(j):
            at = pl.ds(pl.multiple_of(j * step, step), step)
            u = dot(x_buf[of(m), :], w_in[:, at])
            back = dot_nt(gz_buf[of(m), :], w_out[at, :])
            root = math.sqrt(2.0 / math.pi)
            square = u * u
            bend = jnp.tanh(root * (u + 0.044715 * (u * square)))
            act[of(m), at] = (0.5 * u * (1.0 + bend)).astype(bf16)
            slope = 0.5 * (1.0 + bend) + 0.5 * u * (1.0 - bend * bend) * (
                root * (1.0 + (3.0 * 0.044715) * square)
            )
            gu[of(m), at] = (back * slope).astype(bf16)

    def swap(m, way):
        return pltpu.make_async_remote_copy(
            src_ref=part.at[m, way],
            dst_ref=part_got.at[m, way],
            send_sem=sy.at[m, way],
            recv_sem=ry.at[m, way],
            device_id=peer_y,
            device_id_type=MESH,
        )

    def close_rows(m, way):
        @pl.loop(0, model_width // step)
        def _(j):
            at = pl.ds(pl.multiple_of(j * step, step), step)
            if way == 0:
                total = dot(act[of(m), :], w_out[:, at])
            else:
                total = dot_nt(gu[of(m), :], w_in[at, :])
            own[m, way, :, at] = total[:mine]
            for e in range(experts):
                start = mine + e * padded
                part[m, way, e, :, at] = total[start : start + padded].astype(bf16)

        swap(m, way).start()

    def to_source(m, way, k):
        peer = lax.rem(owner + k, experts)
        return pltpu.make_async_remote_copy(
            src_ref=part.at[m, way, peer],
            dst_ref=backs[way].at[m, owner],
            send_sem=sz.at[m, way, k],
            recv_sem=rz.at[m, way, k],
            device_id={"expert": peer},
            device_id_type=MESH,
        )

    def to_self(m, way):
        return pltpu.make_async_copy(
            part.at[m, way, owner], backs[way].at[m, owner], lz.at[m, way]
        )

    def give_back(m, way):
        swap(m, way).wait()

        @pl.loop(0, experts)
        def _(e):
            at = pl.ds(pl.multiple_of(e * padded, padded), padded)
            total = own[m, way, at, :] + part_got[m, way, e].astype(f32)
            part[m, way, e] = total.astype(bf16)

        to_self(m, way).start()

        @pl.loop(1, experts)
        def _(k):
            to_source(m, way, k).start()

    def end_back(m, way):
        to_self(m, way).wait()

        @pl.loop(1, experts)
        def _(k):
            to_source(m, way, k).wait()

    chunks = out_part.shape[0]

    def out_rows(side, j):
        start = side * (half // 2) + j * step
        return dot_tn(act[:, pl.ds(pl.multiple_of(start, step), step)], gz_buf[...])

    def to_x(j):
        return pltpu.make_async_remote_copy(
            src_ref=out_part.at[j],
            dst_ref=out_got.at[j],
            send_sem=sx.at[j],
            recv_sem=rx.at[j],
            device_id=peer_x,
            device_id_type=MESH,
        )

    def put_out(j, slot):
        return pltpu.make_async_copy(out_stage.at[slot], grad_out.at[j], st.at[slot])

    def send_out_rows():
        @pl.loop(0, chunks)
        def _(j):
            out_part[j] = out_rows(1 - row_x, j).astype(bf16)
            to_x(j).start()

    def keep_out_rows():
        for j in range(chunks):
            if j > 1:
                put_out(j - 2, j % 2).wait()
            to_x(j).wait()
            out_stage[j % 2] = out_rows(row_x, j) + out_got[j].astype(f32)
            put_out(j, j % 2).start()

    quarter = in_stage.shape[0]

    def in_rows(y, x):
        start = (2 * y + x) * quarter
        return pl.ds(pl.multiple_of(start, quarter), quarter)

    def in_copies(y):
        return (
            pltpu.make_async_copy(in_part, send_in.at[y], st.at[2]),
            pltpu.make_async_copy(in_stage, keep_in.at[y], st.at[3]),
        )

    def first_rows():
        for y in range(2):
            for kind in range(2):
                if y:
                    in_copies(0)[kind].wait()
                cols = in_rows(y, 1 - row_x if kind == 0 else row_x)

                @pl.loop(0, half // (2 * step))
                def _(j):
                    at = pl.ds(pl.multiple_of(j * 2 * step, 2 * step), 2 * step)
                    value = dot_tn(x_buf[:, cols], gu[:, at])
                    if kind == 0:
                        in_part[:, at] = value.astype(bf16)
                    else:
                        in_stage[:, at] = value

                in_copies(y)[kind].start()

    for i in range(5):
        loads[i].wait()
    open_rows(0)
    close_rows(0, 0)
    close_rows(0, 1)
    for i in range(5, 7):
        loads[i].wait()
    open_rows(1)
    close_rows(1, 0)
    give_back(0, 0)
    close_rows(1, 1)
    send_out_rows()
    give_back(0, 1)
    first_rows()
    give_back(1, 0)
    give_back(1, 1)
    keep_out_rows()
    for j in range(chunks - 2, chunks):
        put_out(j, j % 2).wait()
    for copy in in_copies(1):
        copy.wait()
    for m in range(micros):
        for way in range(2):
            end_back(m, way)


def run_experts(got_h, got_g, w_in, w_out, full, chips):
    experts = 2 * chips
    micros, _, _, padded, model_width = got_h.shape
    rows = 2 * experts * padded
    half = w_in.shape[1]
    shape = jax.ShapeDtypeStruct
    hbm = pl.BlockSpec(memory_space=pl.ANY)
    slots = shape((micros, experts, padded, model_width), bf16)
    chunks = half // 2 // 256
    quarter = model_width // 4
    spots = (micros, 2, experts, padded, model_width)
    return pl.pallas_call(
        functools.partial(expert_kernel, chips, experts),
        out_shape=[
            slots,
            slots,
            shape((2, quarter, half), f32),
            shape((2, quarter, half), bf16),
            shape((chunks, 256, model_width), f32),
        ],
        in_specs=[hbm] * 5,
        out_specs=[hbm] * 5,
        scratch_shapes=[
            pltpu.VMEM((micros * rows, model_width), bf16),
            pltpu.VMEM((micros * rows, model_width), bf16),
            pltpu.VMEM((model_width, half), bf16),
            pltpu.VMEM((half, model_width), bf16),
            pltpu.VMEM((model_width, 128), bf16),
            pltpu.VMEM((micros * rows, half), bf16),
            pltpu.VMEM((micros * rows, half), bf16),
            pltpu.VMEM((micros, 2, rows // 2, model_width), f32),
            pltpu.VMEM(spots, bf16),
            pltpu.VMEM(spots, bf16),
            pltpu.VMEM((chunks, 256, model_width), bf16),
            pltpu.VMEM((chunks, 256, model_width), bf16),
            pltpu.VMEM((2, 256, model_width), f32),
            pltpu.VMEM((quarter, half), bf16),
            pltpu.VMEM((quarter, half), f32),
            DMA((7,)),
            DMA((micros, 2)),
            DMA((micros, 2)),
            DMA((micros, 2, experts)),
            DMA((micros, 2, experts)),
            DMA((micros, 2)),
            DMA((chunks,)),
            DMA((chunks,)),
            DMA((4,)),
        ],
        compiler_params=pltpu.CompilerParams(
            collective_id=3, has_side_effects=True, vmem_limit_bytes=63 * 2**20
        ),
        name="run_experts",
    )(
        got_h.reshape(micros, rows, model_width),
        got_g.reshape(micros, rows, model_width),
        w_in,
        w_out,
        full,
    )


def end_kernel(
    chips,
    experts,
    cut,
    segments,
    routes,
    gains,
    lse,
    probs,
    tokens,
    cotangent,
    qkv_hbm,
    y1_hbm,
    returned_hbm,
    back_hbm,
    attn_hbm,
    mixed_hbm,
    hidden_hbm,
    full_hbm,
    send_in,
    keep_in,
    grad_qkv,
    grad_out,
    grad_small,
    output,
    grad_x,
    grad_in,
    full,
    x_buf,
    g_buf,
    qkv,
    y1_buf,
    returned,
    back,
    attn_in,
    mixed,
    hidden,
    out_buf,
    gx_buf,
    branch,
    gqkv,
    glog_buf,
    go_buf,
    gain_rows,
    grads,
    crecv,
    xrecv,
    yrecv,
    part_z,
    zrecv,
    got_in,
    got_y,
    keep,
    load,
    load_m,
    put,
    si,
    ri,
    siy,
    riy,
    sc,
    rc,
    sx,
    rx,
    sy,
    ry,
    sz,
    rz,
):
    block, chip, core, peer_x, peer_y, peer_core, peers_z = place_of(chips)
    micros, seq_len, model_width = tokens.shape
    width = full.shape[1]
    wide = width - cut
    row_y = block // 2
    opposite = flip(core, 1)
    wide_qkv = 3 * model_width

    late = pl.ds(wide_qkv, width - wide_qkv)
    early = pl.ds(0, wide_qkv)
    once = [
        (full_hbm.at[:, late], full.at[:, late]),
        (full_hbm.at[:, early], full.at[:, early]),
        (keep_in.at[1 - row_y], keep.at[0]),
        (keep_in.at[row_y], keep.at[1]),
        (attn_hbm, attn_in),
        (mixed_hbm, mixed),
        (hidden_hbm, hidden),
    ]
    once = [pltpu.make_async_copy(src, dst, load.at[i]) for i, (src, dst) in enumerate(once)]
    pairs = (
        (returned_hbm, returned),
        (back_hbm, back),
        (cotangent, g_buf),
        (y1_hbm, y1_buf),
        (qkv_hbm, qkv),
        (tokens, x_buf),
    )

    def load_of(i, m):
        src, dst = pairs[i]
        return pltpu.make_async_copy(src.at[m], dst.at[m], load_m.at[i, m])

    once[0].start()
    for i in range(len(pairs)):
        load_of(i, 0).start()
    once[1].start()
    for i in range(len(pairs)):
        load_of(i, 1).start()
    for copy in once[2:]:
        copy.start()

    greet([peer_x, peer_y, peer_core] + peers_z[1:])

    def in_x(j):
        return pltpu.make_async_remote_copy(
            src_ref=send_in.at[1 - row_y if j == 0 else row_y],
            dst_ref=got_in.at[j],
            send_sem=si.at[j],
            recv_sem=ri.at[j],
            device_id=peer_x,
            device_id_type=MESH,
        )

    in_y = pltpu.make_async_remote_copy(
        src_ref=got_in.at[0],
        dst_ref=got_y,
        send_sem=siy,
        recv_sem=riy,
        device_id=peer_y,
        device_id_type=MESH,
    )
    in_x(0).start()
    in_x(1).start()
    strip = 32

    def pass_in_y():
        once[2].wait()
        in_x(0).wait()

        @pl.loop(0, keep.shape[1] // strip)
        def _(j):
            at = pl.ds(pl.multiple_of(j * strip, strip), strip)
            got_in[0, at, :] = (keep[0, at, :] + got_in[0, at, :].astype(f32)).astype(bf16)

        in_y.start()

    def put_in(slot, side):
        half = keep.shape[2]
        cols = pl.ds(pl.multiple_of(side * half, half), half)
        copy = pltpu.make_async_copy(keep.at[slot], grad_in.at[:, cols], put.at[2, slot])
        copy.start()
        return copy

    def end_in():
        once[3].wait()
        in_x(1).wait()

        @pl.loop(0, keep.shape[1] // strip)
        def _(j):
            at = pl.ds(pl.multiple_of(j * strip, strip), strip)
            keep[1, at, :] = keep[1, at, :] + got_in[1, at, :].astype(f32)

        stored = [put_in(1, row_y)]
        in_y.wait()

        @pl.loop(0, keep.shape[1] // strip)
        def _(j):
            at = pl.ds(pl.multiple_of(j * strip, strip), strip)
            keep[0, at, :] = got_y[at, :].astype(f32)

        return stored + [put_in(0, 1 - row_y)]

    def put_out(m):
        return pltpu.make_async_copy(out_buf.at[m], output.at[m], put.at[0, m])

    def put_x(m):
        return pltpu.make_async_copy(gx_buf.at[m], grad_x.at[m], put.at[1, m])

    gain_rows[...] = jnp.zeros(gain_rows.shape, f32)
    scale = 1.0 / math.sqrt(model_width // HEADS)
    low_half = lanes_of((seq_len, 128)) < 64
    once[0].wait()

    @pl.loop(0, micros)
    def _(m):
        here = pl.ds(pl.multiple_of(m * seq_len, seq_len), seq_len)
        for i in range(4):
            load_of(i, m).wait()
        g = g_buf[m].astype(f32)
        route = column(routes[m])
        chosen = choose_slots(route, returned.shape[1], experts)
        moe = dot(chosen, returned[m])
        prob = probs[m]
        one_hot = one_hot_of(route)
        gate = jnp.sum(prob * one_hot, axis=1, keepdims=True)
        y1 = y1_buf[m]
        out_buf[m] = (y1 + gate * moe).astype(bf16)
        put_out(m).start()
        choice = one_hot * jnp.sum(g * moe, axis=1, keepdims=True)
        glog = (prob * (choice - jnp.sum(prob * choice, axis=1, keepdims=True))).astype(bf16)
        glog_buf[here, :] = glog
        grad_h = dot(chosen, back[m]) + dot_nt(glog, full[:, pl.ds(4 * model_width, 128)])
        n2, inv2 = normalize(y1)
        gain_rows[experts + 1 : experts + 2, :] += jnp.sum(grad_h * n2, axis=0, keepdims=True)
        gy1 = g + norm_back(grad_h * gains[1:2, :], n2, inv2)
        gx_buf[m] = gy1
        branch[here, :] = gy1.astype(bf16)
        go_buf[...] = dot_nt(branch[here, :], full[:, pl.ds(wide_qkv, model_width)]).astype(bf16)
        load_of(4, m).wait()
        load_of(5, m).wait()

        @pl.when(m == 1)
        def _():
            pass_in_y()

        allowed = allowed_pairs(segments[m])

        @pl.loop(0, model_width // 128)
        def _(pair):
            at = pl.multiple_of(pair * 128, 128)
            query = qkv[m, :, pl.ds(at, 128)]
            key = qkv[m, :, pl.ds(model_width + at, 128)]
            value = qkv[m, :, pl.ds(2 * model_width + at, 128)]
            grad_o = go_buf[:, pl.ds(at, 128)]
            parts = []
            for side in range(2):
                mine = low_half if side == 0 else jnp.logical_not(low_half)
                scores = dot_nt(jnp.where(mine, query, 0.0).astype(bf16), key) * scale
                head = lanes_of(lse.shape[1:]) == 2 * pair + side
                top = jnp.sum(jnp.where(head, lse[m], 0.0), axis=1, keepdims=True)
                p = jnp.exp(jnp.where(allowed, scores, masked_value) - top)
                gp = dot_nt(jnp.where(mine, grad_o, 0.0).astype(bf16), value)
                gs = (p * (gp - jnp.sum(p * gp, axis=1, keepdims=True))).astype(bf16)
                parts.append(
                    (dot(gs, key) * scale, dot_tn(gs, query) * scale, dot_tn(p.astype(bf16), grad_o))
                )
            for i in range(3):
                both = jnp.where(low_half, parts[0][i], parts[1][i]).astype(bf16)
                gqkv[here, pl.ds(i * model_width + at, 128)] = both

        @pl.when(m == 0)
        def _():
            once[1].wait()

        ga = dot_nt(gqkv[here, :], full[:, pl.ds(0, wide_qkv)])
        n1, inv1 = normalize(x_buf[m].astype(f32))
        gain_rows[experts : experts + 1, :] += jnp.sum(ga * n1, axis=0, keepdims=True)
        gx_buf[m] = gx_buf[m] + norm_back(ga * gains[0:1, :], n1, inv1)
        put_x(m).start()

    for copy in once[4:]:
        copy.wait()
    rows = grads.shape[3]
    span = model_width // 4

    def to_core(b):
        return pltpu.make_async_remote_copy(
            src_ref=grads.at[b, :, opposite],
            dst_ref=crecv.at[b],
            send_sem=sc.at[b],
            recv_sem=rc.at[b],
            device_id=peer_core,
            device_id_type=MESH,
        )

    @pl.loop(0, 4)
    def _(b):
        cols = pl.ds(pl.multiple_of(b * span, span), span)

        def store(start, value):
            value = value.reshape(chips, 2, rows, value.shape[1]).astype(bf16)
            grads[b, :, :, :, pl.ds(start, value.shape[3])] = value

        @pl.loop(0, wide_qkv // 512)
        def _(j):
            start = pl.multiple_of(j * 512, 512)
            store(start, dot_tn(attn_in[:, cols], gqkv[:, pl.ds(start, 512)]))

        store(wide_qkv, dot_tn(mixed[:, cols], branch[...]))
        small = dot_tn(hidden[:, cols], glog_buf[...]) + jnp.transpose(gain_rows[:, cols])
        store(4 * model_width, small)
        to_core(b).start()

    left, right = pl.ds(0, cut), pl.ds(cut, wide)
    order = list(range(chips - 1, -1, -1))
    along_x, along_y, along_z = {}, {}, {}

    def spot(k, origin, cols):
        return (flip(block, origin), flip(chip, k), core, slice(None), cols)

    def begin(k):
        step = flip(chip, k)
        for origin in (3, 1, 2, 0):
            b = flip(block, origin)
            at = (b, step, core)
            grads[at] = (grads[at].astype(f32) + crecv[b, step].astype(f32)).astype(bf16)
            if origin == 3:
                along_x[k, 0] = send(
                    grads.at[spot(k, 3, left)], xrecv.at[k, 0, :, left], sx.at[k, 0], rx.at[k, 0], peer_x
                )
                along_y[k, 0] = send(
                    grads.at[spot(k, 3, right)], yrecv.at[k, 0, :, pl.ds(0, wide)], sy.at[k, 0], ry.at[k, 0], peer_y
                )
            if origin == 1:
                along_x[k, 1] = send(
                    grads.at[spot(k, 1, left)], xrecv.at[k, 1, :, left], sx.at[k, 1], rx.at[k, 1], peer_x
                )
            if origin == 2:
                along_y[k, 1] = send(
                    grads.at[spot(k, 2, right)], yrecv.at[k, 1, :, pl.ds(0, wide)], sy.at[k, 1], ry.at[k, 1], peer_y
                )

    def relay(k):
        along_x[k, 0].wait_recv()
        at = spot(k, 2, left)
        grads[at] = (grads[at].astype(f32) + xrecv[k, 0, :, left].astype(f32)).astype(bf16)
        along_y[k, 2] = send(grads.at[at], yrecv.at[k, 2, :, left], sy.at[k, 2], ry.at[k, 2], peer_y)
        along_y[k, 0].wait_recv()
        at = spot(k, 1, right)
        grads[at] = (grads[at].astype(f32) + yrecv[k, 0, :, pl.ds(0, wide)].astype(f32)).astype(bf16)
        along_x[k, 2] = send(
            grads.at[at], xrecv.at[k, 2, :, pl.ds(0, wide)], sx.at[k, 2], rx.at[k, 2], peer_x
        )

    def finish(k):
        for turn in (1, 2):
            along_x[k, turn].wait_recv()
            along_y[k, turn].wait_recv()
        lhs = (
            grads[spot(k, 0, left)].astype(f32)
            + xrecv[k, 1, :, left].astype(f32)
            + yrecv[k, 2, :, left].astype(f32)
        )
        rhs = (
            grads[spot(k, 0, right)].astype(f32)
            + yrecv[k, 1, :, pl.ds(0, wide)].astype(f32)
            + xrecv[k, 2, :, pl.ds(0, wide)].astype(f32)
        )
        if k:
            part_z[k, :, left] = lhs.astype(bf16)
            part_z[k, :, right] = rhs.astype(bf16)
            along_z[k] = send(part_z.at[k], zrecv.at[k], sz.at[k], rz.at[k], peers_z[k])
        else:
            for j in range(1, chips):
                along_z[j].wait_recv()
                lhs = lhs + zrecv[j, :, left].astype(f32)
                rhs = rhs + zrecv[j, :, right].astype(f32)
            start = 0
            for out in (grad_qkv, grad_out, grad_small):
                w = out.shape[1]
                for lo, hi, value in ((0, cut, lhs), (cut, width, rhs)):
                    a, b = max(start, lo), min(start + w, hi)
                    if a < b:
                        out[:, a - start : b - start] = value[:, a - lo : b - lo]
                start += w

    @pl.loop(0, 4)
    def _(b):
        to_core(b).wait()

    stored = None
    for i in range(chips + 2):
        if i < chips:
            begin(order[i])
        if 0 <= i - 1 < chips:
            relay(order[i - 1])
        if i == chips:
            stored = end_in()
        if i - 2 >= 0:
            finish(order[i - 2])
    for k in order:
        for turn in range(3):
            along_x[k, turn].wait_send()
            along_y[k, turn].wait_send()
        if k:
            along_z[k].wait_send()
    for copy in stored:
        copy.wait()
    for m in range(micros):
        put_out(m).wait()
        put_x(m).wait()


def end_layer(small_inputs, big_inputs, chips):
    tokens, keep_in, full = big_inputs[0], big_inputs[-1], big_inputs[9]
    experts = 2 * chips
    micros, seq_len, model_width = tokens.shape
    spots = big_inputs[4].shape[1]
    width = full.shape[1]
    rows = model_width // (8 * chips)
    cut = (width // 128 + 1) // 2 * 128
    quarter, half = keep_in.shape[1:]
    every = micros * seq_len
    shape = jax.ShapeDtypeStruct
    vmem, hbm = pl.BlockSpec(memory_space=pltpu.VMEM), pl.BlockSpec(memory_space=pl.ANY)
    tall = (micros, seq_len, model_width)
    return pl.pallas_call(
        functools.partial(end_kernel, chips, experts, cut),
        out_shape=[
            shape((rows, 3 * model_width), f32),
            shape((rows, model_width), f32),
            shape((rows, 128), f32),
            shape(tall, bf16),
            shape(tall, f32),
            shape((quarter, 2 * half), f32),
        ],
        in_specs=[vmem] * len(small_inputs) + [hbm] * len(big_inputs),
        out_specs=[vmem] * 3 + [hbm] * 3,
        scratch_shapes=[
            pltpu.VMEM((model_width, width), bf16),
            pltpu.VMEM(tall, bf16),
            pltpu.VMEM(tall, bf16),
            pltpu.VMEM((micros, seq_len, 3 * model_width), bf16),
            pltpu.VMEM(tall, f32),
            pltpu.VMEM((micros, spots, model_width), bf16),
            pltpu.VMEM((micros, spots, model_width), bf16),
            pltpu.VMEM((every, model_width), bf16),
            pltpu.VMEM((every, model_width), bf16),
            pltpu.VMEM((every, model_width), bf16),
            pltpu.VMEM(tall, bf16),
            pltpu.VMEM(tall, f32),
            pltpu.VMEM((every, model_width), bf16),
            pltpu.VMEM((every, 3 * model_width), bf16),
            pltpu.VMEM((every, 128), bf16),
            pltpu.VMEM((seq_len, model_width), bf16),
            pltpu.VMEM((128, model_width), f32),
            pltpu.VMEM((4, chips, 2, rows, width), bf16),
            pltpu.VMEM((4, chips, rows, width), bf16),
            pltpu.VMEM((chips, 3, rows, cut), bf16),
            pltpu.VMEM((chips, 3, rows, cut), bf16),
            pltpu.VMEM((chips, rows, width), bf16),
            pltpu.VMEM((chips, rows, width), bf16),
            pltpu.VMEM((2, quarter, half), bf16),
            pltpu.VMEM((quarter, half), bf16),
            pltpu.VMEM((2, quarter, half), f32),
            DMA((7,)),
            DMA((6, micros)),
            DMA((3, micros)),
            DMA((2,)),
            DMA((2,)),
            DMA(()),
            DMA(()),
            DMA((4,)),
            DMA((4,)),
            DMA((chips, 3)),
            DMA((chips, 3)),
            DMA((chips, 3)),
            DMA((chips, 3)),
            DMA((chips,)),
            DMA((chips,)),
        ],
        compiler_params=pltpu.CompilerParams(
            collective_id=2, has_side_effects=True, vmem_limit_bytes=63 * 2**20
        ),
        name="end_layer",
    )(*small_inputs, *big_inputs)


def on_device(
    tokens,
    segment_ids,
    routes,
    cotangent,
    w_qkv,
    w_attn_out,
    w_router,
    gain_attn,
    gain_moe,
    w_expert_in,
    w_expert_out,
):
    micro_count, _, seq_len, model_width = tokens.shape
    experts = w_router.shape[1]
    chips = model_width // w_qkv.shape[0] // 8

    spare = jnp.zeros((w_qkv.shape[0], 128 - 2 - experts), bf16)
    small = jnp.concatenate([w_router, gain_attn[:, None], gain_moe[:, None], spare], axis=1)
    tokens, cotangent, segment_ids = tokens[:, 0], cotangent[:, 0], segment_ids
    routes = routes.reshape(micro_count, 1, seq_len)
    attn_in, qkv, lse, mixed, residual, hidden, probs, gains, gathered, w_in, w_out, got_g, got_h = (
        begin_layer(
            tokens,
            segment_ids,
            routes,
            cotangent,
            (w_qkv, w_attn_out, small),
            w_expert_in[0],
            w_expert_out[0],
            chips,
        )
    )
    returned, grad_back, keep_in, send_in, grad_out = run_experts(
        got_h,
        got_g,
        w_in.reshape(model_width, -1),
        w_out.reshape(-1, model_width),
        gathered,
        chips,
    )
    flat = (micro_count, -1, model_width)
    grad_qkv, grad_attn_out, small_sum, output, grad_tokens, grad_in = end_layer(
        (segment_ids, routes, gains, lse, probs),
        (
            tokens,
            cotangent,
            qkv,
            residual,
            returned.reshape(flat),
            grad_back.reshape(flat),
            attn_in.reshape(-1, model_width),
            mixed.reshape(-1, model_width),
            hidden.reshape(-1, model_width),
            gathered,
            send_in,
            keep_in,
        ),
        chips,
    )
    return (
        output[:, None],
        grad_tokens[:, None],
        grad_qkv,
        grad_attn_out,
        small_sum[:, :experts],
        small_sum[:, experts],
        small_sum[:, experts + 1],
        grad_in[None],
        grad_out.reshape(1, -1, model_width),
    )


def solution(mesh):
    rows = P(("dp", "expert"))
    seqs = P(None, ("dp", "expert"))
    owned = P("expert", "dp", None)
    return jax.shard_map(
        on_device,
        mesh=mesh,
        in_specs=(seqs, seqs, seqs, seqs, rows, rows, rows, rows, rows, owned, owned),
        out_specs=(seqs, seqs, rows, rows, rows, rows, rows, owned, owned),
        check_vma=False,
    )
```

```python
import functools
import math

import jax
import jax.numpy as jnp
from jax import lax
from jax.experimental import pallas as pl
from jax.experimental.pallas import tpu as pltpu
from jax.sharding import PartitionSpec as P

HEADS = 16
epsilon = 1e-05
masked_value = -1e30
pieces = 8
f32 = jnp.float32
bf16 = jnp.bfloat16

MESH = pl.DeviceIdType.MESH
DMA = pltpu.SemaphoreType.DMA


def flip(index, mask):
    bit = 1
    while bit <= mask:
        if mask & bit:
            index = index + bit - 2 * bit * ((index // bit) % 2)
        bit *= 2
    return index


def place_of(chips):
    block = lax.axis_index("dp")
    owner = lax.axis_index("expert")
    peer_x = {"dp": flip(block, 1)}
    peer_y = {"dp": flip(block, 2)}
    peer_core = {"expert": flip(owner, 1)}
    peers_z = [{"expert": flip(owner, 2 * k)} for k in range(chips)]
    return block, owner // 2, owner % 2, peer_x, peer_y, peer_core, peers_z


def greet(peers):
    barrier = pltpu.get_barrier_semaphore()
    for peer in peers:
        pl.semaphore_signal(barrier, inc=1, device_id=peer, device_id_type=MESH)
    pl.semaphore_wait(barrier, len(peers))


def send(src, dst, send_sem, recv_sem, peer):
    copy = pltpu.make_async_remote_copy(
        src_ref=src, dst_ref=dst, send_sem=send_sem, recv_sem=recv_sem,
        device_id=peer, device_id_type=MESH,
    )
    copy.start()
    return copy


def normalize(values):
    row_mean = jnp.mean(values, axis=-1, keepdims=True)
    centered = values - row_mean
    inv_scale = lax.rsqrt(jnp.mean(centered * centered, axis=-1, keepdims=True) + epsilon)
    return (centered * inv_scale, inv_scale)


def norm_back(grad_normed, normed, inv_scale):
    return inv_scale * (
        grad_normed
        - jnp.mean(grad_normed, axis=-1, keepdims=True)
        - normed * jnp.mean(grad_normed * normed, axis=-1, keepdims=True)
    )


def dot(a, b):
    return jnp.dot(a, b, preferred_element_type=f32)


def dot_nt(a, b):
    return lax.dot_general(a, b, (((1,), (1,)), ((), ())), preferred_element_type=f32)


def dot_tn(a, b):
    return lax.dot_general(a, b, (((0,), (0,)), ((), ())), preferred_element_type=f32)


def lanes_of(shape):
    return lax.broadcasted_iota(jnp.int32, shape, 1)


def rows_of(shape):
    return lax.broadcasted_iota(jnp.int32, shape, 0)


def column(row):
    return jnp.transpose(jnp.broadcast_to(row.astype(f32), (128, row.shape[1])))[:, :1]


def one_hot_of(route):
    return jnp.where(lanes_of((route.shape[0], 128)).astype(f32) == route, 1.0, 0.0)


def choose_slots(route, spots, experts):
    seq_len = route.shape[0]
    capacity = (9 * seq_len + 8 * experts - 1) // (8 * experts)
    one_hot = one_hot_of(route)
    square = (seq_len, seq_len)
    before = jnp.where(lanes_of(square) < rows_of(square), 1.0, 0.0).astype(bf16)
    place = jnp.sum(dot(before, one_hot.astype(bf16)) * one_hot, axis=1, keepdims=True)
    slot = jnp.where(place < capacity, route * (spots // experts) + place, -1.0)
    return jnp.where(lanes_of((seq_len, spots)).astype(f32) == slot, 1.0, 0.0).astype(bf16)


def allowed_pairs(segment_row):
    square = (segment_row.shape[1],) * 2
    same = column(segment_row) == segment_row.astype(f32)
    return (lanes_of(square) <= rows_of(square)) & same


def begin_kernel(
    chips,
    experts,
    tokens,
    segments,
    routes,
    cotangent,
    shard_qkv,
    shard_out,
    shard_small,
    w_in,
    w_out,
    attn_in,
    qkv,
    lse,
    mixed,
    residual,
    hidden,
    probs,
    gains,
    kept_full,
    full_in,
    full_out,
    got_g,
    got_h,
    full,
    slots_g,
    slots_h,
    hold_in,
    hold_out,
    own_sem,
    sz,
    rz,
    sx,
    rx,
    sy,
    ry,
    sc,
    rc,
    sw,
    rw,
    lw,
    sd,
    rd,
    se,
    re,
    ld,
):
    block, chip, core, peer_x, peer_y, peer_core, peers_z = place_of(chips)
    owner = lax.axis_index("expert")
    micros, seq_len, model_width = tokens.shape
    rows = shard_qkv.shape[0]
    width = full.shape[1]
    cut = (width // 128 + 1) // 2 * 128
    halves = (pl.ds(0, cut), pl.ds(cut, width - cut))
    every = pl.ds(0, width)
    half = w_in.shape[1] // 2
    row_y, row_x = block // 2, block % 2

    def part(origin, step, columns):
        start = ((flip(block, origin) * chips + flip(chip, step)) * 2 + core) * rows
        return full.at[pl.ds(pl.multiple_of(start, rows), rows), columns]

    own_copies = []
    for i, (src, at) in enumerate(
        ((shard_qkv, 0), (shard_out, 3 * model_width), (shard_small, 4 * model_width))
    ):
        dst = part(0, 0, pl.ds(at, src.shape[1]))
        own_copies.append(pltpu.make_async_copy(src, dst, own_sem.at[i]))
        own_copies[-1].start()
    others = [{"expert": lax.rem(owner + k, experts)} for k in range(1, experts)]
    greet([peer_x, peer_y] + others)
    for copy in own_copies:
        copy.wait()

    mine = part(0, 0, every)
    along_z = [None] + [send(mine, mine, sz.at[k], rz.at[k], peers_z[k]) for k in range(1, chips)]
    along_x = [[None] * 3 for _ in range(chips)]
    along_y = [[None] * 3 for _ in range(chips)]
    across = [[None] * 4 for _ in range(chips)]

    def to_core(k, origin):
        piece = part(origin, k, every)
        across[k][origin] = send(
            piece, piece, sc.at[k, origin], rc.at[k, origin], peer_core
        )

    def pass_on(k):
        along_x[k][1].wait_recv()
        to_core(k, 1)
        along_y[k][1].wait_recv()
        to_core(k, 2)
        along_x[k][2].wait_recv()
        along_y[k][2].wait_recv()
        to_core(k, 3)

    def spread(k):
        for turn in range(2):
            for copies, s, r, peer, side in (
                (along_x, sx, rx, peer_x, turn),
                (along_y, sy, ry, peer_y, 1 - turn),
            ):
                piece = part(0, k, halves[side])
                copies[k][turn] = send(piece, piece, s.at[k, turn], r.at[k, turn], peer)
        to_core(k, 0)

    def turn_corner(k):
        along_x[k][0].wait_recv()
        piece = part(1, k, halves[0])
        along_y[k][2] = send(piece, piece, sy.at[k, 2], ry.at[k, 2], peer_y)
        along_y[k][0].wait_recv()
        piece = part(2, k, halves[1])
        along_x[k][2] = send(piece, piece, sx.at[k, 2], rx.at[k, 2], peer_x)

    piece_rows = w_out.shape[0] // pieces
    out_x = []

    def send_piece():
        j = len(out_x)
        at = pl.ds(j * piece_rows, piece_rows)
        out_x.append(
            send(w_out.at[at], full_out.at[row_x, at], sw.at[3 + j], rw.at[3 + j], peer_x)
        )

    from_y = []

    def send_strip():
        j = len(from_y)
        size = w_in.shape[0] // pieces
        at = pl.ds(j * size, size)
        from_y.append(
            send(
                w_in.at[at, pl.ds((1 - row_y) * half, half)],
                full_in.at[block, at],
                sw.at[3 + pieces + j], rw.at[3 + pieces + j], peer_y,
            )
        )

    spread(0)

    def put_slots(slots, m, values):
        packed = dot_tn(choose_slots(column(routes[m]), experts * slots.shape[2], experts), values)
        packed = packed.astype(bf16)
        for e in range(experts):
            size = slots.shape[2]
            slots[m, e] = packed[e * size : (e + 1) * size]

    for m in range(micros):
        put_slots(slots_g, m, cotangent[m])

    for k in range(chips):
        if k:
            along_z[k].wait_recv()
            spread(k)
            pass_on(k - 1)
        turn_corner(k)
        if k < pieces // 2:
            send_piece()
            send_strip()

    local_in = pltpu.make_async_copy(w_in.at[:, pl.ds(row_y * half, half)], hold_in, lw.at[0])
    local_out = pltpu.make_async_copy(w_out, hold_out, lw.at[1])
    local_in.start()
    local_out.start()
    while len(from_y) < pieces:
        send_strip()
    from_x = send(
        w_in.at[:, pl.ds(row_y * half, half)], full_in.at[block], sw.at[1], rw.at[1], peer_x
    )
    while len(out_x) < pieces:
        send_piece()

    def slot_copies(way, slots, got, m):
        def to_owner(k):
            peer = lax.rem(owner + k, experts)
            return pltpu.make_async_remote_copy(
                src_ref=slots.at[m, peer],
                dst_ref=got.at[m, 0, owner],
                send_sem=sd.at[way, m, k],
                recv_sem=rd.at[way, m, k],
                device_id={"expert": peer},
                device_id_type=MESH,
            )

        def to_y(k):
            origin = lax.rem(owner - k + experts, experts)
            return pltpu.make_async_remote_copy(
                src_ref=got.at[m, 0, origin],
                dst_ref=got.at[m, 1, origin],
                send_sem=se.at[way, m, k],
                recv_sem=re.at[way, m, k],
                device_id=peer_y,
                device_id_type=MESH,
            )

        own = pltpu.make_async_copy(slots.at[m, owner], got.at[m, 0, owner], ld.at[way, m])
        return to_owner, to_y, own

    def start_slots(way, slots, got, m):
        to_owner, to_y, own = slot_copies(way, slots, got, m)
        own.start()

        @pl.loop(1, experts)
        def _(k):
            to_owner(k).start()

    def relay_slots(way, slots, got, m):
        to_owner, to_y, own = slot_copies(way, slots, got, m)
        own.wait()
        to_y(0).start()

        @pl.loop(1, experts)
        def _(k):
            to_owner(k).wait_recv()
            to_y(k).start()

    def end_slots(way, slots, got, m):
        to_owner, to_y, own = slot_copies(way, slots, got, m)

        @pl.loop(1, experts)
        def _(k):
            to_owner(k).wait_send()

        @pl.loop(0, experts)
        def _(k):
            to_y(k).wait()

    for m in range(micros):
        start_slots(0, slots_g, got_g, m)
    pass_on(chips - 1)
    for k in range(chips):
        for origin in range(4):
            across[k][origin].wait_recv()
    keep = pltpu.make_async_copy(full, kept_full, own_sem.at[3])
    keep.start()
    small = jnp.transpose(full[:, pl.ds(4 * model_width, 128)].astype(f32))
    gains[...] = small[experts : experts + 2]
    local_in.wait()
    local_out.wait()
    store_in = pltpu.make_async_copy(hold_in, full_in.at[block], lw.at[0])
    store_out = pltpu.make_async_copy(hold_out, full_out.at[row_x], lw.at[1])
    store_in.start()
    store_out.start()

    scale = 1.0 / math.sqrt(model_width // HEADS)
    low_half = lanes_of((seq_len, 128)) < 64
    relay_slots(0, slots_g, got_g, 0)
    for m in range(micros):
        x = tokens[m].astype(f32)
        attn_in[m] = (normalize(x)[0] * gains[0:1, :]).astype(bf16)

        @pl.loop(0, 3 * model_width // 512)
        def _(j):
            at = pl.ds(pl.multiple_of(j * 512, 512), 512)
            qkv[m, :, at] = dot(attn_in[m], full[:, at]).astype(bf16)

        allowed = allowed_pairs(segments[m])
        lse[m] = jnp.zeros(lse.shape[1:], f32)

        @pl.loop(0, model_width // 128)
        def _(pair):
            at = pl.multiple_of(pair * 128, 128)
            query = qkv[m, :, pl.ds(at, 128)]
            key = qkv[m, :, pl.ds(model_width + at, 128)]
            value = qkv[m, :, pl.ds(2 * model_width + at, 128)]
            outs = []
            for side in range(2):
                here = low_half if side == 0 else jnp.logical_not(low_half)
                scores = dot_nt(jnp.where(here, query, 0.0).astype(bf16), key) * scale
                masked = jnp.where(allowed, scores, masked_value)
                top = jnp.max(masked, axis=1, keepdims=True)
                weight = jnp.exp(masked - top)
                norm = jnp.sum(weight, axis=1, keepdims=True)
                outs.append(dot((weight / norm).astype(bf16), value))
                head = lanes_of(lse.shape[1:]) == 2 * pair + side
                lse[m] = jnp.where(head, top + jnp.log(norm), lse[m])
            mixed[m, :, pl.ds(at, 128)] = jnp.where(low_half, outs[0], outs[1]).astype(bf16)

        y1 = x + dot(mixed[m], full[:, pl.ds(3 * model_width, model_width)])
        residual[m] = y1
        low = (normalize(y1)[0] * gains[1:2, :]).astype(bf16)
        hidden[m] = low
        put_slots(slots_h, m, low)
        start_slots(1, slots_h, got_h, m)
        logits = dot(low, full[:, pl.ds(4 * model_width, 128)])
        real = lanes_of(logits.shape) < experts
        logits = jnp.where(real, logits, masked_value)
        weight = jnp.where(real, jnp.exp(logits - jnp.max(logits, axis=1, keepdims=True)), 0.0)
        probs[m] = weight / jnp.sum(weight, axis=1, keepdims=True)
        if m + 1 < micros:
            relay_slots(0, slots_g, got_g, m + 1)
        if m:
            relay_slots(1, slots_h, got_h, m - 1)
    for copy in from_y:
        copy.wait_recv()
    piece = full_in.at[flip(block, 2)]
    diagonal = send(piece, piece, sw.at[2], rw.at[2], peer_x)
    relay_slots(1, slots_h, got_h, micros - 1)

    for m in range(micros):
        end_slots(0, slots_g, got_g, m)
        end_slots(1, slots_h, got_h, m)
    keep.wait()
    store_in.wait()
    store_out.wait()
    for copy in from_y:
        copy.wait_send()
    for copy in (from_x, diagonal, *out_x):
        copy.wait()
    for k in range(chips):
        if k:
            along_z[k].wait_send()
        for turn in range(3):
            along_x[k][turn].wait_send()
            along_y[k][turn].wait_send()
        for origin in range(4):
            across[k][origin].wait_send()


def begin_layer(tokens, segments, routes, cotangent, shards, w_in, w_out, chips):
    experts = 2 * chips
    micros, seq_len, model_width = tokens.shape
    capacity = (9 * seq_len + 8 * experts - 1) // (8 * experts)
    padded = (capacity + 7) // 8 * 8
    width = 4 * model_width + 128
    rows, half = w_in.shape[0], w_in.shape[1] // 2
    shape = jax.ShapeDtypeStruct
    vmem, hbm = pl.BlockSpec(memory_space=pltpu.VMEM), pl.BlockSpec(memory_space=pl.ANY)
    spots = (micros, experts, padded, model_width)
    return pl.pallas_call(
        functools.partial(begin_kernel, chips, experts),
        out_shape=[
            shape((micros, seq_len, model_width), bf16),
            shape((micros, seq_len, 3 * model_width), bf16),
            shape((micros, seq_len, 128), f32),
            shape((micros, seq_len, model_width), bf16),
            shape((micros, seq_len, model_width), f32),
            shape((micros, seq_len, model_width), bf16),
            shape((micros, seq_len, 128), f32),
            shape((2, model_width), f32),
            shape((model_width, width), bf16),
            shape((4, rows, half), bf16),
            shape((2,) + w_out.shape, bf16),
            shape((micros, 2, experts, padded, model_width), bf16),
            shape((micros, 2, experts, padded, model_width), bf16),
        ],
        in_specs=[vmem] * 4 + [hbm] * 5,
        out_specs=[vmem] * 8 + [hbm] * 5,
        scratch_shapes=[
            pltpu.VMEM((model_width, width), bf16),
            pltpu.VMEM(spots, bf16),
            pltpu.VMEM(spots, bf16),
            pltpu.VMEM((rows, half), bf16),
            pltpu.VMEM(w_out.shape, bf16),
            DMA((4,)),
            DMA((chips,)),
            DMA((chips,)),
            DMA((chips, 3)),
            DMA((chips, 3)),
            DMA((chips, 3)),
            DMA((chips, 3)),
            DMA((chips, 4)),
            DMA((chips, 4)),
            DMA((3 + 2 * pieces,)),
            DMA((3 + 2 * pieces,)),
            DMA((2,)),
            DMA((2, micros, experts)),
            DMA((2, micros, experts)),
            DMA((2, micros, experts)),
            DMA((2, micros, experts)),
            DMA((2, micros)),
        ],
        compiler_params=pltpu.CompilerParams(
            collective_id=1, has_side_effects=True, vmem_limit_bytes=60 * 2**20
        ),
        name="begin_layer",
    )(tokens, segments, routes, cotangent, *shards, w_in, w_out)


def expert_kernel(
    chips,
    experts,
    got_h,
    got_g,
    w_in_hbm,
    w_out_hbm,
    full,
    returned,
    grad_back,
    keep_in,
    send_in,
    grad_out,
    x_buf,
    gz_buf,
    w_in,
    w_out,
    router,
    act,
    gu,
    own,
    part,
    part_got,
    out_part,
    out_got,
    out_stage,
    in_part,
    in_stage,
    load,
    sy,
    ry,
    sz,
    rz,
    lz,
    sx,
    rx,
    st,
):
    block, chip, core, peer_x, peer_y, peer_core, peers_z = place_of(chips)
    owner = lax.axis_index("expert")
    micros, rows, model_width = got_h.shape
    half = w_in.shape[1]
    mine = rows // 2
    padded = part.shape[3]
    row_x = block % 2
    step = 256
    backs = (returned, grad_back)

    sources = [
        (got_h.at[0], x_buf.at[pl.ds(0, rows)]),
        (w_in_hbm, w_in),
        (w_out_hbm, w_out),
        (full.at[:, pl.ds(4 * model_width, 128)], router),
        (got_g.at[0], gz_buf.at[pl.ds(0, rows)]),
        (got_h.at[1], x_buf.at[pl.ds(rows, rows)]),
        (got_g.at[1], gz_buf.at[pl.ds(rows, rows)]),
    ]
    loads = []
    for i, (src, dst) in enumerate(sources):
        loads.append(pltpu.make_async_copy(src, dst, load.at[i]))
        loads[-1].start()
    greet(
        [peer_x, peer_y]
        + [{"expert": lax.rem(owner + k, experts)} for k in range(1, experts)]
    )

    def of(m):
        return pl.ds(m * rows, rows)

    def gate_rows(m):
        logits = dot(x_buf[of(m), :], router[...])
        lanes = lanes_of(logits.shape)
        logits = jnp.where(lanes < experts, logits, masked_value)
        weight = jnp.exp(logits - jnp.max(logits, axis=1, keepdims=True))
        weight = jnp.where(lanes < experts, weight, 0.0)
        picked = jnp.sum(jnp.where(lanes == owner, weight, 0.0), axis=1, keepdims=True)
        gate = picked / jnp.sum(weight, axis=1, keepdims=True)
        gz_buf[of(m), :] = (gate * gz_buf[of(m), :].astype(f32)).astype(bf16)

    def open_rows(m, forward, backward):
        @pl.loop(0, half // step)
        def _(j):
            at = pl.ds(pl.multiple_of(j * step, step), step)
            u = dot(x_buf[of(m), :], w_in[:, at])
            root = math.sqrt(2.0 / math.pi)
            square = u * u
            bend = jnp.tanh(root * (u + 0.044715 * (u * square)))
            if forward:
                act[of(m), at] = (0.5 * u * (1.0 + bend)).astype(bf16)
            if backward:
                back = dot_nt(gz_buf[of(m), :], w_out[at, :])
                slope = 0.5 * (1.0 + bend) + 0.5 * u * (1.0 - bend * bend) * (
                    root * (1.0 + (3.0 * 0.044715) * square)
                )
                gu[of(m), at] = (back * slope).astype(bf16)

    wing = model_width // 2

    def columns(side):
        return pl.ds(pl.multiple_of(side * wing, wing), wing)

    def swap(m, way, side):
        return pltpu.make_async_remote_copy(
            src_ref=part.at[m, way, :, :, columns(side)],
            dst_ref=part_got.at[m, way, :, :, columns(side)],
            send_sem=sy.at[m, way, side],
            recv_sem=ry.at[m, way, side],
            device_id=peer_y,
            device_id_type=MESH,
        )

    def close_rows(m, way):
        @pl.loop(0, 2)
        def _(side):
            @pl.loop(0, wing // step)
            def _(j):
                at = pl.ds(pl.multiple_of(side * wing + j * step, step), step)
                if way == 0:
                    total = dot(act[of(m), :], w_out[:, at])
                else:
                    total = dot_nt(gu[of(m), :], w_in[at, :])
                own[m, way, :, at] = total[:mine]
                for e in range(experts):
                    start = mine + e * padded
                    part[m, way, e, :, at] = total[start : start + padded].astype(bf16)

            swap(m, way, side).start()

    def to_source(m, way, side, k):
        peer = lax.rem(owner + k, experts)
        return pltpu.make_async_remote_copy(
            src_ref=part.at[m, way, peer, :, columns(side)],
            dst_ref=backs[way].at[m, owner, :, columns(side)],
            send_sem=sz.at[m, way, side, k],
            recv_sem=rz.at[m, way, side, k],
            device_id={"expert": peer},
            device_id_type=MESH,
        )

    def to_self(m, way, side):
        return pltpu.make_async_copy(
            part.at[m, way, owner, :, columns(side)],
            backs[way].at[m, owner, :, columns(side)],
            lz.at[m, way, side],
        )

    def give_back(m, way, side):
        swap(m, way, side).wait()

        @pl.loop(0, experts)
        def _(e):
            at = pl.ds(pl.multiple_of(e * padded, padded), padded)
            cols = columns(side)
            total = own[m, way, at, cols] + part_got[m, way, e, :, cols].astype(f32)
            part[m, way, e, :, cols] = total.astype(bf16)

        to_self(m, way, side).start()

        @pl.loop(1, experts)
        def _(k):
            to_source(m, way, side, k).start()

    def end_back(m, way, side):
        to_self(m, way, side).wait()

        @pl.loop(1, experts)
        def _(k):
            to_source(m, way, side, k).wait()

    chunks = out_part.shape[0]

    def out_rows(side, j):
        start = side * (half // 2) + j * step
        return dot_tn(act[:, pl.ds(pl.multiple_of(start, step), step)], gz_buf[...])

    def to_x(j):
        return pltpu.make_async_remote_copy(
            src_ref=out_part.at[j],
            dst_ref=out_got.at[j],
            send_sem=sx.at[j],
            recv_sem=rx.at[j],
            device_id=peer_x,
            device_id_type=MESH,
        )

    def put_out(j, slot):
        return pltpu.make_async_copy(out_stage.at[slot], grad_out.at[j], st.at[slot])

    def send_out_rows():
        @pl.loop(0, chunks)
        def _(j):
            out_part[j] = out_rows(1 - row_x, j).astype(bf16)
            to_x(j).start()

    def keep_out_rows():
        for j in range(chunks):
            if j > 1:
                put_out(j - 2, j % 2).wait()
            to_x(j).wait()
            out_stage[j % 2] = out_rows(row_x, j) + out_got[j].astype(f32)
            put_out(j, j % 2).start()

    quarter = in_stage.shape[0]

    def in_rows(y, x):
        start = (2 * y + x) * quarter
        return pl.ds(pl.multiple_of(start, quarter), quarter)

    def in_copies(y):
        return (
            pltpu.make_async_copy(in_part, send_in.at[y], st.at[2]),
            pltpu.make_async_copy(in_stage, keep_in.at[y], st.at[3]),
        )

    def first_rows():
        for y in range(2):
            for kind in range(2):
                if y:
                    in_copies(0)[kind].wait()
                cols = in_rows(y, 1 - row_x if kind == 0 else row_x)

                @pl.loop(0, half // (2 * step))
                def _(j):
                    at = pl.ds(pl.multiple_of(j * 2 * step, 2 * step), 2 * step)
                    value = dot_tn(x_buf[:, cols], gu[:, at])
                    if kind == 0:
                        in_part[:, at] = value.astype(bf16)
                    else:
                        in_stage[:, at] = value

                in_copies(y)[kind].start()

    loads[0].wait()
    loads[1].wait()
    open_rows(0, True, False)
    loads[2].wait()
    close_rows(0, 0)
    loads[5].wait()
    open_rows(1, True, False)
    close_rows(1, 0)
    give_back(0, 0, 0)
    for i in (3, 4, 6):
        loads[i].wait()
    gate_rows(0)
    gate_rows(1)
    give_back(0, 0, 1)
    send_out_rows()
    give_back(1, 0, 0)
    open_rows(0, False, True)
    give_back(1, 0, 1)
    close_rows(0, 1)
    open_rows(1, False, True)
    give_back(0, 1, 0)
    close_rows(1, 1)
    give_back(0, 1, 1)
    first_rows()
    give_back(1, 1, 0)
    give_back(1, 1, 1)
    keep_out_rows()
    for j in range(chunks - 2, chunks):
        put_out(j, j % 2).wait()
    for copy in in_copies(1):
        copy.wait()
    for m in range(micros):
        for way in range(2):
            end_back(m, way, 0)
            end_back(m, way, 1)


def run_experts(got_h, got_g, w_in, w_out, full, chips):
    experts = 2 * chips
    micros, _, _, padded, model_width = got_h.shape
    rows = 2 * experts * padded
    half = w_in.shape[1]
    shape = jax.ShapeDtypeStruct
    hbm = pl.BlockSpec(memory_space=pl.ANY)
    slots = shape((micros, experts, padded, model_width), bf16)
    chunks = half // 2 // 256
    quarter = model_width // 4
    spots = (micros, 2, experts, padded, model_width)
    return pl.pallas_call(
        functools.partial(expert_kernel, chips, experts),
        out_shape=[
            slots,
            slots,
            shape((2, quarter, half), f32),
            shape((2, quarter, half), bf16),
            shape((chunks, 256, model_width), f32),
        ],
        in_specs=[hbm] * 5,
        out_specs=[hbm] * 5,
        scratch_shapes=[
            pltpu.VMEM((micros * rows, model_width), bf16),
            pltpu.VMEM((micros * rows, model_width), bf16),
            pltpu.VMEM((model_width, half), bf16),
            pltpu.VMEM((half, model_width), bf16),
            pltpu.VMEM((model_width, 128), bf16),
            pltpu.VMEM((micros * rows, half), bf16),
            pltpu.VMEM((micros * rows, half), bf16),
            pltpu.VMEM((micros, 2, rows // 2, model_width), f32),
            pltpu.VMEM(spots, bf16),
            pltpu.VMEM(spots, bf16),
            pltpu.VMEM((chunks, 256, model_width), bf16),
            pltpu.VMEM((chunks, 256, model_width), bf16),
            pltpu.VMEM((2, 256, model_width), f32),
            pltpu.VMEM((quarter, half), bf16),
            pltpu.VMEM((quarter, half), f32),
            DMA((7,)),
            DMA((micros, 2, 2)),
            DMA((micros, 2, 2)),
            DMA((micros, 2, 2, experts)),
            DMA((micros, 2, 2, experts)),
            DMA((micros, 2, 2)),
            DMA((chunks,)),
            DMA((chunks,)),
            DMA((4,)),
        ],
        compiler_params=pltpu.CompilerParams(
            collective_id=3, has_side_effects=True, vmem_limit_bytes=63 * 2**20
        ),
        name="run_experts",
    )(
        got_h.reshape(micros, rows, model_width),
        got_g.reshape(micros, rows, model_width),
        w_in,
        w_out,
        full,
    )


def end_kernel(
    chips,
    experts,
    cut,
    segments,
    routes,
    gains,
    lse,
    probs,
    tokens,
    cotangent,
    qkv_hbm,
    y1_hbm,
    returned_hbm,
    back_hbm,
    attn_hbm,
    mixed_hbm,
    hidden_hbm,
    full_hbm,
    send_in,
    keep_in,
    grad_qkv,
    grad_out,
    grad_small,
    output,
    grad_x,
    grad_in,
    full,
    x_buf,
    g_buf,
    qkv,
    y1_buf,
    returned,
    back,
    attn_in,
    mixed,
    hidden,
    out_buf,
    gx_buf,
    branch,
    gqkv,
    glog_buf,
    go_buf,
    gain_rows,
    grads,
    crecv,
    xrecv,
    yrecv,
    part_z,
    zrecv,
    got_in,
    got_y,
    keep,
    load,
    load_m,
    put,
    si,
    ri,
    siy,
    riy,
    sc,
    rc,
    sx,
    rx,
    sy,
    ry,
    sz,
    rz,
):
    block, chip, core, peer_x, peer_y, peer_core, peers_z = place_of(chips)
    micros, seq_len, model_width = tokens.shape
    width = full.shape[1]
    wide = width - cut
    row_y = block // 2
    opposite = flip(core, 1)
    wide_qkv = 3 * model_width

    late = pl.ds(wide_qkv, width - wide_qkv)
    early = pl.ds(0, wide_qkv)
    once = [
        (full_hbm.at[:, late], full.at[:, late]),
        (full_hbm.at[:, early], full.at[:, early]),
        (keep_in.at[1 - row_y], keep.at[0]),
        (keep_in.at[row_y], keep.at[1]),
        (attn_hbm, attn_in),
        (mixed_hbm, mixed),
        (hidden_hbm, hidden),
    ]
    once = [pltpu.make_async_copy(src, dst, load.at[i]) for i, (src, dst) in enumerate(once)]
    pairs = (
        (returned_hbm, returned),
        (back_hbm, back),
        (cotangent, g_buf),
        (y1_hbm, y1_buf),
        (qkv_hbm, qkv),
        (tokens, x_buf),
    )

    def load_of(i, m):
        src, dst = pairs[i]
        return pltpu.make_async_copy(src.at[m], dst.at[m], load_m.at[i, m])

    once[0].start()
    for i in range(len(pairs)):
        load_of(i, 0).start()
    once[1].start()
    for i in range(len(pairs)):
        load_of(i, 1).start()
    for copy in once[2:]:
        copy.start()

    greet([peer_x, peer_y, peer_core] + peers_z[1:])

    def in_x(j):
        return pltpu.make_async_remote_copy(
            src_ref=send_in.at[1 - row_y if j == 0 else row_y],
            dst_ref=got_in.at[j],
            send_sem=si.at[j],
            recv_sem=ri.at[j],
            device_id=peer_x,
            device_id_type=MESH,
        )

    in_y = pltpu.make_async_remote_copy(
        src_ref=got_in.at[0],
        dst_ref=got_y,
        send_sem=siy,
        recv_sem=riy,
        device_id=peer_y,
        device_id_type=MESH,
    )
    in_x(0).start()
    in_x(1).start()
    strip = 32

    def pass_in_y():
        once[2].wait()
        in_x(0).wait()

        @pl.loop(0, keep.shape[1] // strip)
        def _(j):
            at = pl.ds(pl.multiple_of(j * strip, strip), strip)
            got_in[0, at, :] = (keep[0, at, :] + got_in[0, at, :].astype(f32)).astype(bf16)

        in_y.start()

    def put_in(slot, side):
        half = keep.shape[2]
        cols = pl.ds(pl.multiple_of(side * half, half), half)
        copy = pltpu.make_async_copy(keep.at[slot], grad_in.at[:, cols], put.at[2, slot])
        copy.start()
        return copy

    def end_in():
        once[3].wait()
        in_x(1).wait()

        @pl.loop(0, keep.shape[1] // strip)
        def _(j):
            at = pl.ds(pl.multiple_of(j * strip, strip), strip)
            keep[1, at, :] = keep[1, at, :] + got_in[1, at, :].astype(f32)

        stored = [put_in(1, row_y)]
        in_y.wait()

        @pl.loop(0, keep.shape[1] // strip)
        def _(j):
            at = pl.ds(pl.multiple_of(j * strip, strip), strip)
            keep[0, at, :] = got_y[at, :].astype(f32)

        return stored + [put_in(0, 1 - row_y)]

    def put_out(m):
        return pltpu.make_async_copy(out_buf.at[m], output.at[m], put.at[0, m])

    def put_x(m):
        return pltpu.make_async_copy(gx_buf.at[m], grad_x.at[m], put.at[1, m])

    gain_rows[...] = jnp.zeros(gain_rows.shape, f32)
    scale = 1.0 / math.sqrt(model_width // HEADS)
    low_half = lanes_of((seq_len, 128)) < 64
    once[0].wait()

    @pl.loop(0, micros)
    def _(m):
        here = pl.ds(pl.multiple_of(m * seq_len, seq_len), seq_len)
        for i in range(4):
            load_of(i, m).wait()
        g = g_buf[m].astype(f32)
        route = column(routes[m])
        chosen = choose_slots(route, returned.shape[1], experts)
        moe = dot(chosen, returned[m])
        prob = probs[m]
        one_hot = one_hot_of(route)
        gate = jnp.sum(prob * one_hot, axis=1, keepdims=True)
        y1 = y1_buf[m]
        out_buf[m] = (y1 + gate * moe).astype(bf16)
        put_out(m).start()
        choice = one_hot * jnp.sum(g * moe, axis=1, keepdims=True)
        glog = (prob * (choice - jnp.sum(prob * choice, axis=1, keepdims=True))).astype(bf16)
        glog_buf[here, :] = glog
        grad_h = dot(chosen, back[m]) + dot_nt(glog, full[:, pl.ds(4 * model_width, 128)])
        n2, inv2 = normalize(y1)
        gain_rows[experts + 1 : experts + 2, :] += jnp.sum(grad_h * n2, axis=0, keepdims=True)
        gy1 = g + norm_back(grad_h * gains[1:2, :], n2, inv2)
        gx_buf[m] = gy1
        branch[here, :] = gy1.astype(bf16)
        go_buf[...] = dot_nt(branch[here, :], full[:, pl.ds(wide_qkv, model_width)]).astype(bf16)
        load_of(4, m).wait()
        load_of(5, m).wait()

        allowed = allowed_pairs(segments[m])

        @pl.loop(0, model_width // 128)
        def _(pair):
            @pl.when((m == 1) & (pair == 4))
            def _():
                pass_in_y()

            at = pl.multiple_of(pair * 128, 128)
            query = qkv[m, :, pl.ds(at, 128)]
            key = qkv[m, :, pl.ds(model_width + at, 128)]
            value = qkv[m, :, pl.ds(2 * model_width + at, 128)]
            grad_o = go_buf[:, pl.ds(at, 128)]
            parts = []
            for side in range(2):
                mine = low_half if side == 0 else jnp.logical_not(low_half)
                scores = dot_nt(jnp.where(mine, query, 0.0).astype(bf16), key) * scale
                head = lanes_of(lse.shape[1:]) == 2 * pair + side
                top = jnp.sum(jnp.where(head, lse[m], 0.0), axis=1, keepdims=True)
                p = jnp.exp(jnp.where(allowed, scores, masked_value) - top)
                gp = dot_nt(jnp.where(mine, grad_o, 0.0).astype(bf16), value)
                gs = (p * (gp - jnp.sum(p * gp, axis=1, keepdims=True))).astype(bf16)
                parts.append(
                    (dot(gs, key) * scale, dot_tn(gs, query) * scale, dot_tn(p.astype(bf16), grad_o))
                )
            for i in range(3):
                both = jnp.where(low_half, parts[0][i], parts[1][i]).astype(bf16)
                gqkv[here, pl.ds(i * model_width + at, 128)] = both

        @pl.when(m == 0)
        def _():
            once[1].wait()

        ga = dot_nt(gqkv[here, :], full[:, pl.ds(0, wide_qkv)])
        n1, inv1 = normalize(x_buf[m].astype(f32))
        gain_rows[experts : experts + 1, :] += jnp.sum(ga * n1, axis=0, keepdims=True)
        gx_buf[m] = gx_buf[m] + norm_back(ga * gains[0:1, :], n1, inv1)
        put_x(m).start()

    for copy in once[4:]:
        copy.wait()
    rows = grads.shape[3]
    span = model_width // 4

    def to_core(b):
        return pltpu.make_async_remote_copy(
            src_ref=grads.at[b, :, opposite],
            dst_ref=crecv.at[b],
            send_sem=sc.at[b],
            recv_sem=rc.at[b],
            device_id=peer_core,
            device_id_type=MESH,
        )

    @pl.loop(0, 4)
    def _(b):
        cols = pl.ds(pl.multiple_of(b * span, span), span)

        def store(start, value):
            value = value.reshape(chips, 2, rows, value.shape[1]).astype(bf16)
            grads[b, :, :, :, pl.ds(start, value.shape[3])] = value

        @pl.loop(0, wide_qkv // 512)
        def _(j):
            start = pl.multiple_of(j * 512, 512)
            store(start, dot_tn(attn_in[:, cols], gqkv[:, pl.ds(start, 512)]))

        store(wide_qkv, dot_tn(mixed[:, cols], branch[...]))
        small = dot_tn(hidden[:, cols], glog_buf[...]) + jnp.transpose(gain_rows[:, cols])
        store(4 * model_width, small)
        to_core(b).start()

    left, right = pl.ds(0, cut), pl.ds(cut, wide)
    order = list(range(chips - 1, -1, -1))
    along_x, along_y, along_z = {}, {}, {}

    def spot(k, origin, cols):
        return (flip(block, origin), flip(chip, k), core, slice(None), cols)

    def begin(k):
        step = flip(chip, k)
        for origin in (3, 1, 2, 0):
            b = flip(block, origin)
            at = (b, step, core)
            grads[at] = (grads[at].astype(f32) + crecv[b, step].astype(f32)).astype(bf16)
            if origin == 3:
                along_x[k, 0] = send(
                    grads.at[spot(k, 3, left)], xrecv.at[k, 0, :, left], sx.at[k, 0], rx.at[k, 0], peer_x
                )
                along_y[k, 0] = send(
                    grads.at[spot(k, 3, right)], yrecv.at[k, 0, :, pl.ds(0, wide)], sy.at[k, 0], ry.at[k, 0], peer_y
                )
            if origin == 1:
                along_x[k, 1] = send(
                    grads.at[spot(k, 1, left)], xrecv.at[k, 1, :, left], sx.at[k, 1], rx.at[k, 1], peer_x
                )
            if origin == 2:
                along_y[k, 1] = send(
                    grads.at[spot(k, 2, right)], yrecv.at[k, 1, :, pl.ds(0, wide)], sy.at[k, 1], ry.at[k, 1], peer_y
                )

    def relay(k):
        along_x[k, 0].wait_recv()
        at = spot(k, 2, left)
        grads[at] = (grads[at].astype(f32) + xrecv[k, 0, :, left].astype(f32)).astype(bf16)
        along_y[k, 2] = send(grads.at[at], yrecv.at[k, 2, :, left], sy.at[k, 2], ry.at[k, 2], peer_y)
        along_y[k, 0].wait_recv()
        at = spot(k, 1, right)
        grads[at] = (grads[at].astype(f32) + yrecv[k, 0, :, pl.ds(0, wide)].astype(f32)).astype(bf16)
        along_x[k, 2] = send(
            grads.at[at], xrecv.at[k, 2, :, pl.ds(0, wide)], sx.at[k, 2], rx.at[k, 2], peer_x
        )

    def finish(k):
        for turn in (1, 2):
            along_x[k, turn].wait_recv()
            along_y[k, turn].wait_recv()
        lhs = (
            grads[spot(k, 0, left)].astype(f32)
            + xrecv[k, 1, :, left].astype(f32)
            + yrecv[k, 2, :, left].astype(f32)
        )
        rhs = (
            grads[spot(k, 0, right)].astype(f32)
            + yrecv[k, 1, :, pl.ds(0, wide)].astype(f32)
            + xrecv[k, 2, :, pl.ds(0, wide)].astype(f32)
        )
        if k:
            part_z[k, :, left] = lhs.astype(bf16)
            part_z[k, :, right] = rhs.astype(bf16)
            along_z[k] = send(part_z.at[k], zrecv.at[k], sz.at[k], rz.at[k], peers_z[k])
        else:
            for j in range(1, chips):
                along_z[j].wait_recv()
                lhs = lhs + zrecv[j, :, left].astype(f32)
                rhs = rhs + zrecv[j, :, right].astype(f32)
            start = 0
            for out in (grad_qkv, grad_out, grad_small):
                w = out.shape[1]
                for lo, hi, value in ((0, cut, lhs), (cut, width, rhs)):
                    a, b = max(start, lo), min(start + w, hi)
                    if a < b:
                        out[:, a - start : b - start] = value[:, a - lo : b - lo]
                start += w

    @pl.loop(0, 4)
    def _(b):
        to_core(b).wait()

    stored = None
    for i in range(chips + 2):
        if i < chips:
            begin(order[i])
        if 0 <= i - 1 < chips:
            relay(order[i - 1])
        if i == chips:
            stored = end_in()
        if i - 2 >= 0:
            finish(order[i - 2])
    for k in order:
        for turn in range(3):
            along_x[k, turn].wait_send()
            along_y[k, turn].wait_send()
        if k:
            along_z[k].wait_send()
    for copy in stored:
        copy.wait()
    for m in range(micros):
        put_out(m).wait()
        put_x(m).wait()


def end_layer(small_inputs, big_inputs, chips):
    tokens, keep_in, full = big_inputs[0], big_inputs[-1], big_inputs[9]
    experts = 2 * chips
    micros, seq_len, model_width = tokens.shape
    spots = big_inputs[4].shape[1]
    width = full.shape[1]
    rows = model_width // (8 * chips)
    cut = (width // 128 + 1) // 2 * 128
    quarter, half = keep_in.shape[1:]
    every = micros * seq_len
    shape = jax.ShapeDtypeStruct
    vmem, hbm = pl.BlockSpec(memory_space=pltpu.VMEM), pl.BlockSpec(memory_space=pl.ANY)
    tall = (micros, seq_len, model_width)
    return pl.pallas_call(
        functools.partial(end_kernel, chips, experts, cut),
        out_shape=[
            shape((rows, 3 * model_width), f32),
            shape((rows, model_width), f32),
            shape((rows, 128), f32),
            shape(tall, bf16),
            shape(tall, f32),
            shape((quarter, 2 * half), f32),
        ],
        in_specs=[vmem] * len(small_inputs) + [hbm] * len(big_inputs),
        out_specs=[vmem] * 3 + [hbm] * 3,
        scratch_shapes=[
            pltpu.VMEM((model_width, width), bf16),
            pltpu.VMEM(tall, bf16),
            pltpu.VMEM(tall, bf16),
            pltpu.VMEM((micros, seq_len, 3 * model_width), bf16),
            pltpu.VMEM(tall, f32),
            pltpu.VMEM((micros, spots, model_width), bf16),
            pltpu.VMEM((micros, spots, model_width), bf16),
            pltpu.VMEM((every, model_width), bf16),
            pltpu.VMEM((every, model_width), bf16),
            pltpu.VMEM((every, model_width), bf16),
            pltpu.VMEM(tall, bf16),
            pltpu.VMEM(tall, f32),
            pltpu.VMEM((every, model_width), bf16),
            pltpu.VMEM((every, 3 * model_width), bf16),
            pltpu.VMEM((every, 128), bf16),
            pltpu.VMEM((seq_len, model_width), bf16),
            pltpu.VMEM((128, model_width), f32),
            pltpu.VMEM((4, chips, 2, rows, width), bf16),
            pltpu.VMEM((4, chips, rows, width), bf16),
            pltpu.VMEM((chips, 3, rows, cut), bf16),
            pltpu.VMEM((chips, 3, rows, cut), bf16),
            pltpu.VMEM((chips, rows, width), bf16),
            pltpu.VMEM((chips, rows, width), bf16),
            pltpu.VMEM((2, quarter, half), bf16),
            pltpu.VMEM((quarter, half), bf16),
            pltpu.VMEM((2, quarter, half), f32),
            DMA((7,)),
            DMA((6, micros)),
            DMA((3, micros)),
            DMA((2,)),
            DMA((2,)),
            DMA(()),
            DMA(()),
            DMA((4,)),
            DMA((4,)),
            DMA((chips, 3)),
            DMA((chips, 3)),
            DMA((chips, 3)),
            DMA((chips, 3)),
            DMA((chips,)),
            DMA((chips,)),
        ],
        compiler_params=pltpu.CompilerParams(
            collective_id=2, has_side_effects=True, vmem_limit_bytes=63 * 2**20
        ),
        name="end_layer",
    )(*small_inputs, *big_inputs)


def on_device(
    tokens,
    segment_ids,
    routes,
    cotangent,
    w_qkv,
    w_attn_out,
    w_router,
    gain_attn,
    gain_moe,
    w_expert_in,
    w_expert_out,
):
    micro_count, _, seq_len, model_width = tokens.shape
    experts = w_router.shape[1]
    chips = model_width // w_qkv.shape[0] // 8

    spare = jnp.zeros((w_qkv.shape[0], 128 - 2 - experts), bf16)
    small = jnp.concatenate([w_router, gain_attn[:, None], gain_moe[:, None], spare], axis=1)
    tokens, cotangent, segment_ids = tokens[:, 0], cotangent[:, 0], segment_ids
    routes = routes.reshape(micro_count, 1, seq_len)
    attn_in, qkv, lse, mixed, residual, hidden, probs, gains, gathered, w_in, w_out, got_g, got_h = (
        begin_layer(
            tokens,
            segment_ids,
            routes,
            cotangent,
            (w_qkv, w_attn_out, small),
            w_expert_in[0],
            w_expert_out[0],
            chips,
        )
    )
    returned, grad_back, keep_in, send_in, grad_out = run_experts(
        got_h,
        got_g,
        w_in.reshape(model_width, -1),
        w_out.reshape(-1, model_width),
        gathered,
        chips,
    )
    flat = (micro_count, -1, model_width)
    grad_qkv, grad_attn_out, small_sum, output, grad_tokens, grad_in = end_layer(
        (segment_ids, routes, gains, lse, probs),
        (
            tokens,
            cotangent,
            qkv,
            residual,
            returned.reshape(flat),
            grad_back.reshape(flat),
            attn_in.reshape(-1, model_width),
            mixed.reshape(-1, model_width),
            hidden.reshape(-1, model_width),
            gathered,
            send_in,
            keep_in,
        ),
        chips,
    )
    return (
        output[:, None],
        grad_tokens[:, None],
        grad_qkv,
        grad_attn_out,
        small_sum[:, :experts],
        small_sum[:, experts],
        small_sum[:, experts + 1],
        grad_in[None],
        grad_out.reshape(1, -1, model_width),
    )


def solution(mesh):
    rows = P(("dp", "expert"))
    seqs = P(None, ("dp", "expert"))
    owned = P("expert", "dp", None)
    return jax.shard_map(
        on_device,
        mesh=mesh,
        in_specs=(seqs, seqs, seqs, seqs, rows, rows, rows, rows, rows, owned, owned),
        out_specs=(seqs, seqs, rows, rows, rows, rows, rows, owned, owned),
        check_vma=False,
    )
```

```python
import functools
import math

import jax
import jax.numpy as jnp
from jax import lax
from jax.experimental import pallas as pl
from jax.experimental.pallas import tpu as pltpu
from jax.sharding import PartitionSpec as P

HEADS = 16
epsilon = 1e-05
masked_value = -1e30
pieces = 8
f32 = jnp.float32
bf16 = jnp.bfloat16

MESH = pl.DeviceIdType.MESH
DMA = pltpu.SemaphoreType.DMA


def flip(index, mask):
    bit = 1
    while bit <= mask:
        if mask & bit:
            index = index + bit - 2 * bit * ((index // bit) % 2)
        bit *= 2
    return index


def place_of(chips):
    block = lax.axis_index("dp")
    owner = lax.axis_index("expert")
    peer_x = {"dp": flip(block, 1)}
    peer_y = {"dp": flip(block, 2)}
    peer_core = {"expert": flip(owner, 1)}
    peers_z = [{"expert": flip(owner, 2 * k)} for k in range(chips)]
    return block, owner // 2, owner % 2, peer_x, peer_y, peer_core, peers_z


def greet(peers):
    barrier = pltpu.get_barrier_semaphore()
    for peer in peers:
        pl.semaphore_signal(barrier, inc=1, device_id=peer, device_id_type=MESH)
    pl.semaphore_wait(barrier, len(peers))


def send(src, dst, send_sem, recv_sem, peer):
    copy = pltpu.make_async_remote_copy(
        src_ref=src, dst_ref=dst, send_sem=send_sem, recv_sem=recv_sem,
        device_id=peer, device_id_type=MESH,
    )
    copy.start()
    return copy


def normalize(values):
    row_mean = jnp.mean(values, axis=-1, keepdims=True)
    centered = values - row_mean
    inv_scale = lax.rsqrt(jnp.mean(centered * centered, axis=-1, keepdims=True) + epsilon)
    return (centered * inv_scale, inv_scale)


def norm_back(grad_normed, normed, inv_scale):
    return inv_scale * (
        grad_normed
        - jnp.mean(grad_normed, axis=-1, keepdims=True)
        - normed * jnp.mean(grad_normed * normed, axis=-1, keepdims=True)
    )


def dot(a, b):
    return jnp.dot(a, b, preferred_element_type=f32)


def dot_nt(a, b):
    return lax.dot_general(a, b, (((1,), (1,)), ((), ())), preferred_element_type=f32)


def dot_tn(a, b):
    return lax.dot_general(a, b, (((0,), (0,)), ((), ())), preferred_element_type=f32)


def lanes_of(shape):
    return lax.broadcasted_iota(jnp.int32, shape, 1)


def rows_of(shape):
    return lax.broadcasted_iota(jnp.int32, shape, 0)


def column(row):
    return jnp.transpose(jnp.broadcast_to(row.astype(f32), (128, row.shape[1])))[:, :1]


def one_hot_of(route):
    return jnp.where(lanes_of((route.shape[0], 128)).astype(f32) == route, 1.0, 0.0)


def choose_slots(route, spots, experts):
    seq_len = route.shape[0]
    capacity = (9 * seq_len + 8 * experts - 1) // (8 * experts)
    one_hot = one_hot_of(route)
    square = (seq_len, seq_len)
    before = jnp.where(lanes_of(square) < rows_of(square), 1.0, 0.0).astype(bf16)
    place = jnp.sum(dot(before, one_hot.astype(bf16)) * one_hot, axis=1, keepdims=True)
    slot = jnp.where(place < capacity, route * (spots // experts) + place, -1.0)
    return jnp.where(lanes_of((seq_len, spots)).astype(f32) == slot, 1.0, 0.0).astype(bf16)


def allowed_pairs(segment_row):
    square = (segment_row.shape[1],) * 2
    same = column(segment_row) == segment_row.astype(f32)
    return (lanes_of(square) <= rows_of(square)) & same


def begin_kernel(
    chips,
    experts,
    tokens,
    segments,
    routes,
    cotangent,
    shard_qkv,
    shard_out,
    shard_small,
    w_in,
    w_out,
    attn_in,
    qkv,
    lse,
    mixed,
    residual,
    hidden,
    probs,
    gains,
    kept_full,
    full_in,
    full_out,
    got_g,
    got_h,
    full,
    slots_g,
    slots_h,
    hold_in,
    hold_out,
    own_sem,
    sz,
    rz,
    sx,
    rx,
    sy,
    ry,
    sc,
    rc,
    sw,
    rw,
    lw,
    sd,
    rd,
    se,
    re,
    ld,
):
    block, chip, core, peer_x, peer_y, peer_core, peers_z = place_of(chips)
    owner = lax.axis_index("expert")
    micros, seq_len, model_width = tokens.shape
    rows = shard_qkv.shape[0]
    width = full.shape[1]
    cut = (width // 128 + 1) // 2 * 128
    halves = (pl.ds(0, cut), pl.ds(cut, width - cut))
    every = pl.ds(0, width)
    half = w_in.shape[1] // 2
    row_y, row_x = block // 2, block % 2

    def part(origin, step, columns):
        start = ((flip(block, origin) * chips + flip(chip, step)) * 2 + core) * rows
        return full.at[pl.ds(pl.multiple_of(start, rows), rows), columns]

    own_copies = []
    for i, (src, at) in enumerate(
        ((shard_qkv, 0), (shard_out, 3 * model_width), (shard_small, 4 * model_width))
    ):
        dst = part(0, 0, pl.ds(at, src.shape[1]))
        own_copies.append(pltpu.make_async_copy(src, dst, own_sem.at[i]))
        own_copies[-1].start()
    others = [{"expert": lax.rem(owner + k, experts)} for k in range(1, experts)]
    greet([peer_x, peer_y] + others)
    for copy in own_copies:
        copy.wait()

    mine = part(0, 0, every)
    along_z = [None] + [send(mine, mine, sz.at[k], rz.at[k], peers_z[k]) for k in range(1, chips)]
    along_x = [[None] * 3 for _ in range(chips)]
    along_y = [[None] * 3 for _ in range(chips)]
    across = [[None] * 4 for _ in range(chips)]

    def to_core(k, origin):
        piece = part(origin, k, every)
        across[k][origin] = send(
            piece, piece, sc.at[k, origin], rc.at[k, origin], peer_core
        )

    def pass_on(k):
        along_x[k][1].wait_recv()
        to_core(k, 1)
        along_y[k][1].wait_recv()
        to_core(k, 2)
        along_x[k][2].wait_recv()
        along_y[k][2].wait_recv()
        to_core(k, 3)

    def spread(k):
        for turn in range(2):
            for copies, s, r, peer, side in (
                (along_x, sx, rx, peer_x, turn),
                (along_y, sy, ry, peer_y, 1 - turn),
            ):
                piece = part(0, k, halves[side])
                copies[k][turn] = send(piece, piece, s.at[k, turn], r.at[k, turn], peer)
        to_core(k, 0)

    def turn_corner(k):
        along_x[k][0].wait_recv()
        piece = part(1, k, halves[0])
        along_y[k][2] = send(piece, piece, sy.at[k, 2], ry.at[k, 2], peer_y)
        along_y[k][0].wait_recv()
        piece = part(2, k, halves[1])
        along_x[k][2] = send(piece, piece, sx.at[k, 2], rx.at[k, 2], peer_x)

    piece_rows = w_out.shape[0] // pieces
    out_x = []

    def send_piece():
        j = len(out_x)
        at = pl.ds(j * piece_rows, piece_rows)
        out_x.append(
            send(w_out.at[at], full_out.at[row_x, at], sw.at[3 + j], rw.at[3 + j], peer_x)
        )

    from_y = []

    def send_strip():
        j = len(from_y)
        size = w_in.shape[0] // pieces
        at = pl.ds(j * size, size)
        from_y.append(
            send(
                w_in.at[at, pl.ds((1 - row_y) * half, half)],
                full_in.at[block, at],
                sw.at[3 + pieces + j], rw.at[3 + pieces + j], peer_y,
            )
        )

    spread(0)

    def put_slots(slots, m, values):
        packed = dot_tn(choose_slots(column(routes[m]), experts * slots.shape[2], experts), values)
        packed = packed.astype(bf16)
        for e in range(experts):
            size = slots.shape[2]
            slots[m, e] = packed[e * size : (e + 1) * size]

    for m in range(micros):
        put_slots(slots_g, m, cotangent[m])

    for k in range(chips):
        if k:
            along_z[k].wait_recv()
            spread(k)
            pass_on(k - 1)
        turn_corner(k)
        if k < pieces // 2:
            send_piece()
            send_strip()

    local_in = pltpu.make_async_copy(w_in.at[:, pl.ds(row_y * half, half)], hold_in, lw.at[0])
    local_out = pltpu.make_async_copy(w_out, hold_out, lw.at[1])
    local_in.start()
    local_out.start()
    while len(from_y) < pieces:
        send_strip()
    from_x = send(
        w_in.at[:, pl.ds(row_y * half, half)], full_in.at[block], sw.at[1], rw.at[1], peer_x
    )
    while len(out_x) < pieces:
        send_piece()

    def slot_copies(way, slots, got, m):
        def to_owner(k):
            peer = lax.rem(owner + k, experts)
            return pltpu.make_async_remote_copy(
                src_ref=slots.at[m, peer],
                dst_ref=got.at[m, 0, owner],
                send_sem=sd.at[way, m, k],
                recv_sem=rd.at[way, m, k],
                device_id={"expert": peer},
                device_id_type=MESH,
            )

        def to_y(k):
            origin = lax.rem(owner - k + experts, experts)
            return pltpu.make_async_remote_copy(
                src_ref=got.at[m, 0, origin],
                dst_ref=got.at[m, 1, origin],
                send_sem=se.at[way, m, k],
                recv_sem=re.at[way, m, k],
                device_id=peer_y,
                device_id_type=MESH,
            )

        own = pltpu.make_async_copy(slots.at[m, owner], got.at[m, 0, owner], ld.at[way, m])
        return to_owner, to_y, own

    def start_slots(way, slots, got, m):
        to_owner, to_y, own = slot_copies(way, slots, got, m)
        own.start()

        @pl.loop(1, experts)
        def _(k):
            to_owner(k).start()

    def relay_slots(way, slots, got, m):
        to_owner, to_y, own = slot_copies(way, slots, got, m)
        own.wait()
        to_y(0).start()

        @pl.loop(1, experts)
        def _(k):
            to_owner(k).wait_recv()
            to_y(k).start()

    def end_slots(way, slots, got, m):
        to_owner, to_y, own = slot_copies(way, slots, got, m)

        @pl.loop(1, experts)
        def _(k):
            to_owner(k).wait_send()

        @pl.loop(0, experts)
        def _(k):
            to_y(k).wait()

    for m in range(micros):
        start_slots(0, slots_g, got_g, m)
    pass_on(chips - 1)
    for k in range(chips):
        for origin in range(4):
            across[k][origin].wait_recv()
    keep = pltpu.make_async_copy(full, kept_full, own_sem.at[3])
    keep.start()
    small = jnp.transpose(full[:, pl.ds(4 * model_width, 128)].astype(f32))
    gains[...] = small[experts : experts + 2]
    local_in.wait()
    local_out.wait()
    store_in = pltpu.make_async_copy(hold_in, full_in.at[block], lw.at[0])
    store_out = pltpu.make_async_copy(hold_out, full_out.at[row_x], lw.at[1])
    store_in.start()
    store_out.start()

    scale = 1.0 / math.sqrt(model_width // HEADS)
    low_half = lanes_of((seq_len, 128)) < 64
    relay_slots(0, slots_g, got_g, 0)
    for m in range(micros):
        x = tokens[m].astype(f32)
        attn_in[m] = (normalize(x)[0] * gains[0:1, :]).astype(bf16)

        @pl.loop(0, 3 * model_width // 512)
        def _(j):
            at = pl.ds(pl.multiple_of(j * 512, 512), 512)
            qkv[m, :, at] = dot(attn_in[m], full[:, at]).astype(bf16)

        allowed = allowed_pairs(segments[m])
        lse[m] = jnp.zeros(lse.shape[1:], f32)

        @pl.loop(0, model_width // 128)
        def _(pair):
            at = pl.multiple_of(pair * 128, 128)
            query = qkv[m, :, pl.ds(at, 128)]
            key = qkv[m, :, pl.ds(model_width + at, 128)]
            value = qkv[m, :, pl.ds(2 * model_width + at, 128)]
            outs = []
            for side in range(2):
                here = low_half if side == 0 else jnp.logical_not(low_half)
                scores = dot_nt(jnp.where(here, query, 0.0).astype(bf16), key) * scale
                masked = jnp.where(allowed, scores, masked_value)
                top = jnp.max(masked, axis=1, keepdims=True)
                weight = jnp.exp(masked - top)
                norm = jnp.sum(weight, axis=1, keepdims=True)
                outs.append(dot((weight / norm).astype(bf16), value))
                head = lanes_of(lse.shape[1:]) == 2 * pair + side
                lse[m] = jnp.where(head, top + jnp.log(norm), lse[m])
            mixed[m, :, pl.ds(at, 128)] = jnp.where(low_half, outs[0], outs[1]).astype(bf16)

        y1 = x + dot(mixed[m], full[:, pl.ds(3 * model_width, model_width)])
        residual[m] = y1
        low = (normalize(y1)[0] * gains[1:2, :]).astype(bf16)
        hidden[m] = low
        put_slots(slots_h, m, low)
        start_slots(1, slots_h, got_h, m)
        logits = dot(low, full[:, pl.ds(4 * model_width, 128)])
        real = lanes_of(logits.shape) < experts
        logits = jnp.where(real, logits, masked_value)
        weight = jnp.where(real, jnp.exp(logits - jnp.max(logits, axis=1, keepdims=True)), 0.0)
        probs[m] = weight / jnp.sum(weight, axis=1, keepdims=True)
        if m + 1 < micros:
            relay_slots(0, slots_g, got_g, m + 1)
        if m:
            relay_slots(1, slots_h, got_h, m - 1)
    for copy in from_y:
        copy.wait_recv()
    piece = full_in.at[flip(block, 2)]
    diagonal = send(piece, piece, sw.at[2], rw.at[2], peer_x)
    relay_slots(1, slots_h, got_h, micros - 1)

    for m in range(micros):
        end_slots(0, slots_g, got_g, m)
        end_slots(1, slots_h, got_h, m)
    keep.wait()
    store_in.wait()
    store_out.wait()
    for copy in from_y:
        copy.wait_send()
    for copy in (from_x, diagonal, *out_x):
        copy.wait()
    for k in range(chips):
        if k:
            along_z[k].wait_send()
        for turn in range(3):
            along_x[k][turn].wait_send()
            along_y[k][turn].wait_send()
        for origin in range(4):
            across[k][origin].wait_send()


def begin_layer(tokens, segments, routes, cotangent, shards, w_in, w_out, chips):
    experts = 2 * chips
    micros, seq_len, model_width = tokens.shape
    capacity = (9 * seq_len + 8 * experts - 1) // (8 * experts)
    padded = (capacity + 7) // 8 * 8
    width = 4 * model_width + 128
    rows, half = w_in.shape[0], w_in.shape[1] // 2
    shape = jax.ShapeDtypeStruct
    vmem, hbm = pl.BlockSpec(memory_space=pltpu.VMEM), pl.BlockSpec(memory_space=pl.ANY)
    spots = (micros, experts, padded, model_width)
    return pl.pallas_call(
        functools.partial(begin_kernel, chips, experts),
        out_shape=[
            shape((micros, seq_len, model_width), bf16),
            shape((micros, seq_len, 3 * model_width), bf16),
            shape((micros, seq_len, 128), f32),
            shape((micros, seq_len, model_width), bf16),
            shape((micros, seq_len, model_width), f32),
            shape((micros, seq_len, model_width), bf16),
            shape((micros, seq_len, 128), f32),
            shape((2, model_width), f32),
            shape((model_width, width), bf16),
            shape((4, rows, half), bf16),
            shape((2,) + w_out.shape, bf16),
            shape((micros, 2, experts, padded, model_width), bf16),
            shape((micros, 2, experts, padded, model_width), bf16),
        ],
        in_specs=[vmem] * 4 + [hbm] * 5,
        out_specs=[vmem] * 8 + [hbm] * 5,
        scratch_shapes=[
            pltpu.VMEM((model_width, width), bf16),
            pltpu.VMEM(spots, bf16),
            pltpu.VMEM(spots, bf16),
            pltpu.VMEM((rows, half), bf16),
            pltpu.VMEM(w_out.shape, bf16),
            DMA((4,)),
            DMA((chips,)),
            DMA((chips,)),
            DMA((chips, 3)),
            DMA((chips, 3)),
            DMA((chips, 3)),
            DMA((chips, 3)),
            DMA((chips, 4)),
            DMA((chips, 4)),
            DMA((3 + 2 * pieces,)),
            DMA((3 + 2 * pieces,)),
            DMA((2,)),
            DMA((2, micros, experts)),
            DMA((2, micros, experts)),
            DMA((2, micros, experts)),
            DMA((2, micros, experts)),
            DMA((2, micros)),
        ],
        compiler_params=pltpu.CompilerParams(
            collective_id=1, has_side_effects=True, vmem_limit_bytes=60 * 2**20
        ),
        name="begin_layer",
    )(tokens, segments, routes, cotangent, *shards, w_in, w_out)


def expert_kernel(
    chips,
    experts,
    got_h,
    got_g,
    w_in_hbm,
    w_out_hbm,
    full,
    returned,
    grad_back,
    keep_in,
    send_in,
    grad_out,
    x_buf,
    gz_buf,
    w_in,
    w_out,
    router,
    act,
    gu,
    own,
    part,
    part_got,
    out_part,
    out_got,
    out_stage,
    in_part,
    in_stage,
    load,
    sy,
    ry,
    sz,
    rz,
    lz,
    sx,
    rx,
    st,
):
    block, chip, core, peer_x, peer_y, peer_core, peers_z = place_of(chips)
    owner = lax.axis_index("expert")
    micros, rows, model_width = got_h.shape
    half = w_in.shape[1]
    mine = rows // 2
    padded = part.shape[3]
    row_x = block % 2
    step = 256
    backs = (returned, grad_back)

    sources = [
        (got_h.at[0], x_buf.at[pl.ds(0, rows)]),
        (w_in_hbm, w_in),
        (w_out_hbm, w_out),
        (full.at[:, pl.ds(4 * model_width, 128)], router),
        (got_g.at[0], gz_buf.at[pl.ds(0, rows)]),
        (got_h.at[1], x_buf.at[pl.ds(rows, rows)]),
        (got_g.at[1], gz_buf.at[pl.ds(rows, rows)]),
    ]
    loads = []
    for i, (src, dst) in enumerate(sources):
        loads.append(pltpu.make_async_copy(src, dst, load.at[i]))
        loads[-1].start()
    greet(
        [peer_x, peer_y]
        + [{"expert": lax.rem(owner + k, experts)} for k in range(1, experts)]
    )

    def of(m):
        return pl.ds(m * rows, rows)

    def gate_rows(m):
        logits = dot(x_buf[of(m), :], router[...])
        lanes = lanes_of(logits.shape)
        logits = jnp.where(lanes < experts, logits, masked_value)
        weight = jnp.exp(logits - jnp.max(logits, axis=1, keepdims=True))
        weight = jnp.where(lanes < experts, weight, 0.0)
        picked = jnp.sum(jnp.where(lanes == owner, weight, 0.0), axis=1, keepdims=True)
        gate = picked / jnp.sum(weight, axis=1, keepdims=True)
        gz_buf[of(m), :] = (gate * gz_buf[of(m), :].astype(f32)).astype(bf16)

    def open_rows(m, forward, backward):
        @pl.loop(0, half // step)
        def _(j):
            at = pl.ds(pl.multiple_of(j * step, step), step)
            u = dot(x_buf[of(m), :], w_in[:, at])
            root = math.sqrt(2.0 / math.pi)
            square = u * u
            bend = jnp.tanh(root * (u + 0.044715 * (u * square)))
            if forward:
                act[of(m), at] = (0.5 * u * (1.0 + bend)).astype(bf16)
            if backward:
                back = dot_nt(gz_buf[of(m), :], w_out[at, :])
                slope = 0.5 * (1.0 + bend) + 0.5 * u * (1.0 - bend * bend) * (
                    root * (1.0 + (3.0 * 0.044715) * square)
                )
                gu[of(m), at] = (back * slope).astype(bf16)

    wing = model_width // 2

    def columns(side):
        return pl.ds(pl.multiple_of(side * wing, wing), wing)

    def swap(m, way, side):
        return pltpu.make_async_remote_copy(
            src_ref=part.at[m, way, :, :, columns(side)],
            dst_ref=part_got.at[m, way, :, :, columns(side)],
            send_sem=sy.at[m, way, side],
            recv_sem=ry.at[m, way, side],
            device_id=peer_y,
            device_id_type=MESH,
        )

    def close_rows(m, way):
        @pl.loop(0, 2)
        def _(side):
            @pl.loop(0, wing // step)
            def _(j):
                at = pl.ds(pl.multiple_of(side * wing + j * step, step), step)
                if way == 0:
                    total = dot(act[of(m), :], w_out[:, at])
                else:
                    total = dot_nt(gu[of(m), :], w_in[at, :])
                own[m, way, :, at] = total[:mine]
                for e in range(experts):
                    start = mine + e * padded
                    part[m, way, e, :, at] = total[start : start + padded].astype(bf16)

            swap(m, way, side).start()

    def to_source(m, way, side, k):
        peer = lax.rem(owner + k, experts)
        return pltpu.make_async_remote_copy(
            src_ref=part.at[m, way, peer, :, columns(side)],
            dst_ref=backs[way].at[m, owner, :, columns(side)],
            send_sem=sz.at[m, way, side, k],
            recv_sem=rz.at[m, way, side, k],
            device_id={"expert": peer},
            device_id_type=MESH,
        )

    def to_self(m, way, side):
        return pltpu.make_async_copy(
            part.at[m, way, owner, :, columns(side)],
            backs[way].at[m, owner, :, columns(side)],
            lz.at[m, way, side],
        )

    def give_back(m, way, side):
        swap(m, way, side).wait()

        @pl.loop(0, experts)
        def _(e):
            at = pl.ds(pl.multiple_of(e * padded, padded), padded)
            cols = columns(side)
            total = own[m, way, at, cols] + part_got[m, way, e, :, cols].astype(f32)
            part[m, way, e, :, cols] = total.astype(bf16)

        to_self(m, way, side).start()

        @pl.loop(1, experts)
        def _(k):
            to_source(m, way, side, k).start()

    def end_back(m, way, side):
        to_self(m, way, side).wait()

        @pl.loop(1, experts)
        def _(k):
            to_source(m, way, side, k).wait()

    chunks = out_part.shape[0]

    def out_rows(side, j):
        start = side * (half // 2) + j * step
        return dot_tn(act[:, pl.ds(pl.multiple_of(start, step), step)], gz_buf[...])

    def to_x(j):
        return pltpu.make_async_remote_copy(
            src_ref=out_part.at[j],
            dst_ref=out_got.at[j],
            send_sem=sx.at[j],
            recv_sem=rx.at[j],
            device_id=peer_x,
            device_id_type=MESH,
        )

    def put_out(j, slot):
        return pltpu.make_async_copy(out_stage.at[slot], grad_out.at[j], st.at[slot])

    def send_out_rows():
        @pl.loop(0, chunks)
        def _(j):
            out_part[j] = out_rows(1 - row_x, j).astype(bf16)
            to_x(j).start()

    def keep_out_rows():
        for j in range(chunks):
            if j > 1:
                put_out(j - 2, j % 2).wait()
            to_x(j).wait()
            out_stage[j % 2] = out_rows(row_x, j) + out_got[j].astype(f32)
            put_out(j, j % 2).start()

    quarter = in_stage.shape[0]

    def in_rows(y, x):
        start = (2 * y + x) * quarter
        return pl.ds(pl.multiple_of(start, quarter), quarter)

    def in_copies(y):
        return (
            pltpu.make_async_copy(in_part, send_in.at[y], st.at[2]),
            pltpu.make_async_copy(in_stage, keep_in.at[y], st.at[3]),
        )

    def first_rows():
        for y in range(2):
            for kind in range(2):
                if y:
                    in_copies(0)[kind].wait()
                cols = in_rows(y, 1 - row_x if kind == 0 else row_x)

                @pl.loop(0, half // (2 * step))
                def _(j):
                    at = pl.ds(pl.multiple_of(j * 2 * step, 2 * step), 2 * step)
                    value = dot_tn(x_buf[:, cols], gu[:, at])
                    if kind == 0:
                        in_part[:, at] = value.astype(bf16)
                    else:
                        in_stage[:, at] = value

                in_copies(y)[kind].start()

    loads[0].wait()
    loads[1].wait()
    open_rows(0, True, False)
    loads[2].wait()
    close_rows(0, 0)
    loads[5].wait()
    open_rows(1, True, False)
    close_rows(1, 0)
    give_back(0, 0, 0)
    for i in (3, 4, 6):
        loads[i].wait()
    gate_rows(0)
    gate_rows(1)
    give_back(0, 0, 1)
    send_out_rows()
    give_back(1, 0, 0)
    open_rows(0, False, True)
    give_back(1, 0, 1)
    close_rows(0, 1)
    open_rows(1, False, True)
    give_back(0, 1, 0)
    close_rows(1, 1)
    give_back(0, 1, 1)
    first_rows()
    give_back(1, 1, 0)
    give_back(1, 1, 1)
    keep_out_rows()
    for j in range(chunks - 2, chunks):
        put_out(j, j % 2).wait()
    for copy in in_copies(1):
        copy.wait()
    for m in range(micros):
        for way in range(2):
            end_back(m, way, 0)
            end_back(m, way, 1)


def run_experts(got_h, got_g, w_in, w_out, full, chips):
    experts = 2 * chips
    micros, _, _, padded, model_width = got_h.shape
    rows = 2 * experts * padded
    half = w_in.shape[1]
    shape = jax.ShapeDtypeStruct
    hbm = pl.BlockSpec(memory_space=pl.ANY)
    slots = shape((micros, experts, padded, model_width), bf16)
    chunks = half // 2 // 256
    quarter = model_width // 4
    spots = (micros, 2, experts, padded, model_width)
    return pl.pallas_call(
        functools.partial(expert_kernel, chips, experts),
        out_shape=[
            slots,
            slots,
            shape((2, quarter, half), f32),
            shape((2, quarter, half), bf16),
            shape((chunks, 256, model_width), f32),
        ],
        in_specs=[hbm] * 5,
        out_specs=[hbm] * 5,
        scratch_shapes=[
            pltpu.VMEM((micros * rows, model_width), bf16),
            pltpu.VMEM((micros * rows, model_width), bf16),
            pltpu.VMEM((model_width, half), bf16),
            pltpu.VMEM((half, model_width), bf16),
            pltpu.VMEM((model_width, 128), bf16),
            pltpu.VMEM((micros * rows, half), bf16),
            pltpu.VMEM((micros * rows, half), bf16),
            pltpu.VMEM((micros, 2, rows // 2, model_width), f32),
            pltpu.VMEM(spots, bf16),
            pltpu.VMEM(spots, bf16),
            pltpu.VMEM((chunks, 256, model_width), bf16),
            pltpu.VMEM((chunks, 256, model_width), bf16),
            pltpu.VMEM((2, 256, model_width), f32),
            pltpu.VMEM((quarter, half), bf16),
            pltpu.VMEM((quarter, half), f32),
            DMA((7,)),
            DMA((micros, 2, 2)),
            DMA((micros, 2, 2)),
            DMA((micros, 2, 2, experts)),
            DMA((micros, 2, 2, experts)),
            DMA((micros, 2, 2)),
            DMA((chunks,)),
            DMA((chunks,)),
            DMA((4,)),
        ],
        compiler_params=pltpu.CompilerParams(
            collective_id=3, has_side_effects=True, vmem_limit_bytes=63 * 2**20
        ),
        name="run_experts",
    )(
        got_h.reshape(micros, rows, model_width),
        got_g.reshape(micros, rows, model_width),
        w_in,
        w_out,
        full,
    )


def end_kernel(
    chips,
    experts,
    cut,
    segments,
    routes,
    gains,
    lse,
    probs,
    tokens,
    cotangent,
    qkv_hbm,
    y1_hbm,
    returned_hbm,
    back_hbm,
    attn_hbm,
    mixed_hbm,
    hidden_hbm,
    full_hbm,
    send_in,
    keep_in,
    grad_qkv,
    grad_out,
    grad_small,
    output,
    grad_x,
    grad_in,
    full,
    x_buf,
    g_buf,
    qkv,
    y1_buf,
    returned,
    back,
    attn_in,
    mixed,
    hidden,
    out_buf,
    gx_buf,
    branch,
    gqkv,
    glog_buf,
    go_buf,
    gain_rows,
    grads,
    crecv,
    xrecv,
    yrecv,
    part_z,
    zrecv,
    brecv,
    got_in,
    got_y,
    keep,
    load,
    load_m,
    put,
    si,
    ri,
    siy,
    riy,
    sc,
    rc,
    sx,
    rx,
    sy,
    ry,
    sz,
    rz,
    sb,
    rb,
):
    block, chip, core, peer_x, peer_y, peer_core, peers_z = place_of(chips)
    micros, seq_len, model_width = tokens.shape
    width = full.shape[1]
    row_y = block // 2
    opposite = flip(core, 1)
    wide_qkv = 3 * model_width

    late = pl.ds(wide_qkv, width - wide_qkv)
    early = pl.ds(0, wide_qkv)
    once = [
        (full_hbm.at[:, late], full.at[:, late]),
        (full_hbm.at[:, early], full.at[:, early]),
        (keep_in.at[1 - row_y], keep.at[0]),
        (keep_in.at[row_y], keep.at[1]),
        (attn_hbm, attn_in),
        (mixed_hbm, mixed),
        (hidden_hbm, hidden),
    ]
    once = [pltpu.make_async_copy(src, dst, load.at[i]) for i, (src, dst) in enumerate(once)]
    pairs = (
        (returned_hbm, returned),
        (back_hbm, back),
        (cotangent, g_buf),
        (y1_hbm, y1_buf),
        (qkv_hbm, qkv),
        (tokens, x_buf),
    )

    def load_of(i, m):
        src, dst = pairs[i]
        return pltpu.make_async_copy(src.at[m], dst.at[m], load_m.at[i, m])

    once[0].start()
    for i in range(len(pairs)):
        load_of(i, 0).start()
    once[1].start()
    for i in range(len(pairs)):
        load_of(i, 1).start()
    for copy in once[2:]:
        copy.start()

    greet([peer_x, peer_y, peer_core] + peers_z[1:])

    def in_x(j):
        return pltpu.make_async_remote_copy(
            src_ref=send_in.at[1 - row_y if j == 0 else row_y],
            dst_ref=got_in.at[j],
            send_sem=si.at[j],
            recv_sem=ri.at[j],
            device_id=peer_x,
            device_id_type=MESH,
        )

    in_y = pltpu.make_async_remote_copy(
        src_ref=got_in.at[0],
        dst_ref=got_y,
        send_sem=siy,
        recv_sem=riy,
        device_id=peer_y,
        device_id_type=MESH,
    )
    in_x(0).start()
    in_x(1).start()
    strip = 32

    def pass_in_y():
        once[2].wait()
        in_x(0).wait()

        @pl.loop(0, keep.shape[1] // strip)
        def _(j):
            at = pl.ds(pl.multiple_of(j * strip, strip), strip)
            got_in[0, at, :] = (keep[0, at, :] + got_in[0, at, :].astype(f32)).astype(bf16)

        in_y.start()

    def put_in(slot, side):
        half = keep.shape[2]
        cols = pl.ds(pl.multiple_of(side * half, half), half)
        copy = pltpu.make_async_copy(keep.at[slot], grad_in.at[:, cols], put.at[2, slot])
        copy.start()
        return copy

    def end_in():
        once[3].wait()
        in_x(1).wait()

        @pl.loop(0, keep.shape[1] // strip)
        def _(j):
            at = pl.ds(pl.multiple_of(j * strip, strip), strip)
            keep[1, at, :] = keep[1, at, :] + got_in[1, at, :].astype(f32)

        stored = [put_in(1, row_y)]
        in_y.wait()

        @pl.loop(0, keep.shape[1] // strip)
        def _(j):
            at = pl.ds(pl.multiple_of(j * strip, strip), strip)
            keep[0, at, :] = got_y[at, :].astype(f32)

        return stored + [put_in(0, 1 - row_y)]

    def put_out(m):
        return pltpu.make_async_copy(out_buf.at[m], output.at[m], put.at[0, m])

    def put_x(m):
        return pltpu.make_async_copy(gx_buf.at[m], grad_x.at[m], put.at[1, m])

    gain_rows[...] = jnp.zeros(gain_rows.shape, f32)
    scale = 1.0 / math.sqrt(model_width // HEADS)
    low_half = lanes_of((seq_len, 128)) < 64
    once[0].wait()

    @pl.loop(0, micros)
    def _(m):
        here = pl.ds(pl.multiple_of(m * seq_len, seq_len), seq_len)
        for i in range(4):
            load_of(i, m).wait()
        g = g_buf[m].astype(f32)
        route = column(routes[m])
        chosen = choose_slots(route, returned.shape[1], experts)
        moe = dot(chosen, returned[m])
        prob = probs[m]
        one_hot = one_hot_of(route)
        gate = jnp.sum(prob * one_hot, axis=1, keepdims=True)
        y1 = y1_buf[m]
        out_buf[m] = (y1 + gate * moe).astype(bf16)
        put_out(m).start()
        choice = one_hot * jnp.sum(g * moe, axis=1, keepdims=True)
        glog = (prob * (choice - jnp.sum(prob * choice, axis=1, keepdims=True))).astype(bf16)
        glog_buf[here, :] = glog
        grad_h = dot(chosen, back[m]) + dot_nt(glog, full[:, pl.ds(4 * model_width, 128)])
        n2, inv2 = normalize(y1)
        gain_rows[experts + 1 : experts + 2, :] += jnp.sum(grad_h * n2, axis=0, keepdims=True)
        gy1 = g + norm_back(grad_h * gains[1:2, :], n2, inv2)
        gx_buf[m] = gy1
        branch[here, :] = gy1.astype(bf16)
        go_buf[...] = dot_nt(branch[here, :], full[:, pl.ds(wide_qkv, model_width)]).astype(bf16)
        load_of(4, m).wait()
        load_of(5, m).wait()

        allowed = allowed_pairs(segments[m])

        @pl.loop(0, model_width // 128)
        def _(pair):
            @pl.when((m == 1) & (pair == 4))
            def _():
                pass_in_y()

            at = pl.multiple_of(pair * 128, 128)
            query = qkv[m, :, pl.ds(at, 128)]
            key = qkv[m, :, pl.ds(model_width + at, 128)]
            value = qkv[m, :, pl.ds(2 * model_width + at, 128)]
            grad_o = go_buf[:, pl.ds(at, 128)]
            parts = []
            for side in range(2):
                mine = low_half if side == 0 else jnp.logical_not(low_half)
                scores = dot_nt(jnp.where(mine, query, 0.0).astype(bf16), key) * scale
                head = lanes_of(lse.shape[1:]) == 2 * pair + side
                top = jnp.sum(jnp.where(head, lse[m], 0.0), axis=1, keepdims=True)
                p = jnp.exp(jnp.where(allowed, scores, masked_value) - top)
                gp = dot_nt(jnp.where(mine, grad_o, 0.0).astype(bf16), value)
                gs = (p * (gp - jnp.sum(p * gp, axis=1, keepdims=True))).astype(bf16)
                parts.append(
                    (dot(gs, key) * scale, dot_tn(gs, query) * scale, dot_tn(p.astype(bf16), grad_o))
                )
            for i in range(3):
                both = jnp.where(low_half, parts[0][i], parts[1][i]).astype(bf16)
                gqkv[here, pl.ds(i * model_width + at, 128)] = both

        @pl.when(m == 0)
        def _():
            once[1].wait()

        ga = dot_nt(gqkv[here, :], full[:, pl.ds(0, wide_qkv)])
        n1, inv1 = normalize(x_buf[m].astype(f32))
        gain_rows[experts : experts + 1, :] += jnp.sum(ga * n1, axis=0, keepdims=True)
        gx_buf[m] = gx_buf[m] + norm_back(ga * gains[0:1, :], n1, inv1)
        put_x(m).start()

    for copy in once[4:]:
        copy.wait()
    rows = grads.shape[3]
    span = model_width // 4

    def to_core(b):
        return pltpu.make_async_remote_copy(
            src_ref=grads.at[b, :, opposite],
            dst_ref=crecv.at[b],
            send_sem=sc.at[b],
            recv_sem=rc.at[b],
            device_id=peer_core,
            device_id_type=MESH,
        )

    @pl.loop(0, 4)
    def _(b):
        cols = pl.ds(pl.multiple_of(b * span, span), span)

        def store(start, value):
            value = value.reshape(chips, 2, rows, value.shape[1]).astype(bf16)
            grads[b, :, :, :, pl.ds(start, value.shape[3])] = value

        @pl.loop(0, wide_qkv // 512)
        def _(j):
            start = pl.multiple_of(j * 512, 512)
            store(start, dot_tn(attn_in[:, cols], gqkv[:, pl.ds(start, 512)]))

        store(wide_qkv, dot_tn(mixed[:, cols], branch[...]))
        small = dot_tn(hidden[:, cols], glog_buf[...]) + jnp.transpose(gain_rows[:, cols])
        store(4 * model_width, small)
        to_core(b).start()

    inner = width - brecv.shape[3]
    outer = pl.ds(inner, width - inner)
    order = list(range(chips - 1, -1, -1))
    along_x, along_y, along_z, along_b = {}, {}, {}, {}

    def halves_of(k):
        low, end = (inner // 256 * 128, inner) if k else (cut, width)
        return pl.ds(0, low), pl.ds(low, end - low), pl.ds(0, end - low)

    def spot(k, origin, cols):
        return (flip(block, origin), flip(chip, k), core, slice(None), cols)

    def add_core(k, origin, cols):
        at = spot(k, origin, cols)
        return grads[at].astype(f32) + crecv[at[:2] + at[3:]].astype(f32)

    def begin_outer(k):
        for origin in range(4):
            at = spot(k, origin, outer)
            grads[at] = add_core(k, origin, outer).astype(bf16)
            along_b[k, origin] = send(
                grads.at[at], brecv.at[k, origin], sb.at[k, origin], rb.at[k, origin], peers_z[k]
            )

    def begin(k):
        left, right, short = halves_of(k)
        for origin in (3, 1, 2, 0):
            at = spot(k, origin, pl.ds(0, inner))
            grads[at] = add_core(k, origin, pl.ds(0, inner)).astype(bf16)
            if k == 0:
                total = add_core(0, origin, outer)
                for j in range(1, chips):
                    along_b[j, origin].wait_recv()
                    total = total + brecv[j, origin].astype(f32)
                grads[spot(0, origin, outer)] = total.astype(bf16)
            if origin == 3:
                along_x[k, 0] = send(
                    grads.at[spot(k, 3, left)], xrecv.at[k, 0, :, left], sx.at[k, 0], rx.at[k, 0], peer_x
                )
                along_y[k, 0] = send(
                    grads.at[spot(k, 3, right)], yrecv.at[k, 0, :, short], sy.at[k, 0], ry.at[k, 0], peer_y
                )
            if origin == 1:
                along_x[k, 1] = send(
                    grads.at[spot(k, 1, left)], xrecv.at[k, 1, :, left], sx.at[k, 1], rx.at[k, 1], peer_x
                )
            if origin == 2:
                along_y[k, 1] = send(
                    grads.at[spot(k, 2, right)], yrecv.at[k, 1, :, short], sy.at[k, 1], ry.at[k, 1], peer_y
                )

    def relay(k):
        left, right, short = halves_of(k)
        along_x[k, 0].wait_recv()
        at = spot(k, 2, left)
        grads[at] = (grads[at].astype(f32) + xrecv[k, 0, :, left].astype(f32)).astype(bf16)
        along_y[k, 2] = send(grads.at[at], yrecv.at[k, 2, :, left], sy.at[k, 2], ry.at[k, 2], peer_y)
        along_y[k, 0].wait_recv()
        at = spot(k, 1, right)
        grads[at] = (grads[at].astype(f32) + yrecv[k, 0, :, short].astype(f32)).astype(bf16)
        along_x[k, 2] = send(
            grads.at[at], xrecv.at[k, 2, :, short], sx.at[k, 2], rx.at[k, 2], peer_x
        )

    def finish(k):
        left, right, short = halves_of(k)
        for turn in (1, 2):
            along_x[k, turn].wait_recv()
            along_y[k, turn].wait_recv()
        lhs = (
            grads[spot(k, 0, left)].astype(f32)
            + xrecv[k, 1, :, left].astype(f32)
            + yrecv[k, 2, :, left].astype(f32)
        )
        rhs = (
            grads[spot(k, 0, right)].astype(f32)
            + yrecv[k, 1, :, short].astype(f32)
            + xrecv[k, 2, :, short].astype(f32)
        )
        if k:
            part_z[k, :, left] = lhs.astype(bf16)
            part_z[k, :, right] = rhs.astype(bf16)
            cols = pl.ds(0, inner)
            along_z[k] = send(
                part_z.at[k, :, cols], zrecv.at[k, :, cols], sz.at[k], rz.at[k], peers_z[k]
            )
        else:
            middle, rhs = rhs[:, : inner - cut], rhs[:, inner - cut :]
            for j in range(1, chips):
                along_z[j].wait_recv()
                lhs = lhs + zrecv[j, :, left].astype(f32)
                middle = middle + zrecv[j, :, pl.ds(cut, inner - cut)].astype(f32)
            start = 0
            for out in (grad_qkv, grad_out, grad_small):
                w = out.shape[1]
                for lo, hi, value in ((0, cut, lhs), (cut, inner, middle), (inner, width, rhs)):
                    a, b = max(start, lo), min(start + w, hi)
                    if a < b:
                        out[:, a - start : b - start] = value[:, a - lo : b - lo]
                start += w

    @pl.loop(0, 4)
    def _(b):
        to_core(b).wait()

    for k in order[:-1]:
        begin_outer(k)
    stored = None
    for i in range(chips + 2):
        if i < chips:
            begin(order[i])
        if 0 <= i - 1 < chips:
            relay(order[i - 1])
        if i == chips:
            stored = end_in()
        if i - 2 >= 0:
            finish(order[i - 2])
    for k in order:
        for turn in range(3):
            along_x[k, turn].wait_send()
            along_y[k, turn].wait_send()
        if k:
            along_z[k].wait_send()
            for origin in range(4):
                along_b[k, origin].wait_send()
    for copy in stored:
        copy.wait()
    for m in range(micros):
        put_out(m).wait()
        put_x(m).wait()


def end_layer(small_inputs, big_inputs, chips):
    tokens, keep_in, full = big_inputs[0], big_inputs[-1], big_inputs[9]
    experts = 2 * chips
    micros, seq_len, model_width = tokens.shape
    spots = big_inputs[4].shape[1]
    width = full.shape[1]
    rows = model_width // (8 * chips)
    cut = (width // 128 + 1) // 2 * 128
    quarter, half = keep_in.shape[1:]
    every = micros * seq_len
    shape = jax.ShapeDtypeStruct
    vmem, hbm = pl.BlockSpec(memory_space=pltpu.VMEM), pl.BlockSpec(memory_space=pl.ANY)
    tall = (micros, seq_len, model_width)
    return pl.pallas_call(
        functools.partial(end_kernel, chips, experts, cut),
        out_shape=[
            shape((rows, 3 * model_width), f32),
            shape((rows, model_width), f32),
            shape((rows, 128), f32),
            shape(tall, bf16),
            shape(tall, f32),
            shape((quarter, 2 * half), f32),
        ],
        in_specs=[vmem] * len(small_inputs) + [hbm] * len(big_inputs),
        out_specs=[vmem] * 3 + [hbm] * 3,
        scratch_shapes=[
            pltpu.VMEM((model_width, width), bf16),
            pltpu.VMEM(tall, bf16),
            pltpu.VMEM(tall, bf16),
            pltpu.VMEM((micros, seq_len, 3 * model_width), bf16),
            pltpu.VMEM(tall, f32),
            pltpu.VMEM((micros, spots, model_width), bf16),
            pltpu.VMEM((micros, spots, model_width), bf16),
            pltpu.VMEM((every, model_width), bf16),
            pltpu.VMEM((every, model_width), bf16),
            pltpu.VMEM((every, model_width), bf16),
            pltpu.VMEM(tall, bf16),
            pltpu.VMEM(tall, f32),
            pltpu.VMEM((every, model_width), bf16),
            pltpu.VMEM((every, 3 * model_width), bf16),
            pltpu.VMEM((every, 128), bf16),
            pltpu.VMEM((seq_len, model_width), bf16),
            pltpu.VMEM((128, model_width), f32),
            pltpu.VMEM((4, chips, 2, rows, width), bf16),
            pltpu.VMEM((4, chips, rows, width), bf16),
            pltpu.VMEM((chips, 3, rows, cut), bf16),
            pltpu.VMEM((chips, 3, rows, cut), bf16),
            pltpu.VMEM((chips, rows, width), bf16),
            pltpu.VMEM((chips, rows, width), bf16),
            pltpu.VMEM((chips, 4, rows, width // 512 * 128), bf16),
            pltpu.VMEM((2, quarter, half), bf16),
            pltpu.VMEM((quarter, half), bf16),
            pltpu.VMEM((2, quarter, half), f32),
            DMA((7,)),
            DMA((6, micros)),
            DMA((3, micros)),
            DMA((2,)),
            DMA((2,)),
            DMA(()),
            DMA(()),
            DMA((4,)),
            DMA((4,)),
            DMA((chips, 3)),
            DMA((chips, 3)),
            DMA((chips, 3)),
            DMA((chips, 3)),
            DMA((chips,)),
            DMA((chips,)),
            DMA((chips, 4)),
            DMA((chips, 4)),
        ],
        compiler_params=pltpu.CompilerParams(
            collective_id=2, has_side_effects=True, vmem_limit_bytes=63 * 2**20
        ),
        name="end_layer",
    )(*small_inputs, *big_inputs)


def on_device(
    tokens,
    segment_ids,
    routes,
    cotangent,
    w_qkv,
    w_attn_out,
    w_router,
    gain_attn,
    gain_moe,
    w_expert_in,
    w_expert_out,
):
    micro_count, _, seq_len, model_width = tokens.shape
    experts = w_router.shape[1]
    chips = model_width // w_qkv.shape[0] // 8

    spare = jnp.zeros((w_qkv.shape[0], 128 - 2 - experts), bf16)
    small = jnp.concatenate([w_router, gain_attn[:, None], gain_moe[:, None], spare], axis=1)
    tokens, cotangent, segment_ids = tokens[:, 0], cotangent[:, 0], segment_ids
    routes = routes.reshape(micro_count, 1, seq_len)
    attn_in, qkv, lse, mixed, residual, hidden, probs, gains, gathered, w_in, w_out, got_g, got_h = (
        begin_layer(
            tokens,
            segment_ids,
            routes,
            cotangent,
            (w_qkv, w_attn_out, small),
            w_expert_in[0],
            w_expert_out[0],
            chips,
        )
    )
    returned, grad_back, keep_in, send_in, grad_out = run_experts(
        got_h,
        got_g,
        w_in.reshape(model_width, -1),
        w_out.reshape(-1, model_width),
        gathered,
        chips,
    )
    flat = (micro_count, -1, model_width)
    grad_qkv, grad_attn_out, small_sum, output, grad_tokens, grad_in = end_layer(
        (segment_ids, routes, gains, lse, probs),
        (
            tokens,
            cotangent,
            qkv,
            residual,
            returned.reshape(flat),
            grad_back.reshape(flat),
            attn_in.reshape(-1, model_width),
            mixed.reshape(-1, model_width),
            hidden.reshape(-1, model_width),
            gathered,
            send_in,
            keep_in,
        ),
        chips,
    )
    return (
        output[:, None],
        grad_tokens[:, None],
        grad_qkv,
        grad_attn_out,
        small_sum[:, :experts],
        small_sum[:, experts],
        small_sum[:, experts + 1],
        grad_in[None],
        grad_out.reshape(1, -1, model_width),
    )


def solution(mesh):
    rows = P(("dp", "expert"))
    seqs = P(None, ("dp", "expert"))
    owned = P("expert", "dp", None)
    return jax.shard_map(
        on_device,
        mesh=mesh,
        in_specs=(seqs, seqs, seqs, seqs, rows, rows, rows, rows, rows, owned, owned),
        out_specs=(seqs, seqs, rows, rows, rows, rows, rows, owned, owned),
        check_vma=False,
    )
```

```python
import functools
import math

import jax
import jax.numpy as jnp
from jax import lax
from jax.experimental import pallas as pl
from jax.experimental.pallas import tpu as pltpu
from jax.sharding import PartitionSpec as P

HEADS = 16
epsilon = 1e-05
masked_value = -1e30
pieces = 8
f32 = jnp.float32
bf16 = jnp.bfloat16

MESH = pl.DeviceIdType.MESH
DMA = pltpu.SemaphoreType.DMA


def flip(index, mask):
    bit = 1
    while bit <= mask:
        if mask & bit:
            index = index + bit - 2 * bit * ((index // bit) % 2)
        bit *= 2
    return index


def place_of(chips):
    block = lax.axis_index("dp")
    owner = lax.axis_index("expert")
    peer_x = {"dp": flip(block, 1)}
    peer_y = {"dp": flip(block, 2)}
    peer_core = {"expert": flip(owner, 1)}
    peers_z = [{"expert": flip(owner, 2 * k)} for k in range(chips)]
    return block, owner // 2, owner % 2, peer_x, peer_y, peer_core, peers_z


def greet(peers):
    barrier = pltpu.get_barrier_semaphore()
    for peer in peers:
        pl.semaphore_signal(barrier, inc=1, device_id=peer, device_id_type=MESH)
    pl.semaphore_wait(barrier, len(peers))


def send(src, dst, send_sem, recv_sem, peer):
    copy = pltpu.make_async_remote_copy(
        src_ref=src, dst_ref=dst, send_sem=send_sem, recv_sem=recv_sem,
        device_id=peer, device_id_type=MESH,
    )
    copy.start()
    return copy


def normalize(values):
    row_mean = jnp.mean(values, axis=-1, keepdims=True)
    centered = values - row_mean
    inv_scale = lax.rsqrt(jnp.mean(centered * centered, axis=-1, keepdims=True) + epsilon)
    return (centered * inv_scale, inv_scale)


def norm_back(grad_normed, normed, inv_scale):
    return inv_scale * (
        grad_normed
        - jnp.mean(grad_normed, axis=-1, keepdims=True)
        - normed * jnp.mean(grad_normed * normed, axis=-1, keepdims=True)
    )


def dot(a, b):
    return jnp.dot(a, b, preferred_element_type=f32)


def dot_nt(a, b):
    return lax.dot_general(a, b, (((1,), (1,)), ((), ())), preferred_element_type=f32)


def dot_tn(a, b):
    return lax.dot_general(a, b, (((0,), (0,)), ((), ())), preferred_element_type=f32)


def lanes_of(shape):
    return lax.broadcasted_iota(jnp.int32, shape, 1)


def rows_of(shape):
    return lax.broadcasted_iota(jnp.int32, shape, 0)


def column(row):
    return jnp.transpose(jnp.broadcast_to(row.astype(f32), (128, row.shape[1])))[:, :1]


def one_hot_of(route):
    return jnp.where(lanes_of((route.shape[0], 128)).astype(f32) == route, 1.0, 0.0)


def choose_slots(route, spots, experts):
    seq_len = route.shape[0]
    capacity = (9 * seq_len + 8 * experts - 1) // (8 * experts)
    one_hot = one_hot_of(route)
    square = (seq_len, seq_len)
    before = jnp.where(lanes_of(square) < rows_of(square), 1.0, 0.0).astype(bf16)
    place = jnp.sum(dot(before, one_hot.astype(bf16)) * one_hot, axis=1, keepdims=True)
    slot = jnp.where(place < capacity, route * (spots // experts) + place, -1.0)
    return jnp.where(lanes_of((seq_len, spots)).astype(f32) == slot, 1.0, 0.0).astype(bf16)


def allowed_pairs(segment_row):
    square = (segment_row.shape[1],) * 2
    same = column(segment_row) == segment_row.astype(f32)
    return (lanes_of(square) <= rows_of(square)) & same


def begin_kernel(
    chips,
    experts,
    tokens,
    segments,
    routes,
    cotangent,
    shard_qkv,
    shard_out,
    shard_small,
    w_in,
    w_out,
    attn_in,
    qkv,
    lse,
    mixed,
    residual,
    hidden,
    probs,
    gains,
    kept_full,
    full_in,
    full_out,
    got_g,
    got_h,
    full,
    slots_g,
    slots_h,
    hold_in,
    hold_out,
    own_sem,
    sz,
    rz,
    sx,
    rx,
    sy,
    ry,
    sc,
    rc,
    sb,
    rb,
    sw,
    rw,
    lw,
    sd,
    rd,
    se,
    re,
    ld,
):
    block, chip, core, peer_x, peer_y, peer_core, peers_z = place_of(chips)
    owner = lax.axis_index("expert")
    micros, seq_len, model_width = tokens.shape
    rows = shard_qkv.shape[0]
    width = full.shape[1]
    cut = width // 128 * 5 // 8 * 128
    every = pl.ds(0, width)
    inner = width // 128 * 5 // 6 * 128
    cut_in = inner // 256 * 128
    outer = pl.ds(inner, width - inner)
    halves_of = [(pl.ds(0, cut), pl.ds(cut, width - cut))]
    halves_of += [(pl.ds(0, cut_in), pl.ds(cut_in, inner - cut_in))] * (chips - 1)
    half = w_in.shape[1] // 2
    row_y, row_x = block // 2, block % 2

    def part(origin, step, columns):
        start = ((flip(block, origin) * chips + flip(chip, step)) * 2 + core) * rows
        return full.at[pl.ds(pl.multiple_of(start, rows), rows), columns]

    own_copies = []
    for i, (src, at) in enumerate(
        ((shard_qkv, 0), (shard_out, 3 * model_width), (shard_small, 4 * model_width))
    ):
        dst = part(0, 0, pl.ds(at, src.shape[1]))
        own_copies.append(pltpu.make_async_copy(src, dst, own_sem.at[i]))
        own_copies[-1].start()
    others = [{"expert": lax.rem(owner + k, experts)} for k in range(1, experts)]
    greet([peer_x, peer_y] + others)
    for copy in own_copies:
        copy.wait()

    mine = part(0, 0, every)
    along_z = [None] + [send(mine, mine, sz.at[k], rz.at[k], peers_z[k]) for k in range(1, chips)]
    along_x = [[None] * 3 for _ in range(chips)]
    along_y = [[None] * 3 for _ in range(chips)]
    across = [[None] * 8 for _ in range(chips)]
    along_b = [[None] * 4 for _ in range(chips)]

    def to_core(k, origin, columns, tail=0):
        piece = part(origin, k, columns)
        at = (k, origin + 4 * tail)
        across[k][at[1]] = send(piece, piece, sc.at[at], rc.at[at], peer_core)

    def to_chips(origin):
        piece = part(origin, 0, outer)
        for k in range(1, chips):
            along_b[k][origin] = send(
                piece, piece, sb.at[k, origin], rb.at[k, origin], peers_z[k]
            )

    def pass_on(k):
        columns = pl.ds(0, inner) if k else every
        along_x[k][1].wait_recv()
        if k == 0:
            to_chips(1)
        to_core(k, 1, columns)
        along_y[k][1].wait_recv()
        to_core(k, 2, columns)
        along_x[k][2].wait_recv()
        if k == 0:
            to_chips(3)
        along_y[k][2].wait_recv()
        to_core(k, 3, columns)

    def spread(k):
        for turn in range(2):
            for copies, s, r, peer, side in (
                (along_x, sx, rx, peer_x, turn),
                (along_y, sy, ry, peer_y, 1 - turn),
            ):
                piece = part(0, k, halves_of[k][side])
                copies[k][turn] = send(piece, piece, s.at[k, turn], r.at[k, turn], peer)
        to_core(k, 0, every)

    def turn_corner(k):
        along_x[k][0].wait_recv()
        piece = part(1, k, halves_of[k][0])
        along_y[k][2] = send(piece, piece, sy.at[k, 2], ry.at[k, 2], peer_y)
        along_y[k][0].wait_recv()
        if k == 0:
            to_chips(2)
        piece = part(2, k, halves_of[k][1])
        along_x[k][2] = send(piece, piece, sx.at[k, 2], rx.at[k, 2], peer_x)

    piece_rows = w_out.shape[0] // pieces
    out_x = []

    def send_piece():
        j = len(out_x)
        at = pl.ds(j * piece_rows, piece_rows)
        out_x.append(
            send(w_out.at[at], full_out.at[row_x, at], sw.at[3 + j], rw.at[3 + j], peer_x)
        )

    from_y = []

    def send_strip():
        j = len(from_y)
        size = w_in.shape[0] // pieces
        at = pl.ds(j * size, size)
        from_y.append(
            send(
                w_in.at[at, pl.ds((1 - row_y) * half, half)],
                full_in.at[block, at],
                sw.at[3 + pieces + j], rw.at[3 + pieces + j], peer_y,
            )
        )

    spread(0)

    def put_slots(slots, m, values):
        packed = dot_tn(choose_slots(column(routes[m]), experts * slots.shape[2], experts), values)
        packed = packed.astype(bf16)
        for e in range(experts):
            size = slots.shape[2]
            slots[m, e] = packed[e * size : (e + 1) * size]

    for m in range(micros):
        put_slots(slots_g, m, cotangent[m])

    for k in range(chips):
        if k:
            along_z[k].wait_recv()
            spread(k)
            pass_on(k - 1)
        turn_corner(k)
        if k < pieces // 2:
            send_piece()
            send_strip()

    local_in = pltpu.make_async_copy(w_in.at[:, pl.ds(row_y * half, half)], hold_in, lw.at[0])
    local_out = pltpu.make_async_copy(w_out, hold_out, lw.at[1])
    local_in.start()
    local_out.start()
    while len(from_y) < pieces:
        send_strip()
    from_x = send(
        w_in.at[:, pl.ds(row_y * half, half)], full_in.at[block], sw.at[1], rw.at[1], peer_x
    )
    while len(out_x) < pieces:
        send_piece()

    def slot_copies(way, slots, got, m):
        def to_owner(k):
            peer = lax.rem(owner + k, experts)
            return pltpu.make_async_remote_copy(
                src_ref=slots.at[m, peer],
                dst_ref=got.at[m, 0, owner],
                send_sem=sd.at[way, m, k],
                recv_sem=rd.at[way, m, k],
                device_id={"expert": peer},
                device_id_type=MESH,
            )

        def to_y(k):
            origin = lax.rem(owner - k + experts, experts)
            return pltpu.make_async_remote_copy(
                src_ref=got.at[m, 0, origin],
                dst_ref=got.at[m, 1, origin],
                send_sem=se.at[way, m, k],
                recv_sem=re.at[way, m, k],
                device_id=peer_y,
                device_id_type=MESH,
            )

        own = pltpu.make_async_copy(slots.at[m, owner], got.at[m, 0, owner], ld.at[way, m])
        return to_owner, to_y, own

    def start_slots(way, slots, got, m):
        to_owner, to_y, own = slot_copies(way, slots, got, m)
        own.start()

        @pl.loop(1, experts)
        def _(k):
            to_owner(k).start()

    def relay_slots(way, slots, got, m):
        to_owner, to_y, own = slot_copies(way, slots, got, m)
        own.wait()
        to_y(0).start()

        @pl.loop(1, experts)
        def _(k):
            to_owner(k).wait_recv()
            to_y(k).start()

    def end_slots(way, slots, got, m):
        to_owner, to_y, own = slot_copies(way, slots, got, m)

        @pl.loop(1, experts)
        def _(k):
            to_owner(k).wait_send()

        @pl.loop(0, experts)
        def _(k):
            to_y(k).wait()

    for m in range(micros):
        start_slots(0, slots_g, got_g, m)
    pass_on(chips - 1)
    for k in range(1, chips):
        for origin in range(1, 4):
            along_b[k][origin].wait_recv()
            to_core(k, origin, outer, 1)
    for k in range(chips):
        for copy in across[k]:
            if copy is not None:
                copy.wait_recv()
    keep = pltpu.make_async_copy(full, kept_full, own_sem.at[3])
    keep.start()
    small = jnp.transpose(full[:, pl.ds(4 * model_width, 128)].astype(f32))
    gains[...] = small[experts : experts + 2]
    local_in.wait()
    local_out.wait()
    store_in = pltpu.make_async_copy(hold_in, full_in.at[block], lw.at[0])
    store_out = pltpu.make_async_copy(hold_out, full_out.at[row_x], lw.at[1])
    store_in.start()
    store_out.start()

    scale = 1.0 / math.sqrt(model_width // HEADS)
    low_half = lanes_of((seq_len, 128)) < 64
    relay_slots(0, slots_g, got_g, 0)
    for m in range(micros):
        x = tokens[m].astype(f32)
        attn_in[m] = (normalize(x)[0] * gains[0:1, :]).astype(bf16)

        @pl.loop(0, 3 * model_width // 512)
        def _(j):
            at = pl.ds(pl.multiple_of(j * 512, 512), 512)
            qkv[m, :, at] = dot(attn_in[m], full[:, at]).astype(bf16)

        allowed = allowed_pairs(segments[m])
        lse[m] = jnp.zeros(lse.shape[1:], f32)

        @pl.loop(0, model_width // 128)
        def _(pair):
            at = pl.multiple_of(pair * 128, 128)
            query = qkv[m, :, pl.ds(at, 128)]
            key = qkv[m, :, pl.ds(model_width + at, 128)]
            value = qkv[m, :, pl.ds(2 * model_width + at, 128)]
            outs = []
            for side in range(2):
                here = low_half if side == 0 else jnp.logical_not(low_half)
                scores = dot_nt(jnp.where(here, query, 0.0).astype(bf16), key) * scale
                masked = jnp.where(allowed, scores, masked_value)
                top = jnp.max(masked, axis=1, keepdims=True)
                weight = jnp.exp(masked - top)
                norm = jnp.sum(weight, axis=1, keepdims=True)
                outs.append(dot((weight / norm).astype(bf16), value))
                head = lanes_of(lse.shape[1:]) == 2 * pair + side
                lse[m] = jnp.where(head, top + jnp.log(norm), lse[m])
            mixed[m, :, pl.ds(at, 128)] = jnp.where(low_half, outs[0], outs[1]).astype(bf16)

        y1 = x + dot(mixed[m], full[:, pl.ds(3 * model_width, model_width)])
        residual[m] = y1
        low = (normalize(y1)[0] * gains[1:2, :]).astype(bf16)
        hidden[m] = low
        put_slots(slots_h, m, low)
        start_slots(1, slots_h, got_h, m)
        logits = dot(low, full[:, pl.ds(4 * model_width, 128)])
        real = lanes_of(logits.shape) < experts
        logits = jnp.where(real, logits, masked_value)
        weight = jnp.where(real, jnp.exp(logits - jnp.max(logits, axis=1, keepdims=True)), 0.0)
        probs[m] = weight / jnp.sum(weight, axis=1, keepdims=True)
        if m + 1 < micros:
            relay_slots(0, slots_g, got_g, m + 1)
        if m:
            relay_slots(1, slots_h, got_h, m - 1)
    for copy in from_y:
        copy.wait_recv()
    piece = full_in.at[flip(block, 2)]
    diagonal = send(piece, piece, sw.at[2], rw.at[2], peer_x)
    relay_slots(1, slots_h, got_h, micros - 1)

    for m in range(micros):
        end_slots(0, slots_g, got_g, m)
        end_slots(1, slots_h, got_h, m)
    keep.wait()
    store_in.wait()
    store_out.wait()
    for copy in from_y:
        copy.wait_send()
    for copy in (from_x, diagonal, *out_x):
        copy.wait()
    for k in range(chips):
        if k:
            along_z[k].wait_send()
        for turn in range(3):
            along_x[k][turn].wait_send()
            along_y[k][turn].wait_send()
        for copy in across[k] + along_b[k]:
            if copy is not None:
                copy.wait_send()


def begin_layer(tokens, segments, routes, cotangent, shards, w_in, w_out, chips):
    experts = 2 * chips
    micros, seq_len, model_width = tokens.shape
    capacity = (9 * seq_len + 8 * experts - 1) // (8 * experts)
    padded = (capacity + 7) // 8 * 8
    width = 4 * model_width + 128
    rows, half = w_in.shape[0], w_in.shape[1] // 2
    shape = jax.ShapeDtypeStruct
    vmem, hbm = pl.BlockSpec(memory_space=pltpu.VMEM), pl.BlockSpec(memory_space=pl.ANY)
    spots = (micros, experts, padded, model_width)
    return pl.pallas_call(
        functools.partial(begin_kernel, chips, experts),
        out_shape=[
            shape((micros, seq_len, model_width), bf16),
            shape((micros, seq_len, 3 * model_width), bf16),
            shape((micros, seq_len, 128), f32),
            shape((micros, seq_len, model_width), bf16),
            shape((micros, seq_len, model_width), f32),
            shape((micros, seq_len, model_width), bf16),
            shape((micros, seq_len, 128), f32),
            shape((2, model_width), f32),
            shape((model_width, width), bf16),
            shape((4, rows, half), bf16),
            shape((2,) + w_out.shape, bf16),
            shape((micros, 2, experts, padded, model_width), bf16),
            shape((micros, 2, experts, padded, model_width), bf16),
        ],
        in_specs=[vmem] * 4 + [hbm] * 5,
        out_specs=[vmem] * 8 + [hbm] * 5,
        scratch_shapes=[
            pltpu.VMEM((model_width, width), bf16),
            pltpu.VMEM(spots, bf16),
            pltpu.VMEM(spots, bf16),
            pltpu.VMEM((rows, half), bf16),
            pltpu.VMEM(w_out.shape, bf16),
            DMA((4,)),
            DMA((chips,)),
            DMA((chips,)),
            DMA((chips, 3)),
            DMA((chips, 3)),
            DMA((chips, 3)),
            DMA((chips, 3)),
            DMA((chips, 8)),
            DMA((chips, 8)),
            DMA((chips, 4)),
            DMA((chips, 4)),
            DMA((3 + 2 * pieces,)),
            DMA((3 + 2 * pieces,)),
            DMA((2,)),
            DMA((2, micros, experts)),
            DMA((2, micros, experts)),
            DMA((2, micros, experts)),
            DMA((2, micros, experts)),
            DMA((2, micros)),
        ],
        compiler_params=pltpu.CompilerParams(
            collective_id=1, has_side_effects=True, vmem_limit_bytes=60 * 2**20
        ),
        name="begin_layer",
    )(tokens, segments, routes, cotangent, *shards, w_in, w_out)


def expert_kernel(
    chips,
    experts,
    got_h,
    got_g,
    w_in_hbm,
    w_out_hbm,
    full,
    returned,
    grad_back,
    keep_in,
    send_in,
    grad_out,
    x_buf,
    gz_buf,
    w_in,
    w_out,
    router,
    act,
    gu,
    own,
    part,
    part_got,
    out_part,
    out_got,
    out_stage,
    in_part,
    in_stage,
    load,
    sy,
    ry,
    sz,
    rz,
    lz,
    sx,
    rx,
    st,
):
    block, chip, core, peer_x, peer_y, peer_core, peers_z = place_of(chips)
    owner = lax.axis_index("expert")
    micros, rows, model_width = got_h.shape
    half = w_in.shape[1]
    mine = rows // 2
    padded = part.shape[3]
    row_x = block % 2
    step = 256
    backs = (returned, grad_back)

    sources = [
        (got_h.at[0], x_buf.at[pl.ds(0, rows)]),
        (w_in_hbm, w_in),
        (w_out_hbm, w_out),
        (full.at[:, pl.ds(4 * model_width, 128)], router),
        (got_g.at[0], gz_buf.at[pl.ds(0, rows)]),
        (got_h.at[1], x_buf.at[pl.ds(rows, rows)]),
        (got_g.at[1], gz_buf.at[pl.ds(rows, rows)]),
    ]
    loads = []
    for i, (src, dst) in enumerate(sources):
        loads.append(pltpu.make_async_copy(src, dst, load.at[i]))
        loads[-1].start()
    greet(
        [peer_x, peer_y]
        + [{"expert": lax.rem(owner + k, experts)} for k in range(1, experts)]
    )

    def of(m):
        return pl.ds(m * rows, rows)

    def gate_rows(m):
        logits = dot(x_buf[of(m), :], router[...])
        lanes = lanes_of(logits.shape)
        logits = jnp.where(lanes < experts, logits, masked_value)
        weight = jnp.exp(logits - jnp.max(logits, axis=1, keepdims=True))
        weight = jnp.where(lanes < experts, weight, 0.0)
        picked = jnp.sum(jnp.where(lanes == owner, weight, 0.0), axis=1, keepdims=True)
        gate = picked / jnp.sum(weight, axis=1, keepdims=True)
        gz_buf[of(m), :] = (gate * gz_buf[of(m), :].astype(f32)).astype(bf16)

    def open_rows(m, forward, backward):
        @pl.loop(0, half // step)
        def _(j):
            at = pl.ds(pl.multiple_of(j * step, step), step)
            u = dot(x_buf[of(m), :], w_in[:, at])
            root = math.sqrt(2.0 / math.pi)
            square = u * u
            bend = jnp.tanh(root * (u + 0.044715 * (u * square)))
            if forward:
                act[of(m), at] = (0.5 * u * (1.0 + bend)).astype(bf16)
            if backward:
                back = dot_nt(gz_buf[of(m), :], w_out[at, :])
                slope = 0.5 * (1.0 + bend) + 0.5 * u * (1.0 - bend * bend) * (
                    root * (1.0 + (3.0 * 0.044715) * square)
                )
                gu[of(m), at] = (back * slope).astype(bf16)

    wing = model_width // 2

    def columns(side):
        return pl.ds(pl.multiple_of(side * wing, wing), wing)

    def swap(m, way, side):
        return pltpu.make_async_remote_copy(
            src_ref=part.at[m, way, :, :, columns(side)],
            dst_ref=part_got.at[m, way, :, :, columns(side)],
            send_sem=sy.at[m, way, side],
            recv_sem=ry.at[m, way, side],
            device_id=peer_y,
            device_id_type=MESH,
        )

    def close_rows(m, way):
        @pl.loop(0, 2)
        def _(side):
            @pl.loop(0, wing // step)
            def _(j):
                at = pl.ds(pl.multiple_of(side * wing + j * step, step), step)
                if way == 0:
                    total = dot(act[of(m), :], w_out[:, at])
                else:
                    total = dot_nt(gu[of(m), :], w_in[at, :])
                own[m, way, :, at] = total[:mine]
                for e in range(experts):
                    start = mine + e * padded
                    part[m, way, e, :, at] = total[start : start + padded].astype(bf16)

            swap(m, way, side).start()

    def to_source(m, way, side, k):
        peer = lax.rem(owner + k, experts)
        return pltpu.make_async_remote_copy(
            src_ref=part.at[m, way, peer, :, columns(side)],
            dst_ref=backs[way].at[m, owner, :, columns(side)],
            send_sem=sz.at[m, way, side, k],
            recv_sem=rz.at[m, way, side, k],
            device_id={"expert": peer},
            device_id_type=MESH,
        )

    def to_self(m, way, side):
        return pltpu.make_async_copy(
            part.at[m, way, owner, :, columns(side)],
            backs[way].at[m, owner, :, columns(side)],
            lz.at[m, way, side],
        )

    def give_back(m, way, side):
        swap(m, way, side).wait()

        @pl.loop(0, experts)
        def _(e):
            at = pl.ds(pl.multiple_of(e * padded, padded), padded)
            cols = columns(side)
            total = own[m, way, at, cols] + part_got[m, way, e, :, cols].astype(f32)
            part[m, way, e, :, cols] = total.astype(bf16)

        to_self(m, way, side).start()

        @pl.loop(1, experts)
        def _(k):
            to_source(m, way, side, k).start()

    def end_back(m, way, side):
        to_self(m, way, side).wait()

        @pl.loop(1, experts)
        def _(k):
            to_source(m, way, side, k).wait()

    chunks = out_part.shape[0]

    def out_rows(side, j):
        start = side * (half // 2) + j * step
        return dot_tn(act[:, pl.ds(pl.multiple_of(start, step), step)], gz_buf[...])

    def to_x(j):
        return pltpu.make_async_remote_copy(
            src_ref=out_part.at[j],
            dst_ref=out_got.at[j],
            send_sem=sx.at[j],
            recv_sem=rx.at[j],
            device_id=peer_x,
            device_id_type=MESH,
        )

    def put_out(j, slot):
        return pltpu.make_async_copy(out_stage.at[slot], grad_out.at[j], st.at[slot])

    def send_out_rows():
        @pl.loop(0, chunks)
        def _(j):
            out_part[j] = out_rows(1 - row_x, j).astype(bf16)
            to_x(j).start()

    def keep_out_rows():
        for j in range(chunks):
            if j > 1:
                put_out(j - 2, j % 2).wait()
            to_x(j).wait()
            out_stage[j % 2] = out_rows(row_x, j) + out_got[j].astype(f32)
            put_out(j, j % 2).start()

    quarter = in_stage.shape[0]

    def in_rows(y, x):
        start = (2 * y + x) * quarter
        return pl.ds(pl.multiple_of(start, quarter), quarter)

    def in_copies(y):
        return (
            pltpu.make_async_copy(in_part, send_in.at[y], st.at[2]),
            pltpu.make_async_copy(in_stage, keep_in.at[y], st.at[3]),
        )

    def first_rows():
        for y in range(2):
            for kind in range(2):
                if y:
                    in_copies(0)[kind].wait()
                cols = in_rows(y, 1 - row_x if kind == 0 else row_x)

                @pl.loop(0, half // (2 * step))
                def _(j):
                    at = pl.ds(pl.multiple_of(j * 2 * step, 2 * step), 2 * step)
                    value = dot_tn(x_buf[:, cols], gu[:, at])
                    if kind == 0:
                        in_part[:, at] = value.astype(bf16)
                    else:
                        in_stage[:, at] = value

                in_copies(y)[kind].start()

    loads[0].wait()
    loads[1].wait()
    open_rows(0, True, False)
    loads[2].wait()
    close_rows(0, 0)
    loads[5].wait()
    open_rows(1, True, False)
    close_rows(1, 0)
    give_back(0, 0, 0)
    for i in (3, 4, 6):
        loads[i].wait()
    gate_rows(0)
    gate_rows(1)
    give_back(0, 0, 1)
    send_out_rows()
    give_back(1, 0, 0)
    open_rows(0, False, True)
    give_back(1, 0, 1)
    close_rows(0, 1)
    open_rows(1, False, True)
    give_back(0, 1, 0)
    close_rows(1, 1)
    give_back(0, 1, 1)
    first_rows()
    give_back(1, 1, 0)
    give_back(1, 1, 1)
    keep_out_rows()
    for j in range(chunks - 2, chunks):
        put_out(j, j % 2).wait()
    for copy in in_copies(1):
        copy.wait()
    for m in range(micros):
        for way in range(2):
            end_back(m, way, 0)
            end_back(m, way, 1)


def run_experts(got_h, got_g, w_in, w_out, full, chips):
    experts = 2 * chips
    micros, _, _, padded, model_width = got_h.shape
    rows = 2 * experts * padded
    half = w_in.shape[1]
    shape = jax.ShapeDtypeStruct
    hbm = pl.BlockSpec(memory_space=pl.ANY)
    slots = shape((micros, experts, padded, model_width), bf16)
    chunks = half // 2 // 256
    quarter = model_width // 4
    spots = (micros, 2, experts, padded, model_width)
    return pl.pallas_call(
        functools.partial(expert_kernel, chips, experts),
        out_shape=[
            slots,
            slots,
            shape((2, quarter, half), f32),
            shape((2, quarter, half), bf16),
            shape((chunks, 256, model_width), f32),
        ],
        in_specs=[hbm] * 5,
        out_specs=[hbm] * 5,
        scratch_shapes=[
            pltpu.VMEM((micros * rows, model_width), bf16),
            pltpu.VMEM((micros * rows, model_width), bf16),
            pltpu.VMEM((model_width, half), bf16),
            pltpu.VMEM((half, model_width), bf16),
            pltpu.VMEM((model_width, 128), bf16),
            pltpu.VMEM((micros * rows, half), bf16),
            pltpu.VMEM((micros * rows, half), bf16),
            pltpu.VMEM((micros, 2, rows // 2, model_width), f32),
            pltpu.VMEM(spots, bf16),
            pltpu.VMEM(spots, bf16),
            pltpu.VMEM((chunks, 256, model_width), bf16),
            pltpu.VMEM((chunks, 256, model_width), bf16),
            pltpu.VMEM((2, 256, model_width), f32),
            pltpu.VMEM((quarter, half), bf16),
            pltpu.VMEM((quarter, half), f32),
            DMA((7,)),
            DMA((micros, 2, 2)),
            DMA((micros, 2, 2)),
            DMA((micros, 2, 2, experts)),
            DMA((micros, 2, 2, experts)),
            DMA((micros, 2, 2)),
            DMA((chunks,)),
            DMA((chunks,)),
            DMA((4,)),
        ],
        compiler_params=pltpu.CompilerParams(
            collective_id=3, has_side_effects=True, vmem_limit_bytes=63 * 2**20
        ),
        name="run_experts",
    )(
        got_h.reshape(micros, rows, model_width),
        got_g.reshape(micros, rows, model_width),
        w_in,
        w_out,
        full,
    )


def end_kernel(
    chips,
    experts,
    cut,
    segments,
    routes,
    gains,
    lse,
    probs,
    tokens,
    cotangent,
    qkv_hbm,
    y1_hbm,
    returned_hbm,
    back_hbm,
    attn_hbm,
    mixed_hbm,
    hidden_hbm,
    full_hbm,
    send_in,
    keep_in,
    grad_qkv,
    grad_out,
    grad_small,
    output,
    grad_x,
    grad_in,
    full,
    x_buf,
    g_buf,
    qkv,
    y1_buf,
    returned,
    back,
    attn_in,
    mixed,
    hidden,
    out_buf,
    gx_buf,
    branch,
    gqkv,
    glog_buf,
    go_buf,
    gain_rows,
    grads,
    crecv,
    xrecv,
    yrecv,
    part_z,
    zrecv,
    brecv,
    got_in,
    got_y,
    keep,
    load,
    load_m,
    put,
    si,
    ri,
    siy,
    riy,
    sc,
    rc,
    sx,
    rx,
    sy,
    ry,
    sz,
    rz,
    sb,
    rb,
):
    block, chip, core, peer_x, peer_y, peer_core, peers_z = place_of(chips)
    micros, seq_len, model_width = tokens.shape
    width = full.shape[1]
    row_y = block // 2
    opposite = flip(core, 1)
    wide_qkv = 3 * model_width

    late = pl.ds(wide_qkv, width - wide_qkv)
    early = pl.ds(0, wide_qkv)
    once = [
        (full_hbm.at[:, late], full.at[:, late]),
        (full_hbm.at[:, early], full.at[:, early]),
        (keep_in.at[1 - row_y], keep.at[0]),
        (keep_in.at[row_y], keep.at[1]),
        (attn_hbm, attn_in),
        (mixed_hbm, mixed),
        (hidden_hbm, hidden),
    ]
    once = [pltpu.make_async_copy(src, dst, load.at[i]) for i, (src, dst) in enumerate(once)]
    pairs = (
        (returned_hbm, returned),
        (back_hbm, back),
        (cotangent, g_buf),
        (y1_hbm, y1_buf),
        (qkv_hbm, qkv),
        (tokens, x_buf),
    )

    def load_of(i, m):
        src, dst = pairs[i]
        return pltpu.make_async_copy(src.at[m], dst.at[m], load_m.at[i, m])

    once[0].start()
    for i in range(len(pairs)):
        load_of(i, 0).start()
    once[1].start()
    for i in range(len(pairs)):
        load_of(i, 1).start()
    for copy in once[2:]:
        copy.start()

    greet([peer_x, peer_y, peer_core] + peers_z[1:])

    def in_x(j):
        return pltpu.make_async_remote_copy(
            src_ref=send_in.at[1 - row_y if j == 0 else row_y],
            dst_ref=got_in.at[j],
            send_sem=si.at[j],
            recv_sem=ri.at[j],
            device_id=peer_x,
            device_id_type=MESH,
        )

    in_y = pltpu.make_async_remote_copy(
        src_ref=got_in.at[0],
        dst_ref=got_y,
        send_sem=siy,
        recv_sem=riy,
        device_id=peer_y,
        device_id_type=MESH,
    )
    in_x(0).start()
    in_x(1).start()
    strip = 32

    def pass_in_y():
        once[2].wait()
        in_x(0).wait()

        @pl.loop(0, keep.shape[1] // strip)
        def _(j):
            at = pl.ds(pl.multiple_of(j * strip, strip), strip)
            got_in[0, at, :] = (keep[0, at, :] + got_in[0, at, :].astype(f32)).astype(bf16)

        in_y.start()

    def put_in(slot, side):
        half = keep.shape[2]
        cols = pl.ds(pl.multiple_of(side * half, half), half)
        copy = pltpu.make_async_copy(keep.at[slot], grad_in.at[:, cols], put.at[2, slot])
        copy.start()
        return copy

    def end_in():
        once[3].wait()
        in_x(1).wait()

        @pl.loop(0, keep.shape[1] // strip)
        def _(j):
            at = pl.ds(pl.multiple_of(j * strip, strip), strip)
            keep[1, at, :] = keep[1, at, :] + got_in[1, at, :].astype(f32)

        stored = [put_in(1, row_y)]
        in_y.wait()

        @pl.loop(0, keep.shape[1] // strip)
        def _(j):
            at = pl.ds(pl.multiple_of(j * strip, strip), strip)
            keep[0, at, :] = got_y[at, :].astype(f32)

        return stored + [put_in(0, 1 - row_y)]

    def put_out(m):
        return pltpu.make_async_copy(out_buf.at[m], output.at[m], put.at[0, m])

    def put_x(m):
        return pltpu.make_async_copy(gx_buf.at[m], grad_x.at[m], put.at[1, m])

    gain_rows[...] = jnp.zeros(gain_rows.shape, f32)
    scale = 1.0 / math.sqrt(model_width // HEADS)
    low_half = lanes_of((seq_len, 128)) < 64
    once[0].wait()

    @pl.loop(0, micros)
    def _(m):
        here = pl.ds(pl.multiple_of(m * seq_len, seq_len), seq_len)
        for i in range(4):
            load_of(i, m).wait()
        g = g_buf[m].astype(f32)
        route = column(routes[m])
        chosen = choose_slots(route, returned.shape[1], experts)
        moe = dot(chosen, returned[m])
        prob = probs[m]
        one_hot = one_hot_of(route)
        gate = jnp.sum(prob * one_hot, axis=1, keepdims=True)
        y1 = y1_buf[m]
        out_buf[m] = (y1 + gate * moe).astype(bf16)
        put_out(m).start()
        choice = one_hot * jnp.sum(g * moe, axis=1, keepdims=True)
        glog = (prob * (choice - jnp.sum(prob * choice, axis=1, keepdims=True))).astype(bf16)
        glog_buf[here, :] = glog
        grad_h = dot(chosen, back[m]) + dot_nt(glog, full[:, pl.ds(4 * model_width, 128)])
        n2, inv2 = normalize(y1)
        gain_rows[experts + 1 : experts + 2, :] += jnp.sum(grad_h * n2, axis=0, keepdims=True)
        gy1 = g + norm_back(grad_h * gains[1:2, :], n2, inv2)
        gx_buf[m] = gy1
        branch[here, :] = gy1.astype(bf16)
        go_buf[...] = dot_nt(branch[here, :], full[:, pl.ds(wide_qkv, model_width)]).astype(bf16)
        load_of(4, m).wait()
        load_of(5, m).wait()

        allowed = allowed_pairs(segments[m])

        @pl.loop(0, model_width // 128)
        def _(pair):
            @pl.when((m == 1) & (pair == 4))
            def _():
                pass_in_y()

            at = pl.multiple_of(pair * 128, 128)
            query = qkv[m, :, pl.ds(at, 128)]
            key = qkv[m, :, pl.ds(model_width + at, 128)]
            value = qkv[m, :, pl.ds(2 * model_width + at, 128)]
            grad_o = go_buf[:, pl.ds(at, 128)]
            parts = []
            for side in range(2):
                mine = low_half if side == 0 else jnp.logical_not(low_half)
                scores = dot_nt(jnp.where(mine, query, 0.0).astype(bf16), key) * scale
                head = lanes_of(lse.shape[1:]) == 2 * pair + side
                top = jnp.sum(jnp.where(head, lse[m], 0.0), axis=1, keepdims=True)
                p = jnp.exp(jnp.where(allowed, scores, masked_value) - top)
                gp = dot_nt(jnp.where(mine, grad_o, 0.0).astype(bf16), value)
                gs = (p * (gp - jnp.sum(p * gp, axis=1, keepdims=True))).astype(bf16)
                parts.append(
                    (dot(gs, key) * scale, dot_tn(gs, query) * scale, dot_tn(p.astype(bf16), grad_o))
                )
            for i in range(3):
                both = jnp.where(low_half, parts[0][i], parts[1][i]).astype(bf16)
                gqkv[here, pl.ds(i * model_width + at, 128)] = both

        @pl.when(m == 0)
        def _():
            once[1].wait()

        ga = dot_nt(gqkv[here, :], full[:, pl.ds(0, wide_qkv)])
        n1, inv1 = normalize(x_buf[m].astype(f32))
        gain_rows[experts : experts + 1, :] += jnp.sum(ga * n1, axis=0, keepdims=True)
        gx_buf[m] = gx_buf[m] + norm_back(ga * gains[0:1, :], n1, inv1)
        put_x(m).start()

    for copy in once[4:]:
        copy.wait()
    rows = grads.shape[3]
    span = model_width // 4

    def to_core(b):
        return pltpu.make_async_remote_copy(
            src_ref=grads.at[b, :, opposite],
            dst_ref=crecv.at[b],
            send_sem=sc.at[b],
            recv_sem=rc.at[b],
            device_id=peer_core,
            device_id_type=MESH,
        )

    @pl.loop(0, 4)
    def _(b):
        cols = pl.ds(pl.multiple_of(b * span, span), span)

        def store(start, value):
            value = value.reshape(chips, 2, rows, value.shape[1]).astype(bf16)
            grads[b, :, :, :, pl.ds(start, value.shape[3])] = value

        @pl.loop(0, wide_qkv // 512)
        def _(j):
            start = pl.multiple_of(j * 512, 512)
            store(start, dot_tn(attn_in[:, cols], gqkv[:, pl.ds(start, 512)]))

        store(wide_qkv, dot_tn(mixed[:, cols], branch[...]))
        small = dot_tn(hidden[:, cols], glog_buf[...]) + jnp.transpose(gain_rows[:, cols])
        store(4 * model_width, small)
        to_core(b).start()

    inner = width - brecv.shape[3]
    outer = pl.ds(inner, width - inner)
    order = list(range(chips - 1, -1, -1))
    along_x, along_y, along_z, along_b = {}, {}, {}, {}

    def halves_of(k):
        low, end = (inner // 256 * 128, inner) if k else (cut, width)
        return pl.ds(0, low), pl.ds(low, end - low), pl.ds(0, end - low)

    def spot(k, origin, cols):
        return (flip(block, origin), flip(chip, k), core, slice(None), cols)

    def add_core(k, origin, cols):
        at = spot(k, origin, cols)
        return grads[at].astype(f32) + crecv[at[:2] + at[3:]].astype(f32)

    def begin_outer(k):
        for origin in range(4):
            at = spot(k, origin, outer)
            grads[at] = add_core(k, origin, outer).astype(bf16)
            along_b[k, origin] = send(
                grads.at[at], brecv.at[k, origin], sb.at[k, origin], rb.at[k, origin], peers_z[k]
            )

    def begin(k):
        left, right, short = halves_of(k)
        for origin in (3, 1, 2, 0):
            at = spot(k, origin, pl.ds(0, inner))
            grads[at] = add_core(k, origin, pl.ds(0, inner)).astype(bf16)
            if k == 0:
                total = add_core(0, origin, outer)
                for j in range(1, chips):
                    along_b[j, origin].wait_recv()
                    total = total + brecv[j, origin].astype(f32)
                grads[spot(0, origin, outer)] = total.astype(bf16)
            if origin == 3:
                along_x[k, 0] = send(
                    grads.at[spot(k, 3, left)], xrecv.at[k, 0, :, left], sx.at[k, 0], rx.at[k, 0], peer_x
                )
                along_y[k, 0] = send(
                    grads.at[spot(k, 3, right)], yrecv.at[k, 0, :, short], sy.at[k, 0], ry.at[k, 0], peer_y
                )
            if origin == 1:
                along_x[k, 1] = send(
                    grads.at[spot(k, 1, left)], xrecv.at[k, 1, :, left], sx.at[k, 1], rx.at[k, 1], peer_x
                )
            if origin == 2:
                along_y[k, 1] = send(
                    grads.at[spot(k, 2, right)], yrecv.at[k, 1, :, short], sy.at[k, 1], ry.at[k, 1], peer_y
                )

    def relay(k):
        left, right, short = halves_of(k)
        along_x[k, 0].wait_recv()
        at = spot(k, 2, left)
        grads[at] = (grads[at].astype(f32) + xrecv[k, 0, :, left].astype(f32)).astype(bf16)
        along_y[k, 2] = send(grads.at[at], yrecv.at[k, 2, :, left], sy.at[k, 2], ry.at[k, 2], peer_y)
        along_y[k, 0].wait_recv()
        at = spot(k, 1, right)
        grads[at] = (grads[at].astype(f32) + yrecv[k, 0, :, short].astype(f32)).astype(bf16)
        along_x[k, 2] = send(
            grads.at[at], xrecv.at[k, 2, :, short], sx.at[k, 2], rx.at[k, 2], peer_x
        )

    def finish(k):
        left, right, short = halves_of(k)
        for turn in (1, 2):
            along_x[k, turn].wait_recv()
            along_y[k, turn].wait_recv()
        lhs = (
            grads[spot(k, 0, left)].astype(f32)
            + xrecv[k, 1, :, left].astype(f32)
            + yrecv[k, 2, :, left].astype(f32)
        )
        rhs = (
            grads[spot(k, 0, right)].astype(f32)
            + yrecv[k, 1, :, short].astype(f32)
            + xrecv[k, 2, :, short].astype(f32)
        )
        if k:
            part_z[k, :, left] = lhs.astype(bf16)
            part_z[k, :, right] = rhs.astype(bf16)
            cols = pl.ds(0, inner)
            along_z[k] = send(
                part_z.at[k, :, cols], zrecv.at[k, :, cols], sz.at[k], rz.at[k], peers_z[k]
            )
        else:
            middle, rhs = rhs[:, : inner - cut], rhs[:, inner - cut :]
            for j in range(1, chips):
                along_z[j].wait_recv()
                lhs = lhs + zrecv[j, :, left].astype(f32)
                middle = middle + zrecv[j, :, pl.ds(cut, inner - cut)].astype(f32)
            start = 0
            for out in (grad_qkv, grad_out, grad_small):
                w = out.shape[1]
                for lo, hi, value in ((0, cut, lhs), (cut, inner, middle), (inner, width, rhs)):
                    a, b = max(start, lo), min(start + w, hi)
                    if a < b:
                        out[:, a - start : b - start] = value[:, a - lo : b - lo]
                start += w

    @pl.loop(0, 4)
    def _(b):
        to_core(b).wait()

    for k in order[:-1]:
        begin_outer(k)
    stored = None
    for i in range(chips + 2):
        if i < chips:
            begin(order[i])
        if 0 <= i - 1 < chips:
            relay(order[i - 1])
        if i == chips:
            stored = end_in()
        if i - 2 >= 0:
            finish(order[i - 2])
    for k in order:
        for turn in range(3):
            along_x[k, turn].wait_send()
            along_y[k, turn].wait_send()
        if k:
            along_z[k].wait_send()
            for origin in range(4):
                along_b[k, origin].wait_send()
    for copy in stored:
        copy.wait()
    for m in range(micros):
        put_out(m).wait()
        put_x(m).wait()


def end_layer(small_inputs, big_inputs, chips):
    tokens, keep_in, full = big_inputs[0], big_inputs[-1], big_inputs[9]
    experts = 2 * chips
    micros, seq_len, model_width = tokens.shape
    spots = big_inputs[4].shape[1]
    width = full.shape[1]
    rows = model_width // (8 * chips)
    cut = (width // 128 + 1) // 2 * 128
    quarter, half = keep_in.shape[1:]
    every = micros * seq_len
    shape = jax.ShapeDtypeStruct
    vmem, hbm = pl.BlockSpec(memory_space=pltpu.VMEM), pl.BlockSpec(memory_space=pl.ANY)
    tall = (micros, seq_len, model_width)
    return pl.pallas_call(
        functools.partial(end_kernel, chips, experts, cut),
        out_shape=[
            shape((rows, 3 * model_width), f32),
            shape((rows, model_width), f32),
            shape((rows, 128), f32),
            shape(tall, bf16),
            shape(tall, f32),
            shape((quarter, 2 * half), f32),
        ],
        in_specs=[vmem] * len(small_inputs) + [hbm] * len(big_inputs),
        out_specs=[vmem] * 3 + [hbm] * 3,
        scratch_shapes=[
            pltpu.VMEM((model_width, width), bf16),
            pltpu.VMEM(tall, bf16),
            pltpu.VMEM(tall, bf16),
            pltpu.VMEM((micros, seq_len, 3 * model_width), bf16),
            pltpu.VMEM(tall, f32),
            pltpu.VMEM((micros, spots, model_width), bf16),
            pltpu.VMEM((micros, spots, model_width), bf16),
            pltpu.VMEM((every, model_width), bf16),
            pltpu.VMEM((every, model_width), bf16),
            pltpu.VMEM((every, model_width), bf16),
            pltpu.VMEM(tall, bf16),
            pltpu.VMEM(tall, f32),
            pltpu.VMEM((every, model_width), bf16),
            pltpu.VMEM((every, 3 * model_width), bf16),
            pltpu.VMEM((every, 128), bf16),
            pltpu.VMEM((seq_len, model_width), bf16),
            pltpu.VMEM((128, model_width), f32),
            pltpu.VMEM((4, chips, 2, rows, width), bf16),
            pltpu.VMEM((4, chips, rows, width), bf16),
            pltpu.VMEM((chips, 3, rows, cut), bf16),
            pltpu.VMEM((chips, 3, rows, cut), bf16),
            pltpu.VMEM((chips, rows, width), bf16),
            pltpu.VMEM((chips, rows, width), bf16),
            pltpu.VMEM((chips, 4, rows, width // 512 * 128), bf16),
            pltpu.VMEM((2, quarter, half), bf16),
            pltpu.VMEM((quarter, half), bf16),
            pltpu.VMEM((2, quarter, half), f32),
            DMA((7,)),
            DMA((6, micros)),
            DMA((3, micros)),
            DMA((2,)),
            DMA((2,)),
            DMA(()),
            DMA(()),
            DMA((4,)),
            DMA((4,)),
            DMA((chips, 3)),
            DMA((chips, 3)),
            DMA((chips, 3)),
            DMA((chips, 3)),
            DMA((chips,)),
            DMA((chips,)),
            DMA((chips, 4)),
            DMA((chips, 4)),
        ],
        compiler_params=pltpu.CompilerParams(
            collective_id=2, has_side_effects=True, vmem_limit_bytes=63 * 2**20
        ),
        name="end_layer",
    )(*small_inputs, *big_inputs)


def on_device(
    tokens,
    segment_ids,
    routes,
    cotangent,
    w_qkv,
    w_attn_out,
    w_router,
    gain_attn,
    gain_moe,
    w_expert_in,
    w_expert_out,
):
    micro_count, _, seq_len, model_width = tokens.shape
    experts = w_router.shape[1]
    chips = model_width // w_qkv.shape[0] // 8

    spare = jnp.zeros((w_qkv.shape[0], 128 - 2 - experts), bf16)
    small = jnp.concatenate([w_router, gain_attn[:, None], gain_moe[:, None], spare], axis=1)
    tokens, cotangent, segment_ids = tokens[:, 0], cotangent[:, 0], segment_ids
    routes = routes.reshape(micro_count, 1, seq_len)
    attn_in, qkv, lse, mixed, residual, hidden, probs, gains, gathered, w_in, w_out, got_g, got_h = (
        begin_layer(
            tokens,
            segment_ids,
            routes,
            cotangent,
            (w_qkv, w_attn_out, small),
            w_expert_in[0],
            w_expert_out[0],
            chips,
        )
    )
    returned, grad_back, keep_in, send_in, grad_out = run_experts(
        got_h,
        got_g,
        w_in.reshape(model_width, -1),
        w_out.reshape(-1, model_width),
        gathered,
        chips,
    )
    flat = (micro_count, -1, model_width)
    grad_qkv, grad_attn_out, small_sum, output, grad_tokens, grad_in = end_layer(
        (segment_ids, routes, gains, lse, probs),
        (
            tokens,
            cotangent,
            qkv,
            residual,
            returned.reshape(flat),
            grad_back.reshape(flat),
            attn_in.reshape(-1, model_width),
            mixed.reshape(-1, model_width),
            hidden.reshape(-1, model_width),
            gathered,
            send_in,
            keep_in,
        ),
        chips,
    )
    return (
        output[:, None],
        grad_tokens[:, None],
        grad_qkv,
        grad_attn_out,
        small_sum[:, :experts],
        small_sum[:, experts],
        small_sum[:, experts + 1],
        grad_in[None],
        grad_out.reshape(1, -1, model_width),
    )


def solution(mesh):
    rows = P(("dp", "expert"))
    seqs = P(None, ("dp", "expert"))
    owned = P("expert", "dp", None)
    return jax.shard_map(
        on_device,
        mesh=mesh,
        in_specs=(seqs, seqs, seqs, seqs, rows, rows, rows, rows, rows, owned, owned),
        out_specs=(seqs, seqs, rows, rows, rows, rows, rows, owned, owned),
        check_vma=False,
    )
```

```python
import functools
import math

import jax
import jax.numpy as jnp
from jax import lax
from jax.experimental import pallas as pl
from jax.experimental.pallas import tpu as pltpu
from jax.sharding import PartitionSpec as P

HEADS = 16
epsilon = 1e-05
masked_value = -1e30
pieces = 8
f32 = jnp.float32
bf16 = jnp.bfloat16

MESH = pl.DeviceIdType.MESH
DMA = pltpu.SemaphoreType.DMA


def flip(index, mask):
    bit = 1
    while bit <= mask:
        if mask & bit:
            index = index + bit - 2 * bit * ((index // bit) % 2)
        bit *= 2
    return index


def place_of(chips):
    block = lax.axis_index("dp")
    owner = lax.axis_index("expert")
    peer_x = {"dp": flip(block, 1)}
    peer_y = {"dp": flip(block, 2)}
    peer_core = {"expert": flip(owner, 1)}
    peers_z = [{"expert": flip(owner, 2 * k)} for k in range(chips)]
    return block, owner // 2, owner % 2, peer_x, peer_y, peer_core, peers_z


def greet(peers):
    barrier = pltpu.get_barrier_semaphore()
    for peer in peers:
        pl.semaphore_signal(barrier, inc=1, device_id=peer, device_id_type=MESH)
    pl.semaphore_wait(barrier, len(peers))


def send(src, dst, send_sem, recv_sem, peer):
    copy = pltpu.make_async_remote_copy(
        src_ref=src, dst_ref=dst, send_sem=send_sem, recv_sem=recv_sem,
        device_id=peer, device_id_type=MESH,
    )
    copy.start()
    return copy


def normalize(values):
    row_mean = jnp.mean(values, axis=-1, keepdims=True)
    centered = values - row_mean
    inv_scale = lax.rsqrt(jnp.mean(centered * centered, axis=-1, keepdims=True) + epsilon)
    return (centered * inv_scale, inv_scale)


def norm_back(grad_normed, normed, inv_scale):
    return inv_scale * (
        grad_normed
        - jnp.mean(grad_normed, axis=-1, keepdims=True)
        - normed * jnp.mean(grad_normed * normed, axis=-1, keepdims=True)
    )


def dot(a, b):
    return jnp.dot(a, b, preferred_element_type=f32)


def dot_nt(a, b):
    return lax.dot_general(a, b, (((1,), (1,)), ((), ())), preferred_element_type=f32)


def dot_tn(a, b):
    return lax.dot_general(a, b, (((0,), (0,)), ((), ())), preferred_element_type=f32)


def lanes_of(shape):
    return lax.broadcasted_iota(jnp.int32, shape, 1)


def rows_of(shape):
    return lax.broadcasted_iota(jnp.int32, shape, 0)


def column(row):
    return jnp.transpose(jnp.broadcast_to(row.astype(f32), (128, row.shape[1])))[:, :1]


def one_hot_of(route):
    return jnp.where(lanes_of((route.shape[0], 128)).astype(f32) == route, 1.0, 0.0)


def choose_slots(route, spots, experts):
    seq_len = route.shape[0]
    capacity = (9 * seq_len + 8 * experts - 1) // (8 * experts)
    one_hot = one_hot_of(route)
    square = (seq_len, seq_len)
    before = jnp.where(lanes_of(square) < rows_of(square), 1.0, 0.0).astype(bf16)
    place = jnp.sum(dot(before, one_hot.astype(bf16)) * one_hot, axis=1, keepdims=True)
    slot = jnp.where(place < capacity, route * (spots // experts) + place, -1.0)
    return jnp.where(lanes_of((seq_len, spots)).astype(f32) == slot, 1.0, 0.0).astype(bf16)


def allowed_pairs(segment_row):
    square = (segment_row.shape[1],) * 2
    same = column(segment_row) == segment_row.astype(f32)
    return (lanes_of(square) <= rows_of(square)) & same


def begin_kernel(
    chips,
    experts,
    tokens,
    segments,
    routes,
    cotangent,
    shard_qkv,
    shard_out,
    shard_small,
    w_in,
    w_out,
    attn_in,
    qkv,
    lse,
    mixed,
    residual,
    hidden,
    probs,
    gains,
    kept_full,
    full_in,
    full_out,
    got_g,
    got_h,
    full,
    slots_g,
    slots_h,
    hold_in,
    hold_out,
    own_sem,
    sz,
    rz,
    sx,
    rx,
    sy,
    ry,
    sc,
    rc,
    sb,
    rb,
    sw,
    rw,
    lw,
    sd,
    rd,
    se,
    re,
    ld,
):
    block, chip, core, peer_x, peer_y, peer_core, peers_z = place_of(chips)
    owner = lax.axis_index("expert")
    micros, seq_len, model_width = tokens.shape
    rows = shard_qkv.shape[0]
    width = full.shape[1]
    cut = width // 128 * 5 // 8 * 128
    every = pl.ds(0, width)
    inner = width // 128 * 5 // 6 * 128
    cut_in = inner // 256 * 128
    outer = pl.ds(inner, width - inner)
    halves_of = [(pl.ds(0, cut), pl.ds(cut, width - cut))]
    halves_of += [(pl.ds(0, cut_in), pl.ds(cut_in, inner - cut_in))] * (chips - 1)
    half = w_in.shape[1] // 2
    row_y, row_x = block // 2, block % 2

    def part(origin, step, columns):
        start = ((flip(block, origin) * chips + flip(chip, step)) * 2 + core) * rows
        return full.at[pl.ds(pl.multiple_of(start, rows), rows), columns]

    own_copies = []
    for i, (src, at) in enumerate(
        ((shard_qkv, 0), (shard_out, 3 * model_width), (shard_small, 4 * model_width))
    ):
        dst = part(0, 0, pl.ds(at, src.shape[1]))
        own_copies.append(pltpu.make_async_copy(src, dst, own_sem.at[i]))
        own_copies[-1].start()
    others = [{"expert": lax.rem(owner + k, experts)} for k in range(1, experts)]
    greet([peer_x, peer_y] + others)
    for copy in own_copies:
        copy.wait()

    mine = part(0, 0, every)
    along_z = [None] + [send(mine, mine, sz.at[k], rz.at[k], peers_z[k]) for k in range(1, chips)]
    along_x = [[None] * 3 for _ in range(chips)]
    along_y = [[None] * 3 for _ in range(chips)]
    across = [[None] * 8 for _ in range(chips)]
    along_b = [[None] * 4 for _ in range(chips)]

    def to_core(k, origin, columns, tail=0):
        piece = part(origin, k, columns)
        at = (k, origin + 4 * tail)
        across[k][at[1]] = send(piece, piece, sc.at[at], rc.at[at], peer_core)

    def to_chips(origin):
        piece = part(origin, 0, outer)
        for k in range(1, chips):
            along_b[k][origin] = send(
                piece, piece, sb.at[k, origin], rb.at[k, origin], peers_z[k]
            )

    def pass_on(k):
        columns = pl.ds(0, inner) if k else every
        along_x[k][1].wait_recv()
        if k == 0:
            to_chips(1)
        to_core(k, 1, columns)
        along_y[k][1].wait_recv()
        to_core(k, 2, columns)
        along_x[k][2].wait_recv()
        if k == 0:
            to_chips(3)
        along_y[k][2].wait_recv()
        to_core(k, 3, columns)

    def spread(k):
        for turn in range(2):
            for copies, s, r, peer, side in (
                (along_x, sx, rx, peer_x, turn),
                (along_y, sy, ry, peer_y, 1 - turn),
            ):
                piece = part(0, k, halves_of[k][side])
                copies[k][turn] = send(piece, piece, s.at[k, turn], r.at[k, turn], peer)
        to_core(k, 0, every)

    def turn_corner(k):
        along_x[k][0].wait_recv()
        piece = part(1, k, halves_of[k][0])
        along_y[k][2] = send(piece, piece, sy.at[k, 2], ry.at[k, 2], peer_y)
        along_y[k][0].wait_recv()
        if k == 0:
            to_chips(2)
        piece = part(2, k, halves_of[k][1])
        along_x[k][2] = send(piece, piece, sx.at[k, 2], rx.at[k, 2], peer_x)

    piece_rows = w_out.shape[0] // pieces
    out_x = []

    def send_piece():
        j = len(out_x)
        at = pl.ds(j * piece_rows, piece_rows)
        out_x.append(
            send(w_out.at[at], full_out.at[row_x, at], sw.at[3 + j], rw.at[3 + j], peer_x)
        )

    from_y = []

    def send_strip():
        j = len(from_y)
        size = w_in.shape[0] // pieces
        at = pl.ds(j * size, size)
        from_y.append(
            send(
                w_in.at[at, pl.ds((1 - row_y) * half, half)],
                full_in.at[block, at],
                sw.at[3 + pieces + j], rw.at[3 + pieces + j], peer_y,
            )
        )

    spread(0)

    def put_slots(slots, m, values):
        packed = dot_tn(choose_slots(column(routes[m]), experts * slots.shape[2], experts), values)
        packed = packed.astype(bf16)
        for e in range(experts):
            size = slots.shape[2]
            slots[m, e] = packed[e * size : (e + 1) * size]

    for m in range(micros):
        put_slots(slots_g, m, cotangent[m])

    for k in range(chips):
        if k:
            along_z[k].wait_recv()
            spread(k)
            pass_on(k - 1)
        turn_corner(k)
        if k < pieces // 2:
            send_piece()
            send_strip()

    local_in = pltpu.make_async_copy(w_in.at[:, pl.ds(row_y * half, half)], hold_in, lw.at[0])
    local_out = pltpu.make_async_copy(w_out, hold_out, lw.at[1])
    local_in.start()
    local_out.start()
    while len(from_y) < pieces:
        send_strip()
    from_x = send(
        w_in.at[:, pl.ds(row_y * half, half)], full_in.at[block], sw.at[1], rw.at[1], peer_x
    )
    while len(out_x) < pieces:
        send_piece()

    def slot_copies(way, slots, got, m):
        def to_owner(k):
            peer = lax.rem(owner + k, experts)
            return pltpu.make_async_remote_copy(
                src_ref=slots.at[m, peer],
                dst_ref=got.at[m, 0, owner],
                send_sem=sd.at[way, m, k],
                recv_sem=rd.at[way, m, k],
                device_id={"expert": peer},
                device_id_type=MESH,
            )

        def to_y(k):
            origin = lax.rem(owner - k + experts, experts)
            return pltpu.make_async_remote_copy(
                src_ref=got.at[m, 0, origin],
                dst_ref=got.at[m, 1, origin],
                send_sem=se.at[way, m, k],
                recv_sem=re.at[way, m, k],
                device_id=peer_y,
                device_id_type=MESH,
            )

        own = pltpu.make_async_copy(slots.at[m, owner], got.at[m, 0, owner], ld.at[way, m])
        return to_owner, to_y, own

    def start_slots(way, slots, got, m):
        to_owner, to_y, own = slot_copies(way, slots, got, m)
        own.start()

        @pl.loop(1, experts)
        def _(k):
            to_owner(k).start()

    def relay_slots(way, slots, got, m):
        to_owner, to_y, own = slot_copies(way, slots, got, m)
        own.wait()
        to_y(0).start()

        @pl.loop(1, experts)
        def _(k):
            to_owner(k).wait_recv()
            to_y(k).start()

    def end_slots(way, slots, got, m):
        to_owner, to_y, own = slot_copies(way, slots, got, m)

        @pl.loop(1, experts)
        def _(k):
            to_owner(k).wait_send()

        @pl.loop(0, experts)
        def _(k):
            to_y(k).wait()

    for m in range(micros):
        start_slots(0, slots_g, got_g, m)
    pass_on(chips - 1)
    for k in range(1, chips):
        for origin in range(1, 4):
            along_b[k][origin].wait_recv()
            to_core(k, origin, outer, 1)
    for k in range(chips):
        for copy in across[k]:
            if copy is not None:
                copy.wait_recv()
    keep = pltpu.make_async_copy(full, kept_full, own_sem.at[3])
    keep.start()
    small = jnp.transpose(full[:, pl.ds(4 * model_width, 128)].astype(f32))
    gains[...] = small[experts : experts + 2]
    local_in.wait()
    local_out.wait()
    store_in = pltpu.make_async_copy(hold_in, full_in.at[block], lw.at[0])
    store_out = pltpu.make_async_copy(hold_out, full_out.at[row_x], lw.at[1])
    store_in.start()
    store_out.start()

    scale = 1.0 / math.sqrt(model_width // HEADS)
    low_half = lanes_of((seq_len, 128)) < 64
    relay_slots(0, slots_g, got_g, 0)
    for m in range(micros):
        x = tokens[m].astype(f32)
        attn_in[m] = (normalize(x)[0] * gains[0:1, :]).astype(bf16)

        @pl.loop(0, 3 * model_width // 512)
        def _(j):
            at = pl.ds(pl.multiple_of(j * 512, 512), 512)
            qkv[m, :, at] = dot(attn_in[m], full[:, at]).astype(bf16)

        allowed = allowed_pairs(segments[m])
        lse[m] = jnp.zeros(lse.shape[1:], f32)

        @pl.loop(0, model_width // 128)
        def _(pair):
            at = pl.multiple_of(pair * 128, 128)
            query = qkv[m, :, pl.ds(at, 128)]
            key = qkv[m, :, pl.ds(model_width + at, 128)]
            value = qkv[m, :, pl.ds(2 * model_width + at, 128)]
            outs = []
            for side in range(2):
                here = low_half if side == 0 else jnp.logical_not(low_half)
                scores = dot_nt(jnp.where(here, query, 0.0).astype(bf16), key) * scale
                masked = jnp.where(allowed, scores, masked_value)
                top = jnp.max(masked, axis=1, keepdims=True)
                weight = jnp.exp(masked - top)
                norm = jnp.sum(weight, axis=1, keepdims=True)
                outs.append(dot((weight / norm).astype(bf16), value))
                head = lanes_of(lse.shape[1:]) == 2 * pair + side
                lse[m] = jnp.where(head, top + jnp.log(norm), lse[m])
            mixed[m, :, pl.ds(at, 128)] = jnp.where(low_half, outs[0], outs[1]).astype(bf16)

        y1 = x + dot(mixed[m], full[:, pl.ds(3 * model_width, model_width)])
        residual[m] = y1
        low = (normalize(y1)[0] * gains[1:2, :]).astype(bf16)
        hidden[m] = low
        put_slots(slots_h, m, low)
        start_slots(1, slots_h, got_h, m)
        logits = dot(low, full[:, pl.ds(4 * model_width, 128)])
        real = lanes_of(logits.shape) < experts
        logits = jnp.where(real, logits, masked_value)
        weight = jnp.where(real, jnp.exp(logits - jnp.max(logits, axis=1, keepdims=True)), 0.0)
        probs[m] = weight / jnp.sum(weight, axis=1, keepdims=True)
        if m + 1 < micros:
            relay_slots(0, slots_g, got_g, m + 1)
        if m:
            relay_slots(1, slots_h, got_h, m - 1)
    for copy in from_y:
        copy.wait_recv()
    piece = full_in.at[flip(block, 2)]
    diagonal = send(piece, piece, sw.at[2], rw.at[2], peer_x)
    relay_slots(1, slots_h, got_h, micros - 1)

    for m in range(micros):
        end_slots(0, slots_g, got_g, m)
        end_slots(1, slots_h, got_h, m)
    keep.wait()
    store_in.wait()
    store_out.wait()
    for copy in from_y:
        copy.wait_send()
    for copy in (from_x, diagonal, *out_x):
        copy.wait()
    for k in range(chips):
        if k:
            along_z[k].wait_send()
        for turn in range(3):
            along_x[k][turn].wait_send()
            along_y[k][turn].wait_send()
        for copy in across[k] + along_b[k]:
            if copy is not None:
                copy.wait_send()


def begin_layer(tokens, segments, routes, cotangent, shards, w_in, w_out, chips):
    experts = 2 * chips
    micros, seq_len, model_width = tokens.shape
    capacity = (9 * seq_len + 8 * experts - 1) // (8 * experts)
    padded = (capacity + 7) // 8 * 8
    width = 4 * model_width + 128
    rows, half = w_in.shape[0], w_in.shape[1] // 2
    shape = jax.ShapeDtypeStruct
    vmem, hbm = pl.BlockSpec(memory_space=pltpu.VMEM), pl.BlockSpec(memory_space=pl.ANY)
    spots = (micros, experts, padded, model_width)
    return pl.pallas_call(
        functools.partial(begin_kernel, chips, experts),
        out_shape=[
            shape((micros, seq_len, model_width), bf16),
            shape((micros, seq_len, 3 * model_width), bf16),
            shape((micros, seq_len, 128), f32),
            shape((micros, seq_len, model_width), bf16),
            shape((micros, seq_len, model_width), f32),
            shape((micros, seq_len, model_width), bf16),
            shape((micros, seq_len, 128), f32),
            shape((2, model_width), f32),
            shape((model_width, width), bf16),
            shape((4, rows, half), bf16),
            shape((2,) + w_out.shape, bf16),
            shape((micros, 2, experts, padded, model_width), bf16),
            shape((micros, 2, experts, padded, model_width), bf16),
        ],
        in_specs=[vmem] * 4 + [hbm] * 5,
        out_specs=[vmem] * 8 + [hbm] * 5,
        scratch_shapes=[
            pltpu.VMEM((model_width, width), bf16),
            pltpu.VMEM(spots, bf16),
            pltpu.VMEM(spots, bf16),
            pltpu.VMEM((rows, half), bf16),
            pltpu.VMEM(w_out.shape, bf16),
            DMA((4,)),
            DMA((chips,)),
            DMA((chips,)),
            DMA((chips, 3)),
            DMA((chips, 3)),
            DMA((chips, 3)),
            DMA((chips, 3)),
            DMA((chips, 8)),
            DMA((chips, 8)),
            DMA((chips, 4)),
            DMA((chips, 4)),
            DMA((3 + 2 * pieces,)),
            DMA((3 + 2 * pieces,)),
            DMA((2,)),
            DMA((2, micros, experts)),
            DMA((2, micros, experts)),
            DMA((2, micros, experts)),
            DMA((2, micros, experts)),
            DMA((2, micros)),
        ],
        compiler_params=pltpu.CompilerParams(
            collective_id=1, has_side_effects=True, vmem_limit_bytes=60 * 2**20
        ),
        name="begin_layer",
    )(tokens, segments, routes, cotangent, *shards, w_in, w_out)


def expert_kernel(
    chips,
    experts,
    got_h,
    got_g,
    w_in_hbm,
    w_out_hbm,
    full,
    returned,
    grad_back,
    keep_in,
    send_in,
    grad_out,
    x_buf,
    gz_buf,
    w_in,
    w_out,
    router,
    act,
    gu,
    own,
    part,
    part_got,
    out_part,
    out_got,
    out_stage,
    in_part,
    in_stage,
    load,
    sy,
    ry,
    sz,
    rz,
    lz,
    sx,
    rx,
    st,
):
    block, chip, core, peer_x, peer_y, peer_core, peers_z = place_of(chips)
    owner = lax.axis_index("expert")
    micros, rows, model_width = got_h.shape
    half = w_in.shape[1]
    mine = rows // 2
    padded = part.shape[3]
    row_x = block % 2
    step = 256
    backs = (returned, grad_back)

    sources = [
        (got_h.at[0], x_buf.at[pl.ds(0, rows)]),
        (w_in_hbm, w_in),
        (w_out_hbm, w_out),
        (full.at[:, pl.ds(4 * model_width, 128)], router),
        (got_g.at[0], gz_buf.at[pl.ds(0, rows)]),
        (got_h.at[1], x_buf.at[pl.ds(rows, rows)]),
        (got_g.at[1], gz_buf.at[pl.ds(rows, rows)]),
    ]
    loads = []
    for i, (src, dst) in enumerate(sources):
        loads.append(pltpu.make_async_copy(src, dst, load.at[i]))
        loads[-1].start()
    greet(
        [peer_x, peer_y]
        + [{"expert": lax.rem(owner + k, experts)} for k in range(1, experts)]
    )

    def of(m):
        return pl.ds(m * rows, rows)

    def gate_rows(m):
        logits = dot(x_buf[of(m), :], router[...])
        lanes = lanes_of(logits.shape)
        logits = jnp.where(lanes < experts, logits, masked_value)
        weight = jnp.exp(logits - jnp.max(logits, axis=1, keepdims=True))
        weight = jnp.where(lanes < experts, weight, 0.0)
        picked = jnp.sum(jnp.where(lanes == owner, weight, 0.0), axis=1, keepdims=True)
        gate = picked / jnp.sum(weight, axis=1, keepdims=True)
        gz_buf[of(m), :] = (gate * gz_buf[of(m), :].astype(f32)).astype(bf16)

    def open_rows(m, forward, backward):
        @pl.loop(0, half // step)
        def _(j):
            at = pl.ds(pl.multiple_of(j * step, step), step)
            u = dot(x_buf[of(m), :], w_in[:, at])
            root = math.sqrt(2.0 / math.pi)
            square = u * u
            bend = jnp.tanh(root * (u + 0.044715 * (u * square)))
            if forward:
                act[of(m), at] = (0.5 * u * (1.0 + bend)).astype(bf16)
            if backward:
                back = dot_nt(gz_buf[of(m), :], w_out[at, :])
                slope = 0.5 * (1.0 + bend) + 0.5 * u * (1.0 - bend * bend) * (
                    root * (1.0 + (3.0 * 0.044715) * square)
                )
                gu[of(m), at] = (back * slope).astype(bf16)

    wing = model_width // 2

    def columns(side):
        return pl.ds(pl.multiple_of(side * wing, wing), wing)

    def swap(m, way, side):
        return pltpu.make_async_remote_copy(
            src_ref=part.at[m, way, :, :, columns(side)],
            dst_ref=part_got.at[m, way, :, :, columns(side)],
            send_sem=sy.at[m, way, side],
            recv_sem=ry.at[m, way, side],
            device_id=peer_y,
            device_id_type=MESH,
        )

    def close_rows(m, way):
        @pl.loop(0, 2)
        def _(side):
            @pl.loop(0, wing // step)
            def _(j):
                at = pl.ds(pl.multiple_of(side * wing + j * step, step), step)
                if way == 0:
                    total = dot(act[of(m), :], w_out[:, at])
                else:
                    total = dot_nt(gu[of(m), :], w_in[at, :])
                own[m, way, :, at] = total[:mine]
                for e in range(experts):
                    start = mine + e * padded
                    part[m, way, e, :, at] = total[start : start + padded].astype(bf16)

            swap(m, way, side).start()

    def to_source(m, way, side, k):
        peer = lax.rem(owner + k, experts)
        return pltpu.make_async_remote_copy(
            src_ref=part.at[m, way, peer, :, columns(side)],
            dst_ref=backs[way].at[m, owner, :, columns(side)],
            send_sem=sz.at[m, way, side, k],
            recv_sem=rz.at[m, way, side, k],
            device_id={"expert": peer},
            device_id_type=MESH,
        )

    def to_self(m, way, side):
        return pltpu.make_async_copy(
            part.at[m, way, owner, :, columns(side)],
            backs[way].at[m, owner, :, columns(side)],
            lz.at[m, way, side],
        )

    def give_back(m, way, side):
        swap(m, way, side).wait()

        @pl.loop(0, experts)
        def _(e):
            at = pl.ds(pl.multiple_of(e * padded, padded), padded)
            cols = columns(side)
            total = own[m, way, at, cols] + part_got[m, way, e, :, cols].astype(f32)
            part[m, way, e, :, cols] = total.astype(bf16)

        to_self(m, way, side).start()

        @pl.loop(1, experts)
        def _(k):
            to_source(m, way, side, k).start()

    def end_back(m, way, side):
        to_self(m, way, side).wait()

        @pl.loop(1, experts)
        def _(k):
            to_source(m, way, side, k).wait()

    chunks = out_part.shape[0]

    def out_rows(side, j):
        start = side * (half // 2) + j * step
        return dot_tn(act[:, pl.ds(pl.multiple_of(start, step), step)], gz_buf[...])

    def to_x(j):
        return pltpu.make_async_remote_copy(
            src_ref=out_part.at[j],
            dst_ref=out_got.at[j],
            send_sem=sx.at[j],
            recv_sem=rx.at[j],
            device_id=peer_x,
            device_id_type=MESH,
        )

    def put_out(j, slot):
        return pltpu.make_async_copy(out_stage.at[slot], grad_out.at[j], st.at[slot])

    def send_out_rows():
        @pl.loop(0, chunks)
        def _(j):
            out_part[j] = out_rows(1 - row_x, j).astype(bf16)
            to_x(j).start()

    def keep_out_rows():
        for j in range(chunks):
            if j > 1:
                put_out(j - 2, j % 2).wait()
            to_x(j).wait()
            out_stage[j % 2] = out_rows(row_x, j) + out_got[j].astype(f32)
            put_out(j, j % 2).start()

    quarter = in_stage.shape[0]

    def in_rows(y, x):
        start = (2 * y + x) * quarter
        return pl.ds(pl.multiple_of(start, quarter), quarter)

    def in_copies(y):
        return (
            pltpu.make_async_copy(in_part, send_in.at[y], st.at[2]),
            pltpu.make_async_copy(in_stage, keep_in.at[y], st.at[3]),
        )

    def first_rows():
        for y in range(2):
            for kind in range(2):
                if y:
                    in_copies(0)[kind].wait()
                cols = in_rows(y, 1 - row_x if kind == 0 else row_x)

                @pl.loop(0, half // (2 * step))
                def _(j):
                    at = pl.ds(pl.multiple_of(j * 2 * step, 2 * step), 2 * step)
                    value = dot_tn(x_buf[:, cols], gu[:, at])
                    if kind == 0:
                        in_part[:, at] = value.astype(bf16)
                    else:
                        in_stage[:, at] = value

                in_copies(y)[kind].start()

    loads[0].wait()
    loads[1].wait()
    open_rows(0, True, False)
    loads[2].wait()
    close_rows(0, 0)
    loads[5].wait()
    open_rows(1, True, False)
    close_rows(1, 0)
    give_back(0, 0, 0)
    for i in (3, 4, 6):
        loads[i].wait()
    gate_rows(0)
    gate_rows(1)
    give_back(0, 0, 1)
    send_out_rows()
    give_back(1, 0, 0)
    open_rows(0, False, True)
    give_back(1, 0, 1)
    close_rows(0, 1)
    open_rows(1, False, True)
    give_back(0, 1, 0)
    close_rows(1, 1)
    give_back(0, 1, 1)
    first_rows()
    give_back(1, 1, 0)
    give_back(1, 1, 1)
    keep_out_rows()
    for j in range(chunks - 2, chunks):
        put_out(j, j % 2).wait()
    for copy in in_copies(1):
        copy.wait()
    for m in range(micros):
        for way in range(2):
            end_back(m, way, 0)
            end_back(m, way, 1)


def run_experts(got_h, got_g, w_in, w_out, full, chips):
    experts = 2 * chips
    micros, _, _, padded, model_width = got_h.shape
    rows = 2 * experts * padded
    half = w_in.shape[1]
    shape = jax.ShapeDtypeStruct
    hbm = pl.BlockSpec(memory_space=pl.ANY)
    slots = shape((micros, experts, padded, model_width), bf16)
    chunks = half // 2 // 256
    quarter = model_width // 4
    spots = (micros, 2, experts, padded, model_width)
    return pl.pallas_call(
        functools.partial(expert_kernel, chips, experts),
        out_shape=[
            slots,
            slots,
            shape((2, quarter, half), f32),
            shape((2, quarter, half), bf16),
            shape((chunks, 256, model_width), f32),
        ],
        in_specs=[hbm] * 5,
        out_specs=[hbm] * 5,
        scratch_shapes=[
            pltpu.VMEM((micros * rows, model_width), bf16),
            pltpu.VMEM((micros * rows, model_width), bf16),
            pltpu.VMEM((model_width, half), bf16),
            pltpu.VMEM((half, model_width), bf16),
            pltpu.VMEM((model_width, 128), bf16),
            pltpu.VMEM((micros * rows, half), bf16),
            pltpu.VMEM((micros * rows, half), bf16),
            pltpu.VMEM((micros, 2, rows // 2, model_width), f32),
            pltpu.VMEM(spots, bf16),
            pltpu.VMEM(spots, bf16),
            pltpu.VMEM((chunks, 256, model_width), bf16),
            pltpu.VMEM((chunks, 256, model_width), bf16),
            pltpu.VMEM((2, 256, model_width), f32),
            pltpu.VMEM((quarter, half), bf16),
            pltpu.VMEM((quarter, half), f32),
            DMA((7,)),
            DMA((micros, 2, 2)),
            DMA((micros, 2, 2)),
            DMA((micros, 2, 2, experts)),
            DMA((micros, 2, 2, experts)),
            DMA((micros, 2, 2)),
            DMA((chunks,)),
            DMA((chunks,)),
            DMA((4,)),
        ],
        compiler_params=pltpu.CompilerParams(
            collective_id=3, has_side_effects=True, vmem_limit_bytes=63 * 2**20
        ),
        name="run_experts",
    )(
        got_h.reshape(micros, rows, model_width),
        got_g.reshape(micros, rows, model_width),
        w_in,
        w_out,
        full,
    )


def end_kernel(
    chips,
    experts,
    cut,
    segments,
    routes,
    gains,
    lse,
    probs,
    tokens,
    cotangent,
    qkv_hbm,
    y1_hbm,
    returned_hbm,
    back_hbm,
    attn_hbm,
    mixed_hbm,
    hidden_hbm,
    full_hbm,
    send_in,
    keep_in,
    grad_qkv,
    grad_out,
    grad_small,
    output,
    grad_x,
    grad_in,
    full,
    x_buf,
    g_buf,
    qkv,
    y1_buf,
    returned,
    back,
    attn_in,
    mixed,
    hidden,
    out_buf,
    gx_buf,
    branch,
    gqkv,
    glog_buf,
    go_buf,
    gain_rows,
    grads,
    crecv,
    xrecv,
    yrecv,
    part_z,
    zrecv,
    brecv,
    got_in,
    got_y,
    keep,
    load,
    load_m,
    put,
    si,
    ri,
    siy,
    riy,
    sc,
    rc,
    sx,
    rx,
    sy,
    ry,
    sz,
    rz,
    sb,
    rb,
):
    block, chip, core, peer_x, peer_y, peer_core, peers_z = place_of(chips)
    micros, seq_len, model_width = tokens.shape
    width = full.shape[1]
    row_y = block // 2
    opposite = flip(core, 1)
    wide_qkv = 3 * model_width

    late = pl.ds(wide_qkv, width - wide_qkv)
    early = pl.ds(0, wide_qkv)
    once = [
        (full_hbm.at[:, late], full.at[:, late]),
        (full_hbm.at[:, early], full.at[:, early]),
        (keep_in.at[1 - row_y], keep.at[0]),
        (keep_in.at[row_y], keep.at[1]),
        (attn_hbm, attn_in),
        (mixed_hbm, mixed),
        (hidden_hbm, hidden),
    ]
    once = [pltpu.make_async_copy(src, dst, load.at[i]) for i, (src, dst) in enumerate(once)]
    pairs = (
        (returned_hbm, returned),
        (back_hbm, back),
        (cotangent, g_buf),
        (y1_hbm, y1_buf),
        (qkv_hbm, qkv),
        (tokens, x_buf),
    )

    def load_of(i, m):
        src, dst = pairs[i]
        return pltpu.make_async_copy(src.at[m], dst.at[m], load_m.at[i, m])

    once[0].start()
    for i in range(len(pairs)):
        load_of(i, 0).start()
    once[1].start()
    for i in range(len(pairs)):
        load_of(i, 1).start()
    for copy in once[2:]:
        copy.start()

    greet([peer_x, peer_y, peer_core] + peers_z[1:])

    def in_x(j):
        return pltpu.make_async_remote_copy(
            src_ref=send_in.at[1 - row_y if j == 0 else row_y],
            dst_ref=got_in.at[j],
            send_sem=si.at[j],
            recv_sem=ri.at[j],
            device_id=peer_x,
            device_id_type=MESH,
        )

    in_y = pltpu.make_async_remote_copy(
        src_ref=got_in.at[0],
        dst_ref=got_y,
        send_sem=siy,
        recv_sem=riy,
        device_id=peer_y,
        device_id_type=MESH,
    )
    in_x(0).start()
    in_x(1).start()
    strip = 32

    def pass_in_y():
        once[2].wait()
        in_x(0).wait()

        @pl.loop(0, keep.shape[1] // strip)
        def _(j):
            at = pl.ds(pl.multiple_of(j * strip, strip), strip)
            got_in[0, at, :] = (keep[0, at, :] + got_in[0, at, :].astype(f32)).astype(bf16)

        in_y.start()

    def put_in(slot, side):
        half = keep.shape[2]
        cols = pl.ds(pl.multiple_of(side * half, half), half)
        copy = pltpu.make_async_copy(keep.at[slot], grad_in.at[:, cols], put.at[2, slot])
        copy.start()
        return copy

    def end_in():
        once[3].wait()
        in_x(1).wait()

        @pl.loop(0, keep.shape[1] // strip)
        def _(j):
            at = pl.ds(pl.multiple_of(j * strip, strip), strip)
            keep[1, at, :] = keep[1, at, :] + got_in[1, at, :].astype(f32)

        stored = [put_in(1, row_y)]
        in_y.wait()

        @pl.loop(0, keep.shape[1] // strip)
        def _(j):
            at = pl.ds(pl.multiple_of(j * strip, strip), strip)
            keep[0, at, :] = got_y[at, :].astype(f32)

        return stored + [put_in(0, 1 - row_y)]

    def put_out(m):
        return pltpu.make_async_copy(out_buf.at[m], output.at[m], put.at[0, m])

    def put_x(m):
        return pltpu.make_async_copy(gx_buf.at[m], grad_x.at[m], put.at[1, m])

    gain_rows[...] = jnp.zeros(gain_rows.shape, f32)
    scale = 1.0 / math.sqrt(model_width // HEADS)
    low_half = lanes_of((seq_len, 128)) < 64
    once[0].wait()

    @pl.loop(0, micros)
    def _(m):
        here = pl.ds(pl.multiple_of(m * seq_len, seq_len), seq_len)
        for i in range(4):
            load_of(i, m).wait()
        g = g_buf[m].astype(f32)
        route = column(routes[m])
        chosen = choose_slots(route, returned.shape[1], experts)
        moe = dot(chosen, returned[m])
        prob = probs[m]
        one_hot = one_hot_of(route)
        gate = jnp.sum(prob * one_hot, axis=1, keepdims=True)
        y1 = y1_buf[m]
        out_buf[m] = (y1 + gate * moe).astype(bf16)
        put_out(m).start()
        choice = one_hot * jnp.sum(g * moe, axis=1, keepdims=True)
        glog = (prob * (choice - jnp.sum(prob * choice, axis=1, keepdims=True))).astype(bf16)
        glog_buf[here, :] = glog
        grad_h = dot(chosen, back[m]) + dot_nt(glog, full[:, pl.ds(4 * model_width, 128)])
        n2, inv2 = normalize(y1)
        gain_rows[experts + 1 : experts + 2, :] += jnp.sum(grad_h * n2, axis=0, keepdims=True)
        gy1 = g + norm_back(grad_h * gains[1:2, :], n2, inv2)
        gx_buf[m] = gy1
        branch[here, :] = gy1.astype(bf16)
        go_buf[...] = dot_nt(branch[here, :], full[:, pl.ds(wide_qkv, model_width)]).astype(bf16)
        load_of(4, m).wait()
        load_of(5, m).wait()

        allowed = allowed_pairs(segments[m])

        @pl.loop(0, model_width // 128)
        def _(pair):
            @pl.when((m == 1) & (pair == 3))
            def _():
                pass_in_y()

            at = pl.multiple_of(pair * 128, 128)
            query = qkv[m, :, pl.ds(at, 128)]
            key = qkv[m, :, pl.ds(model_width + at, 128)]
            value = qkv[m, :, pl.ds(2 * model_width + at, 128)]
            grad_o = go_buf[:, pl.ds(at, 128)]
            parts = []
            for side in range(2):
                mine = low_half if side == 0 else jnp.logical_not(low_half)
                scores = dot_nt(jnp.where(mine, query, 0.0).astype(bf16), key) * scale
                head = lanes_of(lse.shape[1:]) == 2 * pair + side
                top = jnp.sum(jnp.where(head, lse[m], 0.0), axis=1, keepdims=True)
                p = jnp.exp(jnp.where(allowed, scores, masked_value) - top)
                gp = dot_nt(jnp.where(mine, grad_o, 0.0).astype(bf16), value)
                gs = (p * (gp - jnp.sum(p * gp, axis=1, keepdims=True))).astype(bf16)
                parts.append(
                    (dot(gs, key) * scale, dot_tn(gs, query) * scale, dot_tn(p.astype(bf16), grad_o))
                )
            for i in range(3):
                both = jnp.where(low_half, parts[0][i], parts[1][i]).astype(bf16)
                gqkv[here, pl.ds(i * model_width + at, 128)] = both

        @pl.when(m == 0)
        def _():
            once[1].wait()

        ga = dot_nt(gqkv[here, :], full[:, pl.ds(0, wide_qkv)])
        n1, inv1 = normalize(x_buf[m].astype(f32))
        gain_rows[experts : experts + 1, :] += jnp.sum(ga * n1, axis=0, keepdims=True)
        gx_buf[m] = gx_buf[m] + norm_back(ga * gains[0:1, :], n1, inv1)
        put_x(m).start()

    for copy in once[4:]:
        copy.wait()
    rows = grads.shape[3]
    span = model_width // 4

    def to_core(b):
        return pltpu.make_async_remote_copy(
            src_ref=grads.at[b, :, opposite],
            dst_ref=crecv.at[b],
            send_sem=sc.at[b],
            recv_sem=rc.at[b],
            device_id=peer_core,
            device_id_type=MESH,
        )

    @pl.loop(0, 4)
    def _(b):
        cols = pl.ds(pl.multiple_of(b * span, span), span)

        def store(start, value):
            value = value.reshape(chips, 2, rows, value.shape[1]).astype(bf16)
            grads[b, :, :, :, pl.ds(start, value.shape[3])] = value

        @pl.loop(0, wide_qkv // 512)
        def _(j):
            start = pl.multiple_of(j * 512, 512)
            store(start, dot_tn(attn_in[:, cols], gqkv[:, pl.ds(start, 512)]))

        store(wide_qkv, dot_tn(mixed[:, cols], branch[...]))
        small = dot_tn(hidden[:, cols], glog_buf[...]) + jnp.transpose(gain_rows[:, cols])
        store(4 * model_width, small)
        to_core(b).start()

    inner = width - brecv.shape[3]
    outer = pl.ds(inner, width - inner)
    order = list(range(chips - 1, -1, -1))
    along_x, along_y, along_z, along_b = {}, {}, {}, {}

    def halves_of(k):
        low, end = (inner // 256 * 128, inner) if k else (cut, width)
        return pl.ds(0, low), pl.ds(low, end - low), pl.ds(0, end - low)

    def spot(k, origin, cols):
        return (flip(block, origin), flip(chip, k), core, slice(None), cols)

    def add_core(k, origin, cols):
        at = spot(k, origin, cols)
        return grads[at].astype(f32) + crecv[at[:2] + at[3:]].astype(f32)

    def begin_outer(k):
        for origin in range(4):
            at = spot(k, origin, outer)
            grads[at] = add_core(k, origin, outer).astype(bf16)
            along_b[k, origin] = send(
                grads.at[at], brecv.at[k, origin], sb.at[k, origin], rb.at[k, origin], peers_z[k]
            )

    def begin(k):
        left, right, short = halves_of(k)
        for origin in (3, 1, 2, 0):
            at = spot(k, origin, pl.ds(0, inner))
            grads[at] = add_core(k, origin, pl.ds(0, inner)).astype(bf16)
            if k == 0:
                total = add_core(0, origin, outer)
                for j in range(1, chips):
                    along_b[j, origin].wait_recv()
                    total = total + brecv[j, origin].astype(f32)
                grads[spot(0, origin, outer)] = total.astype(bf16)
            if origin == 3:
                along_x[k, 0] = send(
                    grads.at[spot(k, 3, left)], xrecv.at[k, 0, :, left], sx.at[k, 0], rx.at[k, 0], peer_x
                )
                along_y[k, 0] = send(
                    grads.at[spot(k, 3, right)], yrecv.at[k, 0, :, short], sy.at[k, 0], ry.at[k, 0], peer_y
                )
            if origin == 1:
                along_x[k, 1] = send(
                    grads.at[spot(k, 1, left)], xrecv.at[k, 1, :, left], sx.at[k, 1], rx.at[k, 1], peer_x
                )
            if origin == 2:
                along_y[k, 1] = send(
                    grads.at[spot(k, 2, right)], yrecv.at[k, 1, :, short], sy.at[k, 1], ry.at[k, 1], peer_y
                )

    def relay(k):
        left, right, short = halves_of(k)
        along_x[k, 0].wait_recv()
        at = spot(k, 2, left)
        grads[at] = (grads[at].astype(f32) + xrecv[k, 0, :, left].astype(f32)).astype(bf16)
        along_y[k, 2] = send(grads.at[at], yrecv.at[k, 2, :, left], sy.at[k, 2], ry.at[k, 2], peer_y)
        along_y[k, 0].wait_recv()
        at = spot(k, 1, right)
        grads[at] = (grads[at].astype(f32) + yrecv[k, 0, :, short].astype(f32)).astype(bf16)
        along_x[k, 2] = send(
            grads.at[at], xrecv.at[k, 2, :, short], sx.at[k, 2], rx.at[k, 2], peer_x
        )

    def finish(k):
        left, right, short = halves_of(k)
        for turn in (1, 2):
            along_x[k, turn].wait_recv()
            along_y[k, turn].wait_recv()
        lhs = (
            grads[spot(k, 0, left)].astype(f32)
            + xrecv[k, 1, :, left].astype(f32)
            + yrecv[k, 2, :, left].astype(f32)
        )
        rhs = (
            grads[spot(k, 0, right)].astype(f32)
            + yrecv[k, 1, :, short].astype(f32)
            + xrecv[k, 2, :, short].astype(f32)
        )
        if k:
            part_z[k, :, left] = lhs.astype(bf16)
            part_z[k, :, right] = rhs.astype(bf16)
            cols = pl.ds(0, inner)
            along_z[k] = send(
                part_z.at[k, :, cols], zrecv.at[k, :, cols], sz.at[k], rz.at[k], peers_z[k]
            )
        else:
            middle, rhs = rhs[:, : inner - cut], rhs[:, inner - cut :]
            for j in range(1, chips):
                along_z[j].wait_recv()
                lhs = lhs + zrecv[j, :, left].astype(f32)
                middle = middle + zrecv[j, :, pl.ds(cut, inner - cut)].astype(f32)
            start = 0
            for out in (grad_qkv, grad_out, grad_small):
                w = out.shape[1]
                for lo, hi, value in ((0, cut, lhs), (cut, inner, middle), (inner, width, rhs)):
                    a, b = max(start, lo), min(start + w, hi)
                    if a < b:
                        out[:, a - start : b - start] = value[:, a - lo : b - lo]
                start += w

    @pl.loop(0, 4)
    def _(b):
        to_core(b).wait()

    for k in order[:-1]:
        begin_outer(k)
    stored = None
    for i in range(chips + 2):
        if i < chips:
            begin(order[i])
        if 0 <= i - 1 < chips:
            relay(order[i - 1])
        if i == chips:
            stored = end_in()
        if i - 2 >= 0:
            finish(order[i - 2])
    for k in order:
        for turn in range(3):
            along_x[k, turn].wait_send()
            along_y[k, turn].wait_send()
        if k:
            along_z[k].wait_send()
            for origin in range(4):
                along_b[k, origin].wait_send()
    for copy in stored:
        copy.wait()
    for m in range(micros):
        put_out(m).wait()
        put_x(m).wait()


def end_layer(small_inputs, big_inputs, chips):
    tokens, keep_in, full = big_inputs[0], big_inputs[-1], big_inputs[9]
    experts = 2 * chips
    micros, seq_len, model_width = tokens.shape
    spots = big_inputs[4].shape[1]
    width = full.shape[1]
    rows = model_width // (8 * chips)
    cut = (width // 128 + 1) // 2 * 128
    quarter, half = keep_in.shape[1:]
    every = micros * seq_len
    shape = jax.ShapeDtypeStruct
    vmem, hbm = pl.BlockSpec(memory_space=pltpu.VMEM), pl.BlockSpec(memory_space=pl.ANY)
    tall = (micros, seq_len, model_width)
    return pl.pallas_call(
        functools.partial(end_kernel, chips, experts, cut),
        out_shape=[
            shape((rows, 3 * model_width), f32),
            shape((rows, model_width), f32),
            shape((rows, 128), f32),
            shape(tall, bf16),
            shape(tall, f32),
            shape((quarter, 2 * half), f32),
        ],
        in_specs=[vmem] * len(small_inputs) + [hbm] * len(big_inputs),
        out_specs=[vmem] * 3 + [hbm] * 3,
        scratch_shapes=[
            pltpu.VMEM((model_width, width), bf16),
            pltpu.VMEM(tall, bf16),
            pltpu.VMEM(tall, bf16),
            pltpu.VMEM((micros, seq_len, 3 * model_width), bf16),
            pltpu.VMEM(tall, f32),
            pltpu.VMEM((micros, spots, model_width), bf16),
            pltpu.VMEM((micros, spots, model_width), bf16),
            pltpu.VMEM((every, model_width), bf16),
            pltpu.VMEM((every, model_width), bf16),
            pltpu.VMEM((every, model_width), bf16),
            pltpu.VMEM(tall, bf16),
            pltpu.VMEM(tall, f32),
            pltpu.VMEM((every, model_width), bf16),
            pltpu.VMEM((every, 3 * model_width), bf16),
            pltpu.VMEM((every, 128), bf16),
            pltpu.VMEM((seq_len, model_width), bf16),
            pltpu.VMEM((128, model_width), f32),
            pltpu.VMEM((4, chips, 2, rows, width), bf16),
            pltpu.VMEM((4, chips, rows, width), bf16),
            pltpu.VMEM((chips, 3, rows, cut), bf16),
            pltpu.VMEM((chips, 3, rows, cut), bf16),
            pltpu.VMEM((chips, rows, width), bf16),
            pltpu.VMEM((chips, rows, width), bf16),
            pltpu.VMEM((chips, 4, rows, width // 640 * 128), bf16),
            pltpu.VMEM((2, quarter, half), bf16),
            pltpu.VMEM((quarter, half), bf16),
            pltpu.VMEM((2, quarter, half), f32),
            DMA((7,)),
            DMA((6, micros)),
            DMA((3, micros)),
            DMA((2,)),
            DMA((2,)),
            DMA(()),
            DMA(()),
            DMA((4,)),
            DMA((4,)),
            DMA((chips, 3)),
            DMA((chips, 3)),
            DMA((chips, 3)),
            DMA((chips, 3)),
            DMA((chips,)),
            DMA((chips,)),
            DMA((chips, 4)),
            DMA((chips, 4)),
        ],
        compiler_params=pltpu.CompilerParams(
            collective_id=2, has_side_effects=True, vmem_limit_bytes=63 * 2**20
        ),
        name="end_layer",
    )(*small_inputs, *big_inputs)


def on_device(
    tokens,
    segment_ids,
    routes,
    cotangent,
    w_qkv,
    w_attn_out,
    w_router,
    gain_attn,
    gain_moe,
    w_expert_in,
    w_expert_out,
):
    micro_count, _, seq_len, model_width = tokens.shape
    experts = w_router.shape[1]
    chips = model_width // w_qkv.shape[0] // 8

    spare = jnp.zeros((w_qkv.shape[0], 128 - 2 - experts), bf16)
    small = jnp.concatenate([w_router, gain_attn[:, None], gain_moe[:, None], spare], axis=1)
    tokens, cotangent, segment_ids = tokens[:, 0], cotangent[:, 0], segment_ids
    routes = routes.reshape(micro_count, 1, seq_len)
    attn_in, qkv, lse, mixed, residual, hidden, probs, gains, gathered, w_in, w_out, got_g, got_h = (
        begin_layer(
            tokens,
            segment_ids,
            routes,
            cotangent,
            (w_qkv, w_attn_out, small),
            w_expert_in[0],
            w_expert_out[0],
            chips,
        )
    )
    returned, grad_back, keep_in, send_in, grad_out = run_experts(
        got_h,
        got_g,
        w_in.reshape(model_width, -1),
        w_out.reshape(-1, model_width),
        gathered,
        chips,
    )
    flat = (micro_count, -1, model_width)
    grad_qkv, grad_attn_out, small_sum, output, grad_tokens, grad_in = end_layer(
        (segment_ids, routes, gains, lse, probs),
        (
            tokens,
            cotangent,
            qkv,
            residual,
            returned.reshape(flat),
            grad_back.reshape(flat),
            attn_in.reshape(-1, model_width),
            mixed.reshape(-1, model_width),
            hidden.reshape(-1, model_width),
            gathered,
            send_in,
            keep_in,
        ),
        chips,
    )
    return (
        output[:, None],
        grad_tokens[:, None],
        grad_qkv,
        grad_attn_out,
        small_sum[:, :experts],
        small_sum[:, experts],
        small_sum[:, experts + 1],
        grad_in[None],
        grad_out.reshape(1, -1, model_width),
    )


def solution(mesh):
    rows = P(("dp", "expert"))
    seqs = P(None, ("dp", "expert"))
    owned = P("expert", "dp", None)
    return jax.shard_map(
        on_device,
        mesh=mesh,
        in_specs=(seqs, seqs, seqs, seqs, rows, rows, rows, rows, rows, owned, owned),
        out_specs=(seqs, seqs, rows, rows, rows, rows, rows, owned, owned),
        check_vma=False,
    )
```
